32 devices in a mesh: dp: 8 (over z, y), sp: 4 (over x, core).
Axes of the slice: x: 2, y: 2, z: 4, core: 2. Of those that a mesh axis runs over, the one named last changes fastest.
Arguments:
- tokens: bfloat16 [16, 1024, 512], P('dp', 'sp'), may hold values from -6 to 6
- lengths: int32 [16], P('dp'), may hold values from 64 to 1024, as said below
- post_query: bfloat16 [512, 512], replicated, may hold values from -0.25 to 0.25
- post_key: bfloat16 [512, 512], replicated, may hold values from -0.25 to 0.25
- post_value: bfloat16 [512, 512], replicated, may hold values from -0.25 to 0.25
- post_out: bfloat16 [512, 512], replicated, may hold values from -1 to 1
- post_gate: bfloat16 [512, 1376], replicated, may hold values from -0.25 to 0.25
- post_up: bfloat16 [512, 1376], replicated, may hold values from -0.25 to 0.25
- post_down: bfloat16 [1376, 512], replicated, may hold values from -0.15625 to 0.15625
- post_attn_gain: float32 [512], replicated, may hold values from 0.5 to 1.5
- post_ffn_gain: float32 [512], replicated, may hold values from 0.5 to 1.5
- pre_query: bfloat16 [512, 512], replicated, may hold values from -0.25 to 0.25
- pre_key: bfloat16 [512, 512], replicated, may hold values from -0.25 to 0.25
- pre_value: bfloat16 [512, 512], replicated, may hold values from -0.25 to 0.25
- pre_out: bfloat16 [512, 512], replicated, may hold values from -1 to 1
- pre_gate: bfloat16 [512, 1376], replicated, may hold values from -0.25 to 0.25
- pre_up: bfloat16 [512, 1376], replicated, may hold values from -0.25 to 0.25
- pre_down: bfloat16 [1376, 512], replicated, may hold values from -0.15625 to 0.15625
- pre_attn_gain: float32 [512], replicated, may hold values from 0.5 to 1.5
- pre_ffn_gain: float32 [512], replicated, may hold values from 0.5 to 1.5
- out_grad: bfloat16 [16, 1024, 512], P('dp', 'sp'), may hold values from -6 to 6
Outputs:
- output: bfloat16 [16, 1024, 512], P('dp', 'sp')
- tokens_grad: bfloat16 [16, 1024, 512], P('dp', 'sp')
- grad_post_query: float32 [512, 512], replicated
- grad_post_key: float32 [512, 512], replicated
- grad_post_value: float32 [512, 512], replicated
- grad_post_out: float32 [512, 512], replicated
- grad_post_gate: float32 [512, 1376], replicated
- grad_post_up: float32 [512, 1376], replicated
- grad_post_down: float32 [1376, 512], replicated
- grad_post_attn_gain: float32 [512], replicated
- grad_post_ffn_gain: float32 [512], replicated
- grad_pre_query: float32 [512, 512], replicated
- grad_pre_key: float32 [512, 512], replicated
- grad_pre_value: float32 [512, 512], replicated
- grad_pre_out: float32 [512, 512], replicated
- grad_pre_gate: float32 [512, 1376], replicated
- grad_pre_up: float32 [512, 1376], replicated
- grad_pre_down: float32 [1376, 512], replicated
- grad_pre_attn_gain: float32 [512], replicated
- grad_pre_ffn_gain: float32 [512], replicated
The draws below stay inside these ranges and needn't reach their ends.
Inputs may be any that keep to these rules, and one draw needn't show every extreme that they name: `lengths`: some slot has length exactly 1024 and some exactly 64.
All inputs are finite; a program needn't handle non-finite values.
Results may differ from the reference program's by a relative error of at most 0.024.
Values may be sent and summed in bfloat16 or wider, within the bound.
No kernel may reach another device: no remote copies, remote signals or barrier semaphores. Data moves between devices by JAX's collectives and lax.ppermute only.
A program may use at most 192 MiB of HBM per device.

```python
import jax
import jax.numpy as jnp
from jax import lax

D = 512
HEADS = 8
FF = 1376
HD = 64
SEQ = 1024
MIN_LEN = 64
SLOTS_DEV = 2
SLOTS = 16


def draw_lengths(key, part):
    key_list = jax.random.split(key, 4)
    base_len = jax.random.randint(key_list[0], (SLOTS,), MIN_LEN, 2 * MIN_LEN + 1)
    exponent = jnp.minimum(jax.random.randint(key_list[1], (SLOTS,), 0, 6), 4)
    drawn_len = jnp.minimum(base_len * jnp.power(2, exponent), SEQ)
    longest = jax.random.randint(key_list[2], (), 0, SLOTS)
    shortest = (longest + jax.random.randint(key_list[3], (), 1, SLOTS)) % SLOTS
    slot_ids = jnp.arange(SLOTS)
    drawn_len = jnp.where(slot_ids == longest, SEQ, drawn_len)
    drawn_len = jnp.where(slot_ids == shortest, MIN_LEN, drawn_len)
    return drawn_len.astype(jnp.int32)


def steps_of(own_key, dims, cuts, low, largest):
    def one(position, shards_of):
        heights = jax.random.uniform(jax.random.fold_in(jax.random.fold_in(own_key, 6), position), (shards_of,), jnp.float32, low / len(cuts), largest / len(cuts))
        return jnp.repeat(jnp.exp(heights), dims[position] // shards_of).reshape((-1,) + (1,) * (len(dims) - position - 1))

    gain = one(*cuts[0])
    for cut in cuts[1:]:
        gain = gain * one(*cut)
    return gain


def scatter_about(key, shape, width, most, cuts=(), kind=jnp.bfloat16):
    array = jax.random.normal(key, shape, jnp.float32) * width
    if len(cuts) > 0:
        array = steps_of(key, shape, cuts, -0.22, 0.18) * array
    return jnp.clip(array, min=-most, max=most).astype(kind)


def setup_inputs(seed: int = 0) -> dict:
    streams_of = jax.random.split(jax.random.key(seed), 22)
    tokens = scatter_about(streams_of[0], (SLOTS, SEQ, D), 1.0, 6.0, ((0, 8), (1, 4)))
    lengths = draw_lengths(jax.random.fold_in(streams_of[21], 71), 0)
    post_query = scatter_about(streams_of[2], (D, D), D ** -0.5, 0.25)
    post_key = scatter_about(streams_of[3], (D, D), D ** -0.5, 0.25)
    post_value = scatter_about(streams_of[4], (D, D), D ** -0.5, 0.25)
    post_out = scatter_about(streams_of[5], (D, D), (D // 16) ** -0.5, 1.0)
    post_gate = scatter_about(streams_of[6], (D, FF), D ** -0.5, 0.25)
    post_up = scatter_about(streams_of[7], (D, FF), D ** -0.5, 0.25)
    post_down = scatter_about(streams_of[8], (FF, D), FF ** -0.5, 0.15625)
    post_attn_gain = jnp.clip(1.0 + 0.1 * jax.random.normal(streams_of[9], (D,), jnp.float32), 0.5, 1.5)
    post_ffn_gain = jnp.clip(1.0 + 0.1 * jax.random.normal(streams_of[10], (D,), jnp.float32), 0.5, 1.5)
    pre_query = scatter_about(streams_of[11], (D, D), D ** -0.5, 0.25)
    pre_key = scatter_about(streams_of[12], (D, D), D ** -0.5, 0.25)
    pre_value = scatter_about(streams_of[13], (D, D), D ** -0.5, 0.25)
    pre_out = scatter_about(streams_of[14], (D, D), (D // 16) ** -0.5, 1.0)
    pre_gate = scatter_about(streams_of[15], (D, FF), D ** -0.5, 0.25)
    pre_up = scatter_about(streams_of[16], (D, FF), D ** -0.5, 0.25)
    pre_down = scatter_about(streams_of[17], (FF, D), FF ** -0.5, 0.15625)
    pre_attn_gain = jnp.clip(1.0 + 0.1 * jax.random.normal(streams_of[18], (D,), jnp.float32), 0.5, 1.5)
    pre_ffn_gain = jnp.clip(1.0 + 0.1 * jax.random.normal(streams_of[19], (D,), jnp.float32), 0.5, 1.5)
    out_grad = scatter_about(streams_of[20], (SLOTS, SEQ, D), 1.0, 6.0, ((0, 8), (1, 4)))
    return dict(tokens=tokens, lengths=lengths, post_query=post_query, post_key=post_key, post_value=post_value, post_out=post_out, post_gate=post_gate, post_up=post_up, post_down=post_down, post_attn_gain=post_attn_gain, post_ffn_gain=post_ffn_gain, pre_query=pre_query, pre_key=pre_key, pre_value=pre_value, pre_out=pre_out, pre_gate=pre_gate, pre_up=pre_up, pre_down=pre_down, pre_attn_gain=pre_attn_gain, pre_ffn_gain=pre_ffn_gain, out_grad=out_grad)


eps = 1e-06
highest = lax.Precision.HIGHEST

@jax.custom_vjp
def low(v):
    return lax.optimization_barrier(v.astype(jnp.bfloat16)).astype(jnp.float32)

@jax.custom_vjp
def low_back(v):
    return v

def low_keep(v):
    return (low(v), None)

def low_pass(kept, grad):
    return (grad,)

def back_keep(v):
    return (v, None)

def back_low(kept, grad):
    return (low(grad),)
low.defvjp(low_keep, low_pass)
low_back.defvjp(back_keep, back_low)

def norm_rows(values, gain_vec):
    return values * lax.rsqrt(lax.optimization_barrier(jnp.mean(values * values, axis=-1, keepdims=True)) + eps) * gain_vec

def rotary_tables():
    half_dim = HD // 2
    inverse = 10000.0 ** (-jnp.arange(half_dim, dtype=jnp.float32) * 2.0 / HD)
    angles = jnp.arange(SEQ, dtype=jnp.float32)[:, None] * inverse[None, :]
    cosine = jnp.concatenate([jnp.cos(angles), jnp.cos(angles)], axis=-1)
    sine_table = jnp.concatenate([jnp.sin(angles), jnp.sin(angles)], axis=-1)
    return (cosine, sine_table)

def rotate(values, cosine, sine_table):
    half_dim = values.shape[-1] // 2
    turned = jnp.concatenate([-values[..., half_dim:], values[..., :half_dim]], axis=-1)
    return values * cosine[:, None, :] + turned * sine_table[:, None, :]

def project(values, weight):
    return jnp.einsum('nsd,de->nse', values, weight, precision=highest)

def attend_slot(pieces):
    queries, key_heads, value_heads, length = pieces
    score_scale = HD ** (-0.5)
    scores = low_back(jnp.einsum('qhd,khd->hqk', queries, key_heads, precision=highest) * score_scale)
    row_index = jnp.arange(SEQ, dtype=jnp.int32)[:, None]
    col_index = jnp.arange(SEQ, dtype=jnp.int32)[None, :]
    allowed = (col_index <= row_index) & (col_index < length)
    scores = jnp.where(allowed[None], scores, -1000000000.0)
    softmax_p = jnp.exp(scores - jax.nn.logsumexp(scores, axis=-1, keepdims=True))
    mixed_heads = jnp.einsum('hqk,khd->qhd', low(softmax_p), value_heads, precision=highest)
    return low_back(low(mixed_heads))

def layer(inputs, weights, slot_lengths, post_norm, cosine, sine_table):
    w_query, w_key, w_value, w_out, w_gate, w_up, w_down, gain_att, gain_ffn = weights
    slot_count = inputs.shape[0]
    if post_norm:
        entry_rows = low(inputs)
    else:
        entry_rows = low(norm_rows(inputs, gain_att))

    def split_heads(values):
        return values.reshape(slot_count, SEQ, HEADS, HD)
    queries = low_back(low(rotate(split_heads(low_back(project(entry_rows, w_query))), cosine, sine_table)))
    key_heads = low_back(low(rotate(split_heads(low_back(project(entry_rows, w_key))), cosine, sine_table)))
    value_heads = low_back(low(split_heads(project(entry_rows, w_value))))
    mixed_rows = lax.map(jax.checkpoint(attend_slot), (queries, key_heads, value_heads, slot_lengths))
    mixed_rows = mixed_rows.reshape(slot_count, SEQ, D)
    middle = inputs + low_back(project(mixed_rows, w_out))
    if post_norm:
        state_rows = norm_rows(middle, gain_att)
        ffn_in = low(state_rows)
    else:
        state_rows = middle
        ffn_in = low(norm_rows(middle, gain_ffn))
    gate_act = low_back(project(ffn_in, w_gate))
    up_act = low_back(project(ffn_in, w_up))
    hidden = low(jax.nn.silu(gate_act) * up_act)
    result = state_rows + low_back(project(hidden, w_down))
    if post_norm:
        result = norm_rows(result, gain_ffn)
    return result

def reference(tokens, lengths, post_query, post_key, post_value, post_out, post_gate, post_up, post_down, post_attn_gain, post_ffn_gain, pre_query, pre_key, pre_value, pre_out, pre_gate, pre_up, pre_down, pre_attn_gain, pre_ffn_gain, out_grad):
    layer_one = tuple((weight.astype(jnp.float32) for weight in (post_query, post_key, post_value, post_out, post_gate, post_up, post_down, post_attn_gain, post_ffn_gain)))
    layer_two = tuple((weight.astype(jnp.float32) for weight in (pre_query, pre_key, pre_value, pre_out, pre_gate, pre_up, pre_down, pre_attn_gain, pre_ffn_gain)))
    cosine, sine_table = rotary_tables()
    group_count = SLOTS // SLOTS_DEV
    inputs_all = tokens.astype(jnp.float32).reshape(group_count, SLOTS_DEV, SEQ, D)
    cotangent_all = out_grad.astype(jnp.float32).reshape(group_count, SLOTS_DEV, SEQ, D)
    lengths_all = lengths.reshape(group_count, SLOTS_DEV)

    def group_step(totals, pieces):
        inputs, cotangent, group_lengths = pieces

        def forward(inputs_in, weights_one, weights_two):
            middle_state = layer(inputs_in, weights_one, group_lengths, True, cosine, sine_table)
            return layer(middle_state, weights_two, group_lengths, False, cosine, sine_table)
        result, pullback = jax.vjp(forward, inputs, layer_one, layer_two)
        positions = jnp.arange(SEQ, dtype=jnp.int32)
        valid_rows = (positions[None, :] < group_lengths[:, None]).astype(jnp.float32)
        grad_inputs, grads_one, grads_two = pullback(cotangent * valid_rows[:, :, None])
        totals = jax.tree.map(jnp.add, totals, (grads_one, grads_two))
        return (totals, (result.astype(jnp.bfloat16), grad_inputs.astype(jnp.bfloat16)))
    zero_grads = jax.tree.map(jnp.zeros_like, (layer_one, layer_two))
    totals, (results, grad_rows) = lax.scan(group_step, zero_grads, (inputs_all, cotangent_all, lengths_all))
    output = results.reshape(SLOTS, SEQ, D)
    tokens_grad = grad_rows.reshape(SLOTS, SEQ, D)
    grads_one, grads_two = totals
    return (output, tokens_grad, grads_one[0], grads_one[1], grads_one[2], grads_one[3], grads_one[4], grads_one[5], grads_one[6], grads_one[7], grads_one[8], grads_two[0], grads_two[1], grads_two[2], grads_two[3], grads_two[4], grads_two[5], grads_two[6], grads_two[7], grads_two[8])
```

```python
import jax
import jax.numpy as jnp
from jax import lax
from jax.sharding import PartitionSpec as P

HEADS = 8
HD = 64
SEQ = 1024


eps = 1e-06


def norm_rows(values, gain_vec):
    return values * lax.rsqrt(jnp.mean(values * values, axis=-1, keepdims=True) + eps) * gain_vec


def rotary_tables(start, row_count):
    half_dim = HD // 2
    inverse = 10000.0 ** (-jnp.arange(half_dim, dtype=jnp.float32) * 2.0 / HD)
    positions = (start + jnp.arange(row_count, dtype=jnp.int32)).astype(jnp.float32)
    angles = positions[:, None] * inverse[None, :]
    cosine = jnp.concatenate([jnp.cos(angles), jnp.cos(angles)], axis=-1)
    sine_table = jnp.concatenate([jnp.sin(angles), jnp.sin(angles)], axis=-1)
    return (cosine, sine_table)


def rotate(values, cosine, sine_table):
    half_dim = values.shape[-1] // 2
    turned = jnp.concatenate([-values[..., half_dim:], values[..., :half_dim]], axis=-1)
    return values * cosine[:, None, :] + turned * sine_table[:, None, :]


def rotate_back(grads, cosine, sine_table):
    half_dim = grads.shape[-1] // 2
    turned = grads * sine_table[:, None, :]
    backward = jnp.concatenate([turned[..., half_dim:], -turned[..., :half_dim]], axis=-1)
    return grads * cosine[:, None, :] + backward


def gated(gate_act, up_act):
    return jax.nn.silu(gate_act) * up_act


def slot_scores(queries, key_heads, length):
    scores = jnp.einsum(
        "qhd,khd->hqk", queries, key_heads, preferred_element_type=jnp.float32
    ) * HD ** (-0.5)
    row_index = jnp.arange(SEQ, dtype=jnp.int32)[:, None]
    col_index = jnp.arange(SEQ, dtype=jnp.int32)[None, :]
    allowed = (col_index <= row_index) & (col_index < length)
    return jnp.where(allowed[None], scores, -1000000000.0)


def attend_slot(pieces):
    queries, key_heads, value_heads, length = pieces
    scores = slot_scores(queries, key_heads, length)
    maxima = jnp.max(scores, axis=-1, keepdims=True)
    log_total = maxima + jnp.log(jnp.sum(jnp.exp(scores - maxima), axis=-1, keepdims=True))
    softmax_p = jnp.exp(scores - log_total)
    mixed_heads = jnp.einsum(
        "hqk,khd->qhd",
        softmax_p.astype(jnp.bfloat16),
        value_heads,
        preferred_element_type=jnp.float32,
    )
    return (mixed_heads.astype(jnp.bfloat16), log_total)


def attend_back(pieces):
    queries, key_heads, value_heads, log_total, grad_mixed, length = pieces
    softmax_p = jnp.exp(slot_scores(queries, key_heads, length) - log_total)
    grad_values = jnp.einsum(
        "hqk,qhd->khd",
        softmax_p.astype(jnp.bfloat16),
        grad_mixed,
        preferred_element_type=jnp.float32,
    )
    grad_probs = jnp.einsum(
        "qhd,khd->hqk", grad_mixed, value_heads, preferred_element_type=jnp.float32
    )
    row_delta = jnp.sum(softmax_p * grad_probs, axis=-1, keepdims=True)
    grad_scores = (softmax_p * (grad_probs - row_delta)).astype(jnp.bfloat16)
    grad_queries = jnp.einsum(
        "hqk,khd->qhd", grad_scores, key_heads, preferred_element_type=jnp.float32
    ) * HD ** (-0.5)
    grad_keys = jnp.einsum(
        "hqk,qhd->khd", grad_scores, queries, preferred_element_type=jnp.float32
    ) * HD ** (-0.5)
    return (
        grad_queries.astype(jnp.bfloat16),
        grad_keys.astype(jnp.bfloat16),
        grad_values.astype(jnp.bfloat16),
    )


def layer_forward(inputs, weights, lengths, post_norm, cosine, sine_table):
    w_query, w_key, w_value, w_out, w_gate, w_up, w_down, gain_att, gain_ffn = weights
    group = lax.axis_size("sp")
    slot_count, row_count, width = inputs.shape
    local_heads = HEADS // group
    full_rows = row_count * group
    if post_norm:
        entry_rows = inputs.astype(jnp.bfloat16)
    else:
        entry_rows = norm_rows(inputs, gain_att).astype(jnp.bfloat16)

    def rotated(weight):
        product = jnp.einsum("nsd,de->nse", entry_rows, weight, preferred_element_type=jnp.float32)
        turned = rotate(product.reshape(slot_count, row_count, HEADS, HD), cosine, sine_table)
        return turned.astype(jnp.bfloat16).reshape(slot_count, row_count, group, local_heads * HD)

    query_rows = rotated(w_query)
    key_rows = rotated(w_key)
    value_rows = jnp.einsum("nsd,de->nse", entry_rows, w_value, preferred_element_type=jnp.float32)
    value_rows = value_rows.astype(jnp.bfloat16).reshape(
        slot_count, row_count, group, local_heads * HD
    )
    query_heads, key_heads, value_heads = (
        lax.all_to_all(query_rows, "sp", split_axis=2, concat_axis=1, tiled=True),
        lax.all_to_all(key_rows, "sp", split_axis=2, concat_axis=1, tiled=True),
        lax.all_to_all(value_rows, "sp", split_axis=2, concat_axis=1, tiled=True),
    )

    def head_view(values):
        return values.reshape(slot_count, full_rows, local_heads, HD)

    query_heads = head_view(query_heads)
    key_heads = head_view(key_heads)
    value_heads = head_view(value_heads)
    mixed_heads, log_total = lax.map(attend_slot, (query_heads, key_heads, value_heads, lengths))
    mixed_rows = lax.all_to_all(
        mixed_heads.reshape(slot_count, full_rows, 1, local_heads * HD),
        "sp",
        split_axis=1,
        concat_axis=2,
        tiled=True,
    )
    mixed_rows = mixed_rows.reshape(slot_count, row_count, width)
    middle = inputs + jnp.einsum(
        "nsd,de->nse", mixed_rows, w_out, preferred_element_type=jnp.float32
    )
    if post_norm:
        state_rows = norm_rows(middle, gain_att)
        ffn_in = state_rows.astype(jnp.bfloat16)
    else:
        state_rows = middle
        ffn_in = norm_rows(middle, gain_ffn).astype(jnp.bfloat16)
    gate_act = jnp.einsum("nsd,df->nsf", ffn_in, w_gate, preferred_element_type=jnp.float32)
    up_act = jnp.einsum("nsd,df->nsf", ffn_in, w_up, preferred_element_type=jnp.float32)
    hidden = gated(gate_act, up_act).astype(jnp.bfloat16)
    result = state_rows + jnp.einsum(
        "nsf,fd->nsd", hidden, w_down, preferred_element_type=jnp.float32
    )
    saved = (
        inputs,
        entry_rows,
        query_heads,
        key_heads,
        value_heads,
        log_total,
        mixed_rows,
        middle,
        ffn_in,
        gate_act,
        up_act,
        hidden,
        result,
    )
    if post_norm:
        return (norm_rows(result, gain_ffn), saved)
    return (result, saved)


def layer_backward(grad_output, saved, weights, lengths, post_norm, cosine, sine_table):
    w_query, w_key, w_value, w_out, w_gate, w_up, w_down, gain_att, gain_ffn = weights
    (
        inputs,
        entry_rows,
        query_heads,
        key_heads,
        value_heads,
        log_total,
        mixed_rows,
        middle,
        ffn_in,
        gate_act,
        up_act,
        hidden,
        result,
    ) = saved
    group = lax.axis_size("sp")
    slot_count, row_count, width = inputs.shape
    local_heads = HEADS // group
    full_rows = row_count * group
    if post_norm:
        discard, pull_result = jax.vjp(norm_rows, result, gain_ffn)
        grad_result, grad_gain_ffn = pull_result(grad_output)
    else:
        grad_result = grad_output
    grad_down_in = grad_result.astype(jnp.bfloat16)
    grad_w_down = jnp.einsum(
        "nsf,nsd->fd", hidden, grad_down_in, preferred_element_type=jnp.float32
    )
    grad_hidden = jnp.einsum(
        "nsd,fd->nsf", grad_down_in, w_down, preferred_element_type=jnp.float32
    )
    discard, pull_glu = jax.vjp(gated, gate_act, up_act)
    grad_gate, grad_up = pull_glu(grad_hidden)
    grad_gate = grad_gate.astype(jnp.bfloat16)
    grad_up = grad_up.astype(jnp.bfloat16)
    grad_w_gate = jnp.einsum("nsd,nsf->df", ffn_in, grad_gate, preferred_element_type=jnp.float32)
    grad_w_up = jnp.einsum("nsd,nsf->df", ffn_in, grad_up, preferred_element_type=jnp.float32)
    grad_ffn_in = jnp.einsum("nsf,df->nsd", grad_gate, w_gate, preferred_element_type=jnp.float32)
    grad_ffn_in = grad_ffn_in + jnp.einsum(
        "nsf,df->nsd", grad_up, w_up, preferred_element_type=jnp.float32
    )
    if post_norm:
        discard, pull_middle = jax.vjp(norm_rows, middle, gain_att)
        grad_middle, grad_gain_att = pull_middle(grad_result + grad_ffn_in)
    else:
        discard, pull_middle = jax.vjp(norm_rows, middle, gain_ffn)
        grad_normed, grad_gain_ffn = pull_middle(grad_ffn_in)
        grad_middle = grad_result + grad_normed
    grad_attn = grad_middle.astype(jnp.bfloat16)
    grad_w_out = jnp.einsum(
        "nsd,nse->de", mixed_rows, grad_attn, preferred_element_type=jnp.float32
    )
    grad_mixed = jnp.einsum(
        "nse,de->nsd", grad_attn, w_out, preferred_element_type=jnp.float32
    ).astype(jnp.bfloat16)
    grad_mixed = lax.all_to_all(
        grad_mixed.reshape(slot_count, row_count, group, local_heads * HD),
        "sp",
        split_axis=2,
        concat_axis=1,
        tiled=True,
    )
    grad_mixed = grad_mixed.reshape(slot_count, full_rows, local_heads, HD)
    grad_queries, grad_keys, grad_values = lax.map(
        attend_back, (query_heads, key_heads, value_heads, log_total, grad_mixed, lengths)
    )

    def head_pack(values):
        return values.reshape(slot_count, full_rows, 1, local_heads * HD)

    grad_query_rows, grad_key_rows, grad_value_rows = (
        lax.all_to_all(head_pack(grad_queries), "sp", split_axis=1, concat_axis=2, tiled=True),
        lax.all_to_all(head_pack(grad_keys), "sp", split_axis=1, concat_axis=2, tiled=True),
        lax.all_to_all(head_pack(grad_values), "sp", split_axis=1, concat_axis=2, tiled=True),
    )

    def unrotate(values):
        grads = values.astype(jnp.float32).reshape(slot_count, row_count, HEADS, HD)
        return (
            rotate_back(grads, cosine, sine_table)
            .astype(jnp.bfloat16)
            .reshape(slot_count, row_count, width)
        )

    grad_query_pre = unrotate(grad_query_rows)
    grad_key_pre = unrotate(grad_key_rows)
    grad_value_pre = grad_value_rows.reshape(slot_count, row_count, width)
    grad_w_query = jnp.einsum(
        "nsd,nse->de", entry_rows, grad_query_pre, preferred_element_type=jnp.float32
    )
    grad_w_key = jnp.einsum(
        "nsd,nse->de", entry_rows, grad_key_pre, preferred_element_type=jnp.float32
    )
    grad_w_value = jnp.einsum(
        "nsd,nse->de", entry_rows, grad_value_pre, preferred_element_type=jnp.float32
    )
    grad_entry = jnp.einsum(
        "nse,de->nsd", grad_query_pre, w_query, preferred_element_type=jnp.float32
    )
    grad_entry = grad_entry + jnp.einsum(
        "nse,de->nsd", grad_key_pre, w_key, preferred_element_type=jnp.float32
    )
    grad_entry = grad_entry + jnp.einsum(
        "nse,de->nsd", grad_value_pre, w_value, preferred_element_type=jnp.float32
    )
    if post_norm:
        grad_inputs = grad_middle + grad_entry
    else:
        discard, pull_inputs = jax.vjp(norm_rows, inputs, gain_att)
        grad_normed_in, grad_gain_att = pull_inputs(grad_entry)
        grad_inputs = grad_middle + grad_normed_in
    return (
        grad_inputs,
        (
            grad_w_query,
            grad_w_key,
            grad_w_value,
            grad_w_out,
            grad_w_gate,
            grad_w_up,
            grad_w_down,
            grad_gain_att,
            grad_gain_ffn,
        ),
    )


def reduce_grads(grads):
    weights = tuple(grad.astype(jnp.bfloat16) for grad in grads[:7])
    summed = lax.psum(weights, ("dp", "sp"))
    gains = lax.psum(grads[7:], ("dp", "sp"))
    return tuple(grad.astype(jnp.float32) for grad in summed) + tuple(gains)


def body(
    tokens,
    lengths,
    post_query,
    post_key,
    post_value,
    post_out,
    post_gate,
    post_up,
    post_down,
    post_attn_gain,
    post_ffn_gain,
    pre_query,
    pre_key,
    pre_value,
    pre_out,
    pre_gate,
    pre_up,
    pre_down,
    pre_attn_gain,
    pre_ffn_gain,
    out_grad,
):
    slot_count, row_count, width = tokens.shape
    start = lax.axis_index("sp") * row_count
    cosine, sine_table = rotary_tables(start, row_count)
    layer_one = (
        post_query,
        post_key,
        post_value,
        post_out,
        post_gate,
        post_up,
        post_down,
        post_attn_gain,
        post_ffn_gain,
    )
    layer_two = (
        pre_query,
        pre_key,
        pre_value,
        pre_out,
        pre_gate,
        pre_up,
        pre_down,
        pre_attn_gain,
        pre_ffn_gain,
    )
    inputs_one = tokens.astype(jnp.float32)
    middle_state, saved_one = layer_forward(
        inputs_one, layer_one, lengths, True, cosine, sine_table
    )
    final_state, saved_two = layer_forward(
        middle_state, layer_two, lengths, False, cosine, sine_table
    )
    output = final_state.astype(jnp.bfloat16)
    positions = start + jnp.arange(row_count, dtype=jnp.int32)
    valid_rows = (positions[None, :] < lengths[:, None]).astype(jnp.float32)
    grad_final = out_grad.astype(jnp.float32) * valid_rows[:, :, None]
    grad_middle_state, grads_two = layer_backward(
        grad_final, saved_two, layer_two, lengths, False, cosine, sine_table
    )
    grad_tokens, grads_one = layer_backward(
        grad_middle_state, saved_one, layer_one, lengths, True, cosine, sine_table
    )
    grads_one = reduce_grads(grads_one)
    grads_two = reduce_grads(grads_two)
    tokens_grad = grad_tokens.astype(jnp.bfloat16)
    return (
        output,
        tokens_grad,
        grads_one[0],
        grads_one[1],
        grads_one[2],
        grads_one[3],
        grads_one[4],
        grads_one[5],
        grads_one[6],
        grads_one[7],
        grads_one[8],
        grads_two[0],
        grads_two[1],
        grads_two[2],
        grads_two[3],
        grads_two[4],
        grads_two[5],
        grads_two[6],
        grads_two[7],
        grads_two[8],
    )


def solution(mesh):
    in_specs = (
        P("dp", "sp", None),
        P("dp"),
        P(),
        P(),
        P(),
        P(),
        P(),
        P(),
        P(),
        P(),
        P(),
        P(),
        P(),
        P(),
        P(),
        P(),
        P(),
        P(),
        P(),
        P(),
        P("dp", "sp", None),
    )
    out_specs = (
        P("dp", "sp", None),
        P("dp", "sp", None),
        P(),
        P(),
        P(),
        P(),
        P(),
        P(),
        P(),
        P(),
        P(),
        P(),
        P(),
        P(),
        P(),
        P(),
        P(),
        P(),
        P(),
        P(),
    )
    return jax.shard_map(body, mesh=mesh, in_specs=in_specs, out_specs=out_specs, check_vma=False)
```

```python
import jax
import jax.numpy as jnp
from jax import lax
from jax.experimental import pallas as pl
from jax.experimental.pallas import tpu as pltpu
from jax.sharding import PartitionSpec as P

D = 512
HEADS = 8
HD = 64
FF = 1376
SEQ = 1024
EPS = 1e-06
NEG = -1000000000.0
AXES = ("dp", "sp")
BF = jnp.bfloat16
F32 = jnp.float32
LANES = 128
PANELS = D // LANES
BLK = SEQ // 4
ROWS = 2 * BLK
SCALE = HD ** (-0.5)
FFN_ROWS = 3 * PANELS * FF
ATTN_ROWS = 4 * PANELS * D
GAIN_ROWS = 16


def dot(left, right):
    return lax.dot_general(left, right, (((1,), (0,)), ((), ())), preferred_element_type=F32)


def dot_nt(left, right):
    return lax.dot_general(left, right, (((1,), (1,)), ((), ())), preferred_element_type=F32)


def dot_tn(left, right):
    return lax.dot_general(left, right, (((0,), (0,)), ((), ())), preferred_element_type=F32)


def inv_rms(values):
    return lax.rsqrt(jnp.mean(values * values, axis=-1, keepdims=True) + EPS)


def rms_back(values, gain, upstream):
    scale = inv_rms(values)
    weighted = upstream * gain
    grad = scale * weighted - values * (
        scale * scale * scale * jnp.mean(weighted * values, axis=-1, keepdims=True)
    )
    grad_gain = jnp.sum(upstream * (values * scale), axis=0, keepdims=True)
    return grad, grad_gain


class Refs:
    def __init__(self, inputs, outputs, vmem, sems):
        self.vmem, self.outputs, self.sems = vmem, outputs, sems
        self.waiting, self.sent = {}, []
        for k, name in enumerate(inputs):
            copy = pltpu.make_async_copy(inputs[name], vmem[name], sems.at[k])
            copy.start()
            self.waiting[name] = copy
        self.first_out = len(inputs)

    def __getattr__(self, name):
        if name in self.waiting:
            self.waiting.pop(name).wait()
        return self.vmem[name]

    def send(self, *refs):
        for ref in refs:
            for k, name in enumerate(self.outputs):
                if name in self.vmem and self.vmem[name] is ref:
                    sem = self.sems.at[self.first_out + k]
                    copy = pltpu.make_async_copy(ref, self.outputs[name], sem)
                    copy.start()
                    self.sent.append(copy)

    def finish(self):
        for name in list(self.waiting):
            self.waiting.pop(name).wait()
        for copy in self.sent:
            copy.wait()


def run_kernel(body, scalars, ins, outs, scratch, pieces=None, flops=0):
    outs, scratch = dict(outs), dict(scratch)
    twins = list(ins) + list(outs) + list(scratch)
    shapes = [pltpu.VMEM(ins[n].shape, ins[n].dtype) for n in ins]
    shapes += [pltpu.VMEM(*outs[n]) for n in outs] + [pltpu.VMEM(*scratch[n]) for n in scratch]
    n_in, n_out, n_copies = len(ins), len(outs), 1
    out_shapes = [jax.ShapeDtypeStruct(*outs[n]) for n in outs]
    if pieces is not None:
        orders, n_copies, rows = pieces
        twins.append("grads")
        shapes.append(pltpu.VMEM((n_copies * rows, LANES), BF))
        out_shapes += [jax.ShapeDtypeStruct((n_copies // 2 * rows, LANES), BF)] * 2

    def kernel(scalars_ref, *args):
        inputs = dict(zip(ins, args[:n_in]))
        outputs = dict(zip(outs, args[n_in : n_in + n_out]))
        rest = args[n_in + len(out_shapes) :]
        vmem = dict(zip(twins, rest))
        sems, piece_sems = rest[len(twins) :]
        refs = Refs(inputs, outputs, vmem, sems)
        body(refs, scalars_ref)
        if pieces is not None:
            keep, send = args[n_in + n_out : n_in + n_out + 2]
            piece_copies(refs.grads, keep, send, scalars_ref[0], piece_sems, pieces, True)
        refs.finish()

    moved = sum(a.size * a.dtype.itemsize for a in ins.values())
    return pl.pallas_call(
        kernel,
        name=body.__name__,
        out_shape=out_shapes,
        grid_spec=pltpu.PrefetchScalarGridSpec(
            num_scalar_prefetch=1,
            grid=(),
            in_specs=[pl.BlockSpec(memory_space=pl.ANY)] * n_in,
            out_specs=[pl.BlockSpec(memory_space=pl.ANY)] * len(out_shapes),
            scratch_shapes=shapes
            + [pltpu.SemaphoreType.DMA((n_in + n_out,)), pltpu.SemaphoreType.DMA((n_copies,))],
        ),
        compiler_params=pltpu.CompilerParams(vmem_limit_bytes=56 << 20),
        cost_estimate=pl.CostEstimate(flops=flops, transcendentals=0, bytes_accessed=moved),
    )(scalars, *ins.values())


def piece_position(j, me, order):
    where = 0
    for bit in order:
        where = where * 2 + (((me >> bit) & 1) ^ ((j >> bit) & 1))
    return where


def piece_copies(buffer, first, second, me, sems, pieces, out):
    orders, count, rows = pieces

    def copies(mine):
        made = []
        for j in range(count):
            spot = pl.multiple_of(piece_position(j, me, orders[j & 1]) * rows, 16)
            half = first if (j & 1) == mine else second
            here = buffer.at[pl.ds(j * rows, rows), :]
            there = half.at[pl.ds(spot, rows), :]
            ends = (here, there) if out else (there, here)
            made.append(pltpu.make_async_copy(*ends, sems.at[j]))
        for copy in made:
            copy.start()
        for copy in made:
            copy.wait()

    @pl.when(me & 1 == 0)
    def even():
        copies(0)

    @pl.when(me & 1 == 1)
    def odd():
        copies(1)


def head_lanes(rows, which):
    lane = lax.broadcasted_iota(jnp.int32, (rows, LANES), 1)
    return (lane < HD) if which == 0 else (lane >= HD)


def only_head(panel, which):
    return jnp.where(head_lanes(panel.shape[0], which), panel, jnp.zeros_like(panel))


def turned(panel):
    lane = lax.broadcasted_iota(jnp.int32, panel.shape, 1)
    return jnp.where(
        lane % HD < HD // 2,
        pltpu.roll(panel, LANES - HD // 2, 1),
        pltpu.roll(panel, HD // 2, 1),
    )


def block_rows(index):
    return pl.ds(pl.multiple_of(index * BLK, BLK), BLK)


def panel_cols(panel):
    return slice(panel * LANES, (panel + 1) * LANES)


def blocks_of(sp):
    return sp, 3 - sp


def project_heads(refs, sp, entry, own):
    for half, block in enumerate(blocks_of(sp)):
        here = slice(half * BLK, (half + 1) * BLK)
        there = block_rows(block)
        rows = entry[here, :]
        keys = dot(rows, refs.w_key[...])
        refs.v[there, :] = dot(rows, refs.w_value[...]).astype(BF)
        if own:
            queries = dot(rows, refs.w_query[...])
        cosine = refs.cosine[there, :]
        sine = refs.sine[there, :]
        for panel in range(PANELS):
            cols = panel_cols(panel)
            part = keys[:, cols]
            refs.k[there, cols] = (part * cosine + turned(part) * sine).astype(BF)
            if own:
                part = queries[:, cols]
                refs.q[here, cols] = (part * cosine + turned(part) * sine).astype(BF) * SCALE


def query_blocks(sp, low):
    chip = sp >> 1
    return (block_rows(chip), low + 1), (block_rows(1 - chip), 4 - low)


def both_ways(sp, step):
    low = (sp & 1) ^ (sp >> 1)

    @pl.when(low == 0)
    def outer():
        step(0)

    @pl.when(low == 1)
    def inner():
        step(1)


def attend(refs, scalars, low):
    sp, length = scalars[1], scalars[2]
    lane = lax.broadcasted_iota(jnp.int32, (BLK, LANES), 1)

    def panel_step(panel, carry):
        cols = pl.ds(pl.multiple_of(panel * LANES, LANES), LANES)
        for rows, blocks in query_blocks(sp, low):
            seen = blocks * BLK
            queries = refs.q[rows, cols]
            outs, logs = [], []
            for which in range(2):
                scores = dot_nt(only_head(queries, which), refs.k[0:seen, cols])
                key_at = lax.broadcasted_iota(jnp.int32, (BLK, seen), 1)
                row_at = lax.broadcasted_iota(jnp.int32, (BLK, seen), 0) + (blocks - 1) * BLK
                scores = jnp.where((key_at <= row_at) & (key_at < length), scores, NEG)
                top = jnp.max(scores, axis=-1, keepdims=True)
                weights = jnp.exp(scores - top)
                total = jnp.sum(weights, axis=-1, keepdims=True)
                outs.append(dot(weights.astype(BF), refs.v[0:seen, cols]) / total)
                logs.append(top + jnp.log(total))
            refs.mixed[rows, cols] = jnp.where(head_lanes(BLK, 0), outs[0], outs[1]).astype(BF)
            kept = jnp.where(lane == 2 * panel, logs[0], refs.lse[rows, :])
            refs.lse[rows, :] = jnp.where(lane == 2 * panel + 1, logs[1], kept)
        return carry

    lax.fori_loop(0, PANELS, panel_step, 0)


def attention_forward(refs, scalars):
    sp = scalars[1]
    project_heads(refs, sp, refs.own, True)
    project_heads(refs, sp ^ 1, refs.sib, False)
    refs.lse[...] = jnp.zeros((ROWS, LANES), F32)
    both_ways(sp, lambda low: attend(refs, scalars, low))
    refs.send(refs.q, refs.k, refs.v, refs.lse, refs.mixed)


def ffn_forward(refs, ffn_in):
    for half in range(2):
        rows = slice(half * BLK, (half + 1) * BLK)
        gate = dot_nt(ffn_in[rows, :], refs.w_gate[...])
        up = dot_nt(ffn_in[rows, :], refs.w_up[...])
        refs.gate[rows, :] = gate
        refs.up[rows, :] = up
        refs.hidden[rows, :] = (gate * jax.nn.sigmoid(gate) * up).astype(BF)


def store_panels(refs, at, grad):
    height = grad.shape[0]
    for panel in range(PANELS):
        put = slice(at + panel * height, at + (panel + 1) * height)
        refs.grads[put, :] = grad[:, panel_cols(panel)].astype(BF)


def ffn_weight_grads(refs, at, ffn_in, grad_result):
    grad_down = grad_result.astype(BF)
    store_panels(refs, at, dot_tn(refs.hidden[...], grad_down))
    for half in range(2):
        rows = slice(half * BLK, (half + 1) * BLK)
        grad_hidden = dot_nt(grad_down[rows, :], refs.w_down[...])
        gate = refs.gate[rows, :]
        sigma = jax.nn.sigmoid(gate)
        grad_gate = grad_hidden * refs.up[rows, :] * (sigma * (1.0 + gate * (1.0 - sigma)))
        refs.dgate[rows, :] = grad_gate.astype(BF)
        refs.dup[rows, :] = (grad_hidden * (gate * sigma)).astype(BF)
    store_panels(refs, at + PANELS * FF, dot_tn(refs.dgate[...], ffn_in))
    store_panels(refs, at + 2 * PANELS * FF, dot_tn(refs.dup[...], ffn_in))


def ffn_input_grad(refs):
    return dot(refs.dgate[...], refs.w_gate[...]) + dot(refs.dup[...], refs.w_up[...])


def clear_tail(refs, start):
    end = refs.grads.shape[0]
    refs.grads[start:end, :] = jnp.zeros((end - start, LANES), BF)


def store_gains(refs, at, gains):
    row = lax.broadcasted_iota(jnp.int32, (GAIN_ROWS, LANES), 0)
    block = jnp.zeros((GAIN_ROWS, LANES), F32)
    for slot, gain in enumerate(gains):
        for panel in range(PANELS):
            block = jnp.where(row == PANELS * slot + panel, gain[:, panel_cols(panel)], block)
    refs.grads[at : at + GAIN_ROWS, :] = block.astype(BF)


def post_forward(refs, scalars):
    attention_forward(refs, scalars)
    middle = refs.own[...].astype(F32) + dot(refs.mixed[...], refs.w_out[...])
    refs.middle[...] = middle
    refs.send(refs.middle)
    state = middle * inv_rms(middle) * refs.attn_gain[...]
    ffn_forward(refs, state.astype(BF))
    result = state + dot(refs.hidden[...], refs.w_down[...])
    refs.result[...] = result
    output = result * inv_rms(result) * refs.ffn_gain[...]
    entry = output * inv_rms(output) * refs.next_gain[...]
    refs.entry[...] = entry.astype(BF)
    refs.send(refs.result, refs.entry)


def pre_forward(refs, scalars):
    attention_forward(refs, scalars)
    clear_tail(refs, FFN_ROWS)
    result = refs.result[...]
    inputs = result * inv_rms(result) * refs.last_gain[...]
    middle = inputs + dot(refs.mixed[...], refs.w_out[...])
    refs.middle[...] = middle
    refs.send(refs.middle)
    ffn_in = (middle * inv_rms(middle) * refs.ffn_gain[...]).astype(BF)
    ffn_forward(refs, ffn_in)
    output = middle + dot(refs.hidden[...], refs.w_down[...])
    refs.output[...] = output.astype(BF)
    refs.send(refs.output)
    sp, length = scalars[1], scalars[2]
    row = lax.broadcasted_iota(jnp.int32, (ROWS, D), 0)
    position = row + jnp.where(row < BLK, sp * BLK, (2 - sp) * BLK)
    cotangent = jnp.where(position < length, refs.cotangent[...].astype(F32), 0.0)
    refs.upstream[...] = cotangent
    refs.send(refs.upstream)
    ffn_weight_grads(refs, 0, ffn_in, cotangent)
    refs.send(refs.dgate, refs.dup)


def attend_back(refs, scalars, low):
    sp, length = scalars[1], scalars[2]
    if low == 1:
        refs.dk[3 * BLK :, :] = jnp.zeros((BLK, D), F32)
        refs.dv[3 * BLK :, :] = jnp.zeros((BLK, D), F32)

    def panel_step(panel, carry):
        cols = pl.ds(pl.multiple_of(panel * LANES, LANES), LANES)
        for rows, blocks in reversed(query_blocks(sp, low)):
            seen = blocks * BLK
            queries = refs.q[rows, cols]
            grads = refs.gmix[rows, cols]
            keys = refs.k[0:seen, cols]
            values = refs.v[0:seen, cols]
            key_at = lax.broadcasted_iota(jnp.int32, (seen, BLK), 0)
            row_at = lax.broadcasted_iota(jnp.int32, (seen, BLK), 1) + (blocks - 1) * BLK
            allowed = (key_at <= row_at) & (key_at < length)
            grad_q = jnp.zeros((BLK, LANES), F32)
            grad_k = jnp.zeros((seen, LANES), F32)
            grad_v = jnp.zeros((seen, LANES), F32)
            for which in range(2):
                q_head = only_head(queries, which)
                g_head = only_head(grads, which)
                at = pl.ds(2 * panel + which, 1)
                scores = jnp.where(allowed, dot_nt(keys, q_head), NEG)
                probs = jnp.exp(scores - refs.lse_t[at, rows])
                grad_p = dot_nt(values, g_head)
                grad_s = (probs * (grad_p - refs.delta_t[at, rows])).astype(BF)
                grad_v = grad_v + dot(probs.astype(BF), g_head)
                grad_k = grad_k + dot(grad_s, q_head)
                grad_q = grad_q + dot_tn(grad_s, only_head(keys, which))
            refs.dq[rows, cols] = grad_q * SCALE
            if blocks == 4 - low:
                refs.dk[0:seen, cols] = grad_k
                refs.dv[0:seen, cols] = grad_v
            else:
                refs.dk[0:seen, cols] += grad_k
                refs.dv[0:seen, cols] += grad_v
        return carry

    lax.fori_loop(0, PANELS, panel_step, 0)


def attention_backward(refs, scalars, grad_middle):
    sp = scalars[1]
    grad_attn = grad_middle.astype(BF)
    mixed = refs.mixed[...]
    grad_mixed = dot_nt(grad_attn, refs.w_out[...]).astype(BF)
    refs.gmix[...] = grad_mixed
    product = grad_mixed.astype(F32) * mixed.astype(F32)
    high = product.astype(BF)
    rest = (product - high.astype(F32)).astype(BF)
    head_of = lax.broadcasted_iota(jnp.int32, (HEADS, D), 1) // HD
    pick = (head_of == lax.broadcasted_iota(jnp.int32, (HEADS, D), 0)).astype(F32).astype(BF)
    refs.delta_t[...] = dot_nt(pick, high) + dot_nt(pick, rest)
    refs.lse_t[...] = jnp.transpose(refs.lse[...])[0:HEADS, :]
    refs.q, refs.k, refs.v
    both_ways(sp, lambda low: attend_back(refs, scalars, low))

    def unrotated(ref, here, there, cols):
        part = ref[here, cols]
        return (part * refs.cosine[there, :] - turned(part) * refs.sine[there, :]).astype(BF)

    for spot, block in enumerate(blocks_of(sp) + blocks_of(sp ^ 1)):
        put, there = slice(spot * BLK, (spot + 1) * BLK), block_rows(block)
        refs.dvp[put, :] = refs.dv[there, :].astype(BF)
        for panel in range(PANELS):
            cols = panel_cols(panel)
            refs.dkp[put, cols] = unrotated(refs.dk, there, there, cols)
            if spot < 2:
                refs.dqp[put, cols] = unrotated(refs.dq, put, there, cols)
    refs.send(refs.dqp, refs.dkp, refs.dvp)
    w_key, w_value = refs.w_key[...], refs.w_value[...]
    theirs = slice(ROWS, 2 * ROWS)
    ge_sib = dot_nt(refs.dkp[theirs, :], w_key) + dot_nt(refs.dvp[theirs, :], w_value)
    refs.ge_sib[...] = ge_sib.astype(BF)
    refs.send(refs.ge_sib)
    mine = slice(0, ROWS)
    return (
        dot_nt(refs.dqp[...], refs.w_query[...])
        + dot_nt(refs.dkp[mine, :], w_key)
        + dot_nt(refs.dvp[mine, :], w_value)
    )


def pre_attention_backward(refs, scalars):
    grad_normed, grad_gain = rms_back(refs.middle[...], refs.ffn_gain[...], ffn_input_grad(refs))
    grad_middle = refs.upstream[...] + grad_normed
    refs.grad_middle[...] = grad_middle
    refs.grad_gain[...] = grad_gain
    refs.send(refs.grad_middle, refs.grad_gain)
    refs.ge_own[...] = attention_backward(refs, scalars, grad_middle)
    refs.send(refs.ge_own)


def post_attention_backward(refs, scalars):
    grad_middle = refs.grad_middle[...]
    refs.ge_own[...] = grad_middle + attention_backward(refs, scalars, grad_middle)
    refs.send(refs.ge_own)


def attention_weight_grads(refs, at):
    step = PANELS * D
    store_panels(refs, at, dot_tn(refs.mixed[...], refs.grad_middle[...].astype(BF)))
    own, sib = refs.own[...], refs.sib[...]
    store_panels(refs, at + step, dot_tn(own, refs.dqp[...]))
    for k, ref in enumerate((refs.dkp, refs.dvp)):
        total = dot_tn(own, ref[0:ROWS, :]) + dot_tn(sib, ref[ROWS : 2 * ROWS, :])
        store_panels(refs, at + (k + 2) * step, total)


def last_weight_grads(refs, scalars):
    attention_weight_grads(refs, 0)
    if refs.grads.shape[0] > ATTN_ROWS:
        clear_tail(refs, ATTN_ROWS)


def post_ffn_backward(refs, scalars):
    attention_weight_grads(refs, FFN_ROWS)
    clear_tail(refs, FFN_ROWS + ATTN_ROWS)
    middle = refs.middle[...]
    gain = refs.attn_gain[...]
    ffn_in = (middle * inv_rms(middle) * gain).astype(BF)
    ffn_forward(refs, ffn_in)
    result = refs.result[...]
    out_gain = refs.ffn_gain[...]
    inputs = result * inv_rms(result) * out_gain
    grad_entry = refs.ge_own[...] + refs.ge_recv[...].astype(F32)
    grad_normed, grad_next = rms_back(inputs, refs.next_gain[...], grad_entry)
    grad_result, grad_ffn_gain = rms_back(result, out_gain, refs.grad_middle[...] + grad_normed)
    ffn_weight_grads(refs, 0, ffn_in, grad_result)
    grad_middle, grad_attn_gain = rms_back(middle, gain, grad_result + ffn_input_grad(refs))
    refs.new_middle[...] = grad_middle
    refs.send(refs.new_middle)
    gains = (refs.grad_gain[...], grad_next, grad_ffn_gain, grad_attn_gain)
    store_gains(refs, FFN_ROWS + ATTN_ROWS, gains)


def unpack(first, second, scalars, pieces, heights, gains):
    orders, count, rows = pieces
    shapes = [(height, D) for height in heights] + [(PANELS, LANES)] * gains

    def unpack(scalars_ref, first_ref, second_ref, *rest):
        outs, buffer, sems = rest[: len(shapes)], rest[-2], rest[-1]
        piece_copies(buffer, first_ref, second_ref, scalars_ref[0], sems, pieces, False)
        at = 0
        for height, out in zip(heights, outs):
            for panel in range(PANELS):
                out[:, panel_cols(panel)] = buffer[at : at + height, :].astype(F32)
                at += height
        if gains:
            block = buffer[at : at + GAIN_ROWS, :].astype(F32)
            for slot in range(gains):
                outs[len(heights) + slot][...] = block[PANELS * slot : PANELS * (slot + 1), :]

    return pl.pallas_call(
        unpack,
        name=unpack.__name__,
        out_shape=[jax.ShapeDtypeStruct(shape, F32) for shape in shapes],
        grid_spec=pltpu.PrefetchScalarGridSpec(
            num_scalar_prefetch=1,
            grid=(),
            in_specs=[pl.BlockSpec(memory_space=pl.ANY)] * 2,
            out_specs=[pl.BlockSpec(memory_space=pltpu.VMEM)] * len(shapes),
            scratch_shapes=[
                pltpu.VMEM((count * rows, LANES), BF),
                pltpu.SemaphoreType.DMA((count,)),
            ],
        ),
        compiler_params=pltpu.CompilerParams(vmem_limit_bytes=40 << 20),
        cost_estimate=pl.CostEstimate(
            flops=0, transcendentals=0, bytes_accessed=6 * count * rows * LANES
        ),
    )(scalars, first, second)


def solution(mesh):
    n_dp, n_sp = mesh.shape["dp"], mesh.shape["sp"]
    count = n_dp * n_sp
    if n_sp != 4 or n_dp & (n_dp - 1) or n_dp < 2:
        raise ValueError
    bits = count.bit_length() - 1

    def swap(array, move):
        return lax.ppermute(array, AXES, [(k, move(k)) for k in range(count)])

    def sibling(array):
        return swap(array, lambda k: k ^ 1)

    tail = list(range(3, bits))
    orders = ([1, 2] + tail, [2, 1] + tail)

    def pieces_for(used):
        return orders, count, pl.cdiv(pl.cdiv(used, count), 16) * 16

    class Sum:
        def __init__(self, keep, send):
            self.keep, self.wire, self.stage = keep, sibling(send), 0

        def move(self, stage):
            return lambda k: k ^ (1 << orders[k & 1][stage])

        def step(self):
            last = bits - 1
            if self.stage < last:
                half = self.keep.shape[0] // 2
                total = self.keep.astype(F32) + self.wire.astype(F32)
                self.wire = swap(total[half:].astype(BF), self.move(self.stage))
                self.keep = total[:half].astype(BF)
            else:
                if self.stage == last:
                    self.keep = (self.keep.astype(F32) + self.wire.astype(F32)).astype(BF)
                else:
                    self.keep = jnp.concatenate([self.keep, self.wire], axis=0)
                back = 2 * last - 1 - self.stage
                self.wire = sibling(self.keep) if back < 0 else swap(self.keep, self.move(back))
            self.stage += 1

        def before(self, array):
            array, self.wire = lax.optimization_barrier((array, self.wire))
            self.step()
            return array

        def finish(self):
            while self.stage < 2 * bits - 1:
                self.step()
            return self.keep, self.wire

    def body(tokens, lengths, *rest):
        out_grad = rest[-1]
        post_query, post_key, post_value, post_out, post_gate, post_up, post_down = rest[0:7]
        pre_query, pre_key, pre_value, pre_out, pre_gate, pre_up, pre_down = rest[9:16]
        gains = [rest[k].reshape(1, D) for k in (7, 8, 16, 17)]
        post_attn_gain, post_ffn_gain, pre_attn_gain, pre_ffn_gain = gains
        sp = lax.axis_index("sp")
        me = lax.axis_index("dp") * n_sp + sp
        chip = sp >> 1
        scalars = jnp.stack([me, sp, lengths[chip]]).astype(jnp.int32)

        def to_slot(array):
            mine = lax.dynamic_index_in_dim(array, chip, 0, keepdims=False)
            other = lax.dynamic_index_in_dim(array, 1 - chip, 0, keepdims=False)
            return jnp.concatenate([mine, swap(other, lambda k: k ^ 3)], axis=0)

        def from_slot(array):
            mine, other = array[:BLK], swap(array[BLK:], lambda k: k ^ 3)
            return jnp.where(chip == 0, jnp.stack([mine, other]), jnp.stack([other, mine]))

        inverse = 10000.0 ** (-jnp.arange(HD // 2, dtype=F32) * 2.0 / HD)
        angles = jnp.arange(SEQ, dtype=F32)[:, None] * inverse[None, :]
        cosine = jnp.tile(jnp.cos(angles), (1, 4))
        sine = jnp.tile(jnp.concatenate([-jnp.sin(angles), jnp.sin(angles)], axis=-1), (1, 2))
        tables = dict(cosine=cosine, sine=sine)

        own_one = to_slot(tokens)
        sib_one = sibling(own_one)
        cotangent = to_slot(out_grad)

        rows_bf, rows_f32, full_bf = ((ROWS, D), BF), ((ROWS, D), F32), ((SEQ, D), BF)
        wide_bf, wide_f32 = ((ROWS, FF), BF), ((ROWS, FF), F32)
        saved = dict(q=rows_bf, k=full_bf, v=full_bf, lse=((ROWS, LANES), F32), mixed=rows_bf)
        wide = dict(gate=wide_f32, up=wide_f32, hidden=wide_bf)
        wide_back = dict(dgate=wide_bf, dup=wide_bf)
        ffn_pieces = pieces_for(FFN_ROWS)
        both_pieces = pieces_for(FFN_ROWS + ATTN_ROWS + GAIN_ROWS)
        attn_pieces = pieces_for(ATTN_ROWS)
        post_ffn = dict(w_gate=post_gate.T, w_up=post_up.T, w_down=post_down)
        pre_ffn = dict(w_gate=pre_gate.T, w_up=pre_up.T, w_down=pre_down)

        q1, k1, v1, lse1, mixed1, middle1, result1, entry2 = run_kernel(
            post_forward,
            scalars,
            dict(own=own_one, w_key=post_key, w_value=post_value, w_query=post_query, **tables)
            | dict(sib=sib_one, w_out=post_out, attn_gain=post_attn_gain, **post_ffn)
            | dict(ffn_gain=post_ffn_gain, next_gain=pre_attn_gain),
            saved | dict(middle=rows_f32, result=rows_f32, entry=rows_bf),
            wide,
            flops=8 * 10**9,
        )
        sib_two = sibling(entry2)
        pre_out_shapes = dict(middle=rows_f32, output=rows_bf, upstream=rows_f32)
        q2, k2, v2, lse2, mixed2, middle2, out_rows, upstream2, dgate2, dup2, keep, send = run_kernel(
            pre_forward,
            scalars,
            dict(own=entry2, w_key=pre_key, w_value=pre_value, w_query=pre_query, **tables)
            | dict(sib=sib_two, result=result1, last_gain=post_ffn_gain, w_out=pre_out)
            | dict(ffn_gain=pre_ffn_gain, cotangent=cotangent, **pre_ffn),
            saved | pre_out_shapes | wide_back,
            wide,
            pieces=ffn_pieces,
            flops=14 * 10**9,
        )
        sum_ffn2 = Sum(keep, send)

        back_outs = dict(dqp=rows_bf, dkp=full_bf, dvp=full_bf, ge_sib=rows_bf)
        head_f32 = ((HEADS, ROWS), F32)
        full_f32 = ((SEQ, D), F32)
        back_scratch = dict(gmix=rows_bf, lse_t=head_f32, delta_t=head_f32, dq=rows_f32)
        back_scratch |= dict(dk=full_f32, dv=full_f32)

        dqp, dkp, dvp, ge_sib, grad_middle2, grad_gain, ge_own = run_kernel(
            pre_attention_backward,
            scalars,
            dict(dgate=dgate2, w_gate=pre_ffn["w_gate"], dup=dup2, w_up=pre_ffn["w_up"])
            | dict(middle=middle2, ffn_gain=pre_ffn_gain, upstream=upstream2)
            | dict(mixed=mixed2, w_out=pre_out, lse=lse2, q=q2, k=k2, v=v2, **tables)
            | dict(w_key=pre_key, w_value=pre_value, w_query=pre_query),
            back_outs | dict(grad_middle=rows_f32, grad_gain=((1, D), F32), ge_own=rows_f32),
            back_scratch,
            flops=12 * 10**9,
        )
        ge_recv = sibling(ge_sib)
        ge_recv = sum_ffn2.before(ge_recv)
        grad_middle1, keep, send = run_kernel(
            post_ffn_backward,
            scalars,
            dict(mixed=mixed2, grad_middle=grad_middle2, own=entry2, sib=sib_two)
            | dict(dqp=dqp, dkp=dkp, dvp=dvp, middle=middle1, attn_gain=post_attn_gain, **post_ffn)
            | dict(result=result1, ffn_gain=post_ffn_gain, ge_own=ge_own, ge_recv=ge_recv)
            | dict(next_gain=pre_attn_gain, grad_gain=grad_gain),
            dict(new_middle=rows_f32),
            wide | wide_back,
            pieces=both_pieces,
            flops=10 * 10**9,
        )
        sum_both = Sum(keep, send)
        grad_middle1 = sum_ffn2.before(grad_middle1)
        dqp, dkp, dvp, ge_sib, ge_own = run_kernel(
            post_attention_backward,
            scalars,
            dict(grad_middle=grad_middle1, mixed=mixed1, w_out=post_out)
            | dict(lse=lse1, q=q1, k=k1, v=v1, **tables)
            | dict(w_key=post_key, w_value=post_value, w_query=post_query),
            back_outs | dict(ge_own=rows_f32),
            back_scratch,
            flops=12 * 10**9,
        )
        dqp = sum_ffn2.before(dqp)
        dqp = sum_both.before(dqp)
        keep, send = run_kernel(
            last_weight_grads,
            scalars,
            dict(mixed=mixed1, grad_middle=grad_middle1, own=own_one, sib=sib_one)
            | dict(dqp=dqp, dkp=dkp, dvp=dvp),
            {},
            {},
            pieces=attn_pieces,
            flops=3 * 10**9,
        )
        sum_attn1 = Sum(keep, send)
        ge_recv = sibling(ge_sib)
        output = from_slot(out_rows)
        tokens_grad = from_slot((ge_own + ge_recv.astype(F32)).astype(BF))

        ffn_heights, attn_heights = [FF] * 3, [D] * 4
        down2, gate2, up2 = unpack(*sum_ffn2.finish(), scalars, ffn_pieces, ffn_heights, 0)
        both = unpack(*sum_both.finish(), scalars, both_pieces, ffn_heights + attn_heights, 4)
        down1, gate1, up1, out2, query2, key2, value2 = both[:7]
        gain_pre_ffn, gain_pre_attn, gain_post_ffn, gain_post_attn = (g.reshape(D) for g in both[7:])
        out1, query1, key1, value1 = unpack(
            *sum_attn1.finish(), scalars, attn_pieces, attn_heights, 0
        )
        post_grads = (query1, key1, value1, out1, gate1.T, up1.T, down1, gain_post_attn, gain_post_ffn)
        pre_grads = (query2, key2, value2, out2, gate2.T, up2.T, down2, gain_pre_attn, gain_pre_ffn)
        return (output, tokens_grad) + post_grads + pre_grads

    spread = P("dp", "sp", None)
    in_specs = (spread, P("dp")) + (P(),) * 18 + (spread,)
    out_specs = (spread, spread) + (P(),) * 18
    return jax.shard_map(body, mesh=mesh, in_specs=in_specs, out_specs=out_specs, check_vma=False)
```

```python
import jax
import jax.numpy as jnp
import numpy as np
from jax import lax
from jax.experimental import pallas as pl
from jax.experimental.pallas import tpu as pltpu
from jax.sharding import PartitionSpec as P

D = 512
HEADS = 8
HD = 64
FF = 1376
SEQ = 1024
EPS = 1e-06
NEG = -1000000000.0
AXES = ("dp", "sp")
BF = jnp.bfloat16
F32 = jnp.float32
LANES = 128
PANELS = D // LANES
BLK = SEQ // 4
ROWS = 2 * BLK
HALF = D // 2
SCALE = HD ** (-0.5)
FFN_ROWS = 3 * PANELS * FF
ATTN_ROWS = 4 * PANELS * D
GAIN_ROWS = 16
VMEM_LIMIT = 28 << 20


def dot(left, right):
    return lax.dot_general(left, right, (((1,), (0,)), ((), ())), preferred_element_type=F32)


def dot_nt(left, right):
    return lax.dot_general(left, right, (((1,), (1,)), ((), ())), preferred_element_type=F32)


def dot_tn(left, right):
    return lax.dot_general(left, right, (((0,), (0,)), ((), ())), preferred_element_type=F32)


def inv_rms(values):
    return lax.rsqrt(jnp.mean(values * values, axis=-1, keepdims=True) + EPS)


def rms_back(values, gain, upstream):
    scale = inv_rms(values)
    weighted = upstream * gain
    grad = scale * weighted - values * (
        scale * scale * scale * jnp.mean(weighted * values, axis=-1, keepdims=True)
    )
    grad_gain = jnp.sum(upstream * (values * scale), axis=0, keepdims=True)
    return grad, grad_gain


class Refs:
    def __init__(self, vmem, fetched, stored, sems):
        self.vmem, self.stored, self.sems = vmem, stored, sems
        self.waiting, self.sent = {}, []
        for name in fetched:
            copy = pltpu.make_async_copy(fetched[name], vmem[name], self.next_sem())
            copy.start()
            self.waiting[name] = copy

    used = 0

    def next_sem(self):
        self.used += 1
        return self.sems.at[self.used - 1]

    def __getattr__(self, name):
        if name in self.waiting:
            self.waiting.pop(name).wait()
        return self.vmem[name]

    def send(self, *refs):
        for ref in refs:
            for name in self.stored:
                if self.vmem[name] is ref:
                    copy = pltpu.make_async_copy(ref, self.stored[name], self.next_sem())
                    copy.start()
                    self.sent.append(copy)

    def finish(self):
        for name in list(self.waiting):
            self.waiting.pop(name).wait()
        for copy in self.sent:
            copy.wait()


def in_hbm(array):
    return pltpu.with_memory_space_constraint(array, pltpu.HBM)


def run_kernel(body, scalars, fetched, ins, outs, stored, scratch):
    names = list(ins) + list(outs) + list(fetched) + list(stored) + list(scratch)
    n_f, n_in, n_out, n_st = len(fetched), len(ins), len(outs), len(stored)
    shapes = [pltpu.VMEM(fetched[n].shape, fetched[n].dtype) for n in fetched]
    shapes += [pltpu.VMEM(*stored[n]) for n in stored]
    shapes += [pltpu.VMEM(*scratch[n]) for n in scratch]

    def kernel(scalars_ref, *args):
        head = n_f + n_in + n_out
        hbm_in, on_chip, hbm_out = args[:n_f], args[n_f:head], args[head : head + n_st]
        vmem = dict(zip(names, on_chip + args[head + n_st : -1]))
        refs = Refs(vmem, dict(zip(fetched, hbm_in)), dict(zip(stored, hbm_out)), args[-1])
        body(refs, scalars_ref)
        refs.finish()

    on_chip, off_chip = (pl.BlockSpec(memory_space=m) for m in (pltpu.VMEM, pltpu.HBM))
    made = pl.pallas_call(
        kernel,
        name=body.__name__,
        out_shape=[jax.ShapeDtypeStruct(*t[n]) for t in (outs, stored) for n in t],
        grid_spec=pltpu.PrefetchScalarGridSpec(
            num_scalar_prefetch=1,
            grid=(),
            in_specs=[off_chip] * n_f + [on_chip] * n_in,
            out_specs=[on_chip] * n_out + [off_chip] * n_st,
            scratch_shapes=shapes + [pltpu.SemaphoreType.DMA((max(n_f + n_st, 1),))],
        ),
        compiler_params=pltpu.CompilerParams(vmem_limit_bytes=VMEM_LIMIT),
        cost_estimate=pl.CostEstimate(flops=0, transcendentals=0, bytes_accessed=1),
    )(scalars, *[in_hbm(a) for a in fetched.values()], *ins.values())
    return list(made[:n_out]) + [in_hbm(a) for a in made[n_out:]]


def piece_position(j, me, order):
    where = 0
    for bit in order:
        where = where * 2 + (((me >> bit) & 1) ^ ((j >> bit) & 1))
    return where


def segments(pieces, start, end):
    rows = pieces[2]
    while start < end:
        stop = min(end, (start // rows + 1) * rows)
        yield start // rows, start % rows, start, stop - start
        start = stop


def put_rows(refs, pieces, start, block):
    orders, count, rows = pieces
    me = refs.me
    for j, inside, at, length in segments(pieces, start, start + block.shape[0]):
        spot = piece_position(j, me, orders[j & 1]) + ((me ^ j) & 1) * (count // 2)
        put = pl.ds(pl.multiple_of(spot * rows + inside, 16), length)
        refs.grads[put, :] = block[at - start : at - start + length, :]


def head_lanes(rows, which):
    lane = lax.broadcasted_iota(jnp.int32, (rows, LANES), 1)
    return (lane < HD) if which == 0 else (lane >= HD)


def only_head(panel, which):
    return jnp.where(head_lanes(panel.shape[0], which), panel, jnp.zeros_like(panel))


def turned(panel):
    lane = lax.broadcasted_iota(jnp.int32, panel.shape, 1)
    return jnp.where(
        lane % HD < HD // 2,
        pltpu.roll(panel, LANES - HD // 2, 1),
        pltpu.roll(panel, HD // 2, 1),
    )


def block_rows(index):
    return pl.ds(pl.multiple_of(index * BLK, BLK), BLK)


def rope_tables():
    lane = np.arange(LANES)
    inverse = np.float32(10000.0) ** (-np.arange(HD // 2, dtype=np.float32) * np.float32(2.0 / HD))
    places = np.concatenate([np.arange(BLK), np.arange(8) * BLK]).astype(np.float32)
    angles = (places[:, None] * inverse[None, :])[:, lane % (HD // 2)].astype(np.float64)
    sign = np.where(lane % HD < HD // 2, -1.0, 1.0)
    return np.cos(angles).astype(np.float32), (np.sin(angles) * sign).astype(np.float32)


def rope_of(refs, block):
    cosine, sine = refs.cosine[0:BLK, :], refs.sine[0:BLK, :]
    start = pl.ds(BLK + block, 1)
    start_cos, start_sin = refs.cosine[start, :], refs.sine[start, :]
    return cosine * start_cos - sine * start_sin, sine * start_cos + cosine * start_sin


def panel_cols(panel):
    return slice(panel * LANES, (panel + 1) * LANES)


def blocks_of(sp):
    return sp, 3 - sp


def project_heads(refs, sp, entry, own):
    for half, block in enumerate(blocks_of(sp)):
        here = slice(half * BLK, (half + 1) * BLK)
        there = block_rows(block)
        rows = entry[here, :]
        keys = dot(rows, refs.w_key[...])
        refs.v[there, :] = dot(rows, refs.w_value[...]).astype(BF)
        if own:
            queries = dot(rows, refs.w_query[...])
        cosine, sine = rope_of(refs, block)
        for panel in range(PANELS):
            cols = panel_cols(panel)
            part = keys[:, cols]
            refs.k[there, cols] = (part * cosine + turned(part) * sine).astype(BF)
            if own:
                part = queries[:, cols]
                refs.q[here, cols] = (part * cosine + turned(part) * sine).astype(BF) * SCALE


def query_blocks(sp, low):
    chip = sp >> 1
    return (block_rows(chip), low + 1), (block_rows(1 - chip), 4 - low)


def both_ways(sp, step):
    low = (sp & 1) ^ (sp >> 1)

    @pl.when(low == 0)
    def outer():
        step(0)

    @pl.when(low == 1)
    def inner():
        step(1)


def attend(refs, scalars, low):
    sp, length = scalars[1], scalars[2]
    lane = lax.broadcasted_iota(jnp.int32, (BLK, LANES), 1)

    def panel_step(panel, carry):
        cols = pl.ds(pl.multiple_of(panel * LANES, LANES), LANES)
        for rows, blocks in query_blocks(sp, low):
            seen = blocks * BLK
            queries = refs.q[rows, cols]
            outs, logs = [], []
            for which in range(2):
                scores = dot_nt(only_head(queries, which), refs.k[0:seen, cols])
                key_at = lax.broadcasted_iota(jnp.int32, (BLK, seen), 1)
                row_at = lax.broadcasted_iota(jnp.int32, (BLK, seen), 0) + (blocks - 1) * BLK
                scores = jnp.where((key_at <= row_at) & (key_at < length), scores, NEG)
                top = jnp.max(scores, axis=-1, keepdims=True)
                weights = jnp.exp(scores - top)
                total = jnp.sum(weights, axis=-1, keepdims=True)
                outs.append(dot(weights.astype(BF), refs.v[0:seen, cols]) / total)
                logs.append(top + jnp.log(total))
            refs.mixed[rows, cols] = jnp.where(head_lanes(BLK, 0), outs[0], outs[1]).astype(BF)
            kept = jnp.where(lane == 2 * panel, logs[0], refs.lse[rows, :])
            refs.lse[rows, :] = jnp.where(lane == 2 * panel + 1, logs[1], kept)
        return carry

    lax.fori_loop(0, PANELS, panel_step, 0)


def attention_forward(refs, scalars):
    sp = scalars[1]
    project_heads(refs, sp, refs.own, True)
    project_heads(refs, sp ^ 1, refs.sib, False)
    refs.send(refs.q, refs.k, refs.v)
    refs.lse[...] = jnp.zeros((ROWS, LANES), F32)
    both_ways(sp, lambda low: attend(refs, scalars, low))
    refs.send(refs.lse, refs.mixed)


def ffn_forward(refs, ffn_in):
    for half in range(2):
        rows = slice(half * BLK, (half + 1) * BLK)
        gate = dot_nt(ffn_in[rows, :], refs.w_gate[...])
        up = dot_nt(ffn_in[rows, :], refs.w_up[...])
        refs.gate[rows, :] = gate
        refs.up[rows, :] = up
        refs.hidden[rows, :] = (gate * jax.nn.sigmoid(gate) * up).astype(BF)


def store_panels(refs, at, grad):
    height, width = grad.shape
    for panel in range(width // LANES):
        block = grad[:, panel_cols(panel)].astype(BF)
        put_rows(refs, refs.pieces, at + panel * height, block)


def ffn_weight_grads(refs, at, ffn_in, grad_result):
    grad_down = grad_result.astype(BF)
    store_panels(refs, at, dot_tn(refs.hidden[...], grad_down))
    for half in range(2):
        rows = slice(half * BLK, (half + 1) * BLK)
        grad_hidden = dot_nt(grad_down[rows, :], refs.w_down[...])
        gate = refs.gate[rows, :]
        sigma = jax.nn.sigmoid(gate)
        grad_gate = grad_hidden * refs.up[rows, :] * (sigma * (1.0 + gate * (1.0 - sigma)))
        refs.dgate[rows, :] = grad_gate.astype(BF)
        refs.dup[rows, :] = (grad_hidden * (gate * sigma)).astype(BF)
    store_panels(refs, at + PANELS * FF, dot_tn(refs.dgate[...], ffn_in))
    store_panels(refs, at + 2 * PANELS * FF, dot_tn(refs.dup[...], ffn_in))


def ffn_input_grad(refs):
    return dot(refs.dgate[...], refs.w_gate[...]) + dot(refs.dup[...], refs.w_up[...])


def store_tail(refs, gains):
    end = refs.grads.shape[0]
    row = lax.broadcasted_iota(jnp.int32, (end - FFN_ROWS, LANES), 0)
    block = jnp.zeros((end - FFN_ROWS, LANES), F32)
    for slot, gain in enumerate(gains):
        for panel in range(PANELS):
            block = jnp.where(row == PANELS * slot + panel, gain[:, panel_cols(panel)], block)
    put_rows(refs, refs.pieces, FFN_ROWS, block.astype(BF))


def post_forward(refs, scalars):
    attention_forward(refs, scalars)
    middle = refs.own[...].astype(F32) + dot(refs.mixed[...], refs.w_out[...])
    refs.middle[...] = middle
    refs.send(refs.middle)
    state = middle * inv_rms(middle) * refs.attn_gain[...]
    ffn_forward(refs, state.astype(BF))
    result = state + dot(refs.hidden[...], refs.w_down[...])
    refs.result[...] = result
    refs.send(refs.result)
    output = result * inv_rms(result) * refs.ffn_gain[...]
    entry = output * inv_rms(output) * refs.next_gain[...]
    refs.entry[...] = entry.astype(BF)


def masked_cotangent(refs, scalars):
    sp, length = scalars[1], scalars[2]
    row = lax.broadcasted_iota(jnp.int32, (ROWS, D), 0)
    position = row + jnp.where(row < BLK, sp * BLK, (2 - sp) * BLK)
    return jnp.where(position < length, refs.cotangent[...].astype(F32), 0.0)


def pre_ffn_forward(refs, scalars):
    store_tail(refs, ())
    result = refs.result[...]
    inputs = result * inv_rms(result) * refs.last_gain[...]
    middle = inputs + dot(refs.mixed[...], refs.w_out[...])
    refs.middle[...] = middle
    ffn_in = (middle * inv_rms(middle) * refs.ffn_gain[...]).astype(BF)
    ffn_forward(refs, ffn_in)
    output = middle + dot(refs.hidden[...], refs.w_down[...])
    refs.output[...] = output.astype(BF)
    ffn_weight_grads(refs, 0, ffn_in, masked_cotangent(refs, scalars))


def attend_back(refs, scalars, low, first_panel):
    sp, length = scalars[1], scalars[2]
    if low == 1:
        refs.dk[3 * BLK :, :] = jnp.zeros((BLK, HALF), F32)
        refs.dv[3 * BLK :, :] = jnp.zeros((BLK, HALF), F32)

    def panel_step(panel, carry):
        cols = pl.ds(pl.multiple_of((first_panel + panel) * LANES, LANES), LANES)
        put = pl.ds(pl.multiple_of(panel * LANES, LANES), LANES)
        for rows, blocks in reversed(query_blocks(sp, low)):
            seen = blocks * BLK
            queries = refs.q[rows, cols]
            grads = refs.gmix[rows, cols]
            keys = refs.k[0:seen, cols]
            values = refs.v[0:seen, cols]
            key_at = lax.broadcasted_iota(jnp.int32, (seen, BLK), 0)
            row_at = lax.broadcasted_iota(jnp.int32, (seen, BLK), 1) + (blocks - 1) * BLK
            allowed = (key_at <= row_at) & (key_at < length)
            grad_q = jnp.zeros((BLK, LANES), F32)
            grad_k = jnp.zeros((seen, LANES), F32)
            grad_v = jnp.zeros((seen, LANES), F32)
            for which in range(2):
                q_head = only_head(queries, which)
                g_head = only_head(grads, which)
                at = pl.ds(2 * (first_panel + panel) + which, 1)
                scores = jnp.where(allowed, dot_nt(keys, q_head), NEG)
                probs = jnp.exp(scores - refs.lse_t[at, rows])
                grad_p = dot_nt(values, g_head)
                grad_s = (probs * (grad_p - refs.delta_t[at, rows])).astype(BF)
                grad_v = grad_v + dot(probs.astype(BF), g_head)
                grad_k = grad_k + dot(grad_s, q_head)
                grad_q = grad_q + dot_tn(grad_s, only_head(keys, which))
            refs.dq[rows, put] = grad_q * SCALE
            if blocks == 4 - low:
                refs.dk[0:seen, put] = grad_k
                refs.dv[0:seen, put] = grad_v
            else:
                refs.dk[0:seen, put] += grad_k
                refs.dv[0:seen, put] += grad_v
        return carry

    lax.fori_loop(0, PANELS // 2, panel_step, 0)


def start_attention_backward(refs, grad_middle):
    grad_mixed = dot_nt(grad_middle.astype(BF), refs.w_out[...]).astype(BF)
    refs.gmix[...] = grad_mixed
    product = grad_mixed.astype(F32) * refs.mixed[...].astype(F32)
    high = product.astype(BF)
    rest = (product - high.astype(F32)).astype(BF)
    head_of = lax.broadcasted_iota(jnp.int32, (HEADS, D), 1) // HD
    pick = (head_of == lax.broadcasted_iota(jnp.int32, (HEADS, D), 0)).astype(F32).astype(BF)
    refs.delta_t[...] = dot_nt(pick, high) + dot_nt(pick, rest)
    refs.lse_t[...] = jnp.transpose(refs.lse[...])[0:HEADS, :]


def attention_backward(refs, scalars, first_panel):
    sp = scalars[1]
    refs.q, refs.k, refs.v
    both_ways(sp, lambda low: attend_back(refs, scalars, low, first_panel))

    for spot, block in enumerate(blocks_of(sp) + blocks_of(sp ^ 1)):
        put, there = slice(spot * BLK, (spot + 1) * BLK), block_rows(block)
        refs.dvp[put, :] = refs.dv[there, :].astype(BF)
        cosine, sine = rope_of(refs, block)
        for panel in range(PANELS // 2):
            cols = panel_cols(panel)
            part = refs.dk[there, cols]
            refs.dkp[put, cols] = (part * cosine - turned(part) * sine).astype(BF)
            if spot < 2:
                part = refs.dq[put, cols]
                refs.dqp[put, cols] = (part * cosine - turned(part) * sine).astype(BF)
    cols = slice(first_panel * LANES, first_panel * LANES + HALF)
    w_query, w_key, w_value = refs.w_query[:, cols], refs.w_key[:, cols], refs.w_value[:, cols]
    mine, theirs = slice(0, ROWS), slice(ROWS, 2 * ROWS)
    ge_sib = dot_nt(refs.dkp[theirs, :], w_key) + dot_nt(refs.dvp[theirs, :], w_value)
    ge_own = (
        dot_nt(refs.dqp[...], w_query)
        + dot_nt(refs.dkp[mine, :], w_key)
        + dot_nt(refs.dvp[mine, :], w_value)
    )
    return ge_own, ge_sib


def first_heads_backward(refs, scalars):
    refs.ge_own[...], refs.ge_sib[...] = attention_backward(refs, scalars, 0)


def last_heads_backward(refs, scalars):
    ge_own, ge_sib = attention_backward(refs, scalars, PANELS // 2)
    refs.ge_own[...] = refs.part_own[...] + ge_own
    refs.ge_sib[...] = (refs.part_sib[...] + ge_sib).astype(BF)


def pre_middle_backward(refs, scalars):
    grad_normed, grad_gain = rms_back(refs.middle[...], refs.ffn_gain[...], ffn_input_grad(refs))
    grad_middle = masked_cotangent(refs, scalars) + grad_normed
    refs.grad_middle[...] = grad_middle
    refs.grad_gain[...] = grad_gain
    start_attention_backward(refs, grad_middle)


def attention_weight_grads(refs, scalars):
    step = PANELS * D
    store_panels(refs, 0, dot_tn(refs.mixed[...], refs.grad_middle[...].astype(BF)))
    own, sib = refs.own[...], refs.sib[...]
    for half in range(2):
        put = half * step // 2
        dqp, dkp, dvp = ((refs.dqa, refs.dka, refs.dva), (refs.dqb, refs.dkb, refs.dvb))[half]
        store_panels(refs, step + put, dot_tn(own, dqp[...]))
        for k, ref in enumerate((dkp, dvp)):
            total = dot_tn(own, ref[0:ROWS, :]) + dot_tn(sib, ref[ROWS : 2 * ROWS, :])
            store_panels(refs, (k + 2) * step + put, total)


def post_ffn_again(refs, scalars):
    middle = refs.middle[...]
    ffn_in = (middle * inv_rms(middle) * refs.attn_gain[...]).astype(BF)
    refs.ffn_in[...] = ffn_in
    ffn_forward(refs, ffn_in)


def post_ffn_backward(refs, scalars):
    middle, result = refs.middle[...], refs.result[...]
    out_gain = refs.ffn_gain[...]
    inputs = result * inv_rms(result) * out_gain
    grad_entry = refs.ge_own[...] + refs.ge_recv[...].astype(F32)
    grad_normed, grad_next = rms_back(inputs, refs.next_gain[...], grad_entry)
    grad_result, grad_ffn_gain = rms_back(result, out_gain, refs.grad_middle[...] + grad_normed)
    ffn_weight_grads(refs, 0, refs.ffn_in[...], grad_result)
    upstream = grad_result + ffn_input_grad(refs)
    grad_middle, grad_attn_gain = rms_back(middle, refs.attn_gain[...], upstream)
    refs.new_middle[...] = grad_middle
    store_tail(refs, (refs.grad_gain[...], grad_next, grad_ffn_gain, grad_attn_gain))
    start_attention_backward(refs, grad_middle)


def unpack(mine, other, scalars, pieces, heights, gains):
    orders, count, rows = pieces
    shapes = [(height, D) for height in heights] + [(PANELS, LANES)] * gains
    n_out = len(shapes)

    def unpack(scalars_ref, mine_ref, other_ref, *rest):
        outs, staged, sems = rest[:n_out], rest[n_out : 2 * n_out], rest[-1]
        me = scalars_ref[0]

        def lay_out(halves):
            sent, at = [], 0
            for k in range(n_out):
                height, width = shapes[k]
                if k < len(heights):
                    for panel in range(PANELS):
                        for j, inside, row, length in segments(pieces, at, at + height):
                            spot = piece_position(j, me, orders[j & 1]) * rows + inside
                            take = pl.ds(pl.multiple_of(spot, 16), length)
                            put = slice(row - at, row - at + length)
                            staged[k][put, panel_cols(panel)] = halves[j & 1][take, :].astype(F32)
                        at += height
                else:
                    if k == len(heights):
                        ((j, inside, row, length),) = segments(pieces, at, at + GAIN_ROWS)
                        spot = piece_position(j, me, orders[j & 1]) * rows + inside
                        take = pl.ds(pl.multiple_of(spot, 16), GAIN_ROWS)
                        block = halves[j & 1][take, :].astype(F32)
                    slot = (k - len(heights)) * PANELS
                    staged[k][...] = block[slot : slot + PANELS, :]
                sent.append(pltpu.make_async_copy(staged[k], outs[k], sems.at[k]))
                sent[-1].start()
            for copy in sent:
                copy.wait()

        @pl.when(me & 1 == 0)
        def even():
            lay_out((mine_ref, other_ref))

        @pl.when(me & 1 == 1)
        def odd():
            lay_out((other_ref, mine_ref))

    on_chip, off_chip = (pl.BlockSpec(memory_space=m) for m in (pltpu.VMEM, pltpu.HBM))
    return pl.pallas_call(
        unpack,
        name=unpack.__name__,
        out_shape=[jax.ShapeDtypeStruct(shape, F32) for shape in shapes],
        grid_spec=pltpu.PrefetchScalarGridSpec(
            num_scalar_prefetch=1,
            grid=(),
            in_specs=[on_chip] * 2,
            out_specs=[off_chip] * n_out,
            scratch_shapes=[pltpu.VMEM(shape, F32) for shape in shapes]
            + [pltpu.SemaphoreType.DMA((n_out,))],
        ),
        compiler_params=pltpu.CompilerParams(vmem_limit_bytes=VMEM_LIMIT),
        cost_estimate=pl.CostEstimate(flops=0, transcendentals=0, bytes_accessed=1),
    )(scalars, mine, other)


def solution(mesh):
    n_dp, n_sp = mesh.shape["dp"], mesh.shape["sp"]
    count = n_dp * n_sp
    if n_sp != 4 or n_dp & (n_dp - 1) or n_dp < 2:
        raise ValueError
    bits = count.bit_length() - 1

    def swap(array, move):
        return lax.ppermute(array, AXES, [(k, move(k)) for k in range(count)])

    def sibling(array):
        return swap(array, lambda k: k ^ 1)

    tail = list(range(3, bits))
    orders = ([1, 2] + tail, [2, 1] + tail)

    def pieces_for(used):
        return orders, count, pl.cdiv(pl.cdiv(used, count), 16) * 16

    class Chain:
        def __init__(self):
            self.token = None

        def after(self, *arrays):
            if self.token is None:
                return arrays
            return lax.optimization_barrier(arrays + (self.token,))[:-1]

    class Sum:
        def __init__(self, chain, pieces, heights, gains):
            self.chain, self.pieces, self.heights, self.gains = chain, pieces, heights, gains
            self.stage, self.result = 0, None

        def move(self, stage):
            return lambda k: k ^ (1 << orders[k & 1][stage])

        def put(self, grads):
            half = grads.shape[0] // 2
            sent = grads[half:]
            self.keep, self.wire = grads[:half], sibling(sent)
            self.chain.token = sent

        def step(self):
            last = bits - 1
            if self.stage > 2 * last:
                return
            keep, wire = self.chain.after(self.keep, self.wire)
            if self.stage < last:
                half = keep.shape[0] // 2
                total = keep.astype(F32) + wire.astype(F32)
                sent, self.keep = total[half:].astype(BF), total[:half].astype(BF)
                self.wire = swap(sent, self.move(self.stage))
            else:
                if self.stage == last:
                    sent = (keep.astype(F32) + wire.astype(F32)).astype(BF)
                else:
                    sent = jnp.concatenate([keep, wire], axis=0)
                back = 2 * last - 1 - self.stage
                self.keep = sent
                self.wire = sibling(sent) if back < 0 else swap(sent, self.move(back))
            self.chain.token = sent
            self.stage += 1

        def unpack(self, scalars):
            if self.result is None and self.stage == 2 * bits - 1:
                ready = self.chain.after(self.keep, self.wire)
                self.result = unpack(*ready, scalars, self.pieces, self.heights, self.gains)
                self.chain.token = self.result[-1]

    def body(tokens, lengths, *rest):
        out_grad = rest[-1]
        post_query, post_key, post_value, post_out, post_gate, post_up, post_down = rest[0:7]
        pre_query, pre_key, pre_value, pre_out, pre_gate, pre_up, pre_down = rest[9:16]
        gains = [rest[k].reshape(1, D) for k in (7, 8, 16, 17)]
        post_attn_gain, post_ffn_gain, pre_attn_gain, pre_ffn_gain = gains
        sp = lax.axis_index("sp")
        me = lax.axis_index("dp") * n_sp + sp
        chip = sp >> 1
        scalars = jnp.stack([me, sp, lengths[chip]]).astype(jnp.int32)

        def to_slot(array):
            mine = lax.dynamic_index_in_dim(array, chip, 0, keepdims=False)
            other = lax.dynamic_index_in_dim(array, 1 - chip, 0, keepdims=False)
            return jnp.concatenate([mine, swap(other, lambda k: k ^ 3)], axis=0)

        cosine, sine = rope_tables()
        tables = dict(cosine=cosine, sine=sine)

        own_one = to_slot(tokens)
        sib_one = sibling(own_one)
        cotangent = to_slot(out_grad)

        rows_bf, rows_f32, full_bf = ((ROWS, D), BF), ((ROWS, D), F32), ((SEQ, D), BF)
        wide_bf, wide_f32 = ((ROWS, FF), BF), ((ROWS, FF), F32)
        gain_f32, head_f32 = ((1, D), F32), ((HEADS, ROWS), F32)
        half_bf, half_f32 = ((SEQ, HALF), BF), ((SEQ, HALF), F32)
        half_rows_bf, half_rows_f32 = ((ROWS, HALF), BF), ((ROWS, HALF), F32)
        saved = dict(q=rows_bf, k=full_bf, v=full_bf, lse=((ROWS, LANES), F32), mixed=rows_bf)
        wide = dict(gate=wide_f32, up=wide_f32, hidden=wide_bf)
        wide_back = dict(dgate=wide_bf, dup=wide_bf)
        post_ffn = dict(w_gate=post_gate.T, w_up=post_up.T, w_down=post_down)
        pre_ffn = dict(w_gate=pre_gate.T, w_up=pre_up.T, w_down=pre_down)
        post_qkv = dict(w_key=post_key, w_value=post_value, w_query=post_query)
        pre_qkv = dict(w_key=pre_key, w_value=pre_value, w_query=pre_query)
        heads_outs = dict(dqp=half_rows_bf, dkp=half_bf, dvp=half_bf, ge_own=rows_f32)
        heads_tmp = dict(dq=half_rows_f32, dk=half_f32, dv=half_f32)
        start_outs = dict(gmix=rows_bf, delta_t=head_f32, lse_t=head_f32)

        chain = Chain()
        ffn_pieces, attn_pieces = pieces_for(FFN_ROWS + GAIN_ROWS), pieces_for(ATTN_ROWS)
        ffn_grads = dict(grads=((count * ffn_pieces[2], LANES), BF))
        attn_grads = dict(grads=((count * attn_pieces[2], LANES), BF))
        ffn2 = Sum(chain, ffn_pieces, [FF] * 3, 0)
        ffn1 = Sum(chain, ffn_pieces, [FF] * 3, 4)
        attn2 = Sum(chain, attn_pieces, [D] * 4, 0)
        attn1 = Sum(chain, attn_pieces, [D] * 4, 0)

        def run(body, fetched, ins, outs, stored, scratch, token=0, pieces=None):
            def bound(refs, scalars_ref):
                refs.pieces, refs.me = pieces, scalars_ref[0]
                body(refs, scalars_ref)

            bound.__name__ = body.__name__
            made = run_kernel(bound, *chain.after(scalars), fetched, ins, outs, stored, scratch)
            chain.token = made[token]
            return made

        class Home:
            def start(self, array):
                self.mine, (other,) = array[:BLK], chain.after(array[BLK:])
                self.wire = swap(other, lambda k: k ^ 3)
                chain.token = other

            def finish(self):
                mine, other = chain.after(self.mine, self.wire)
                ways = jnp.stack([mine, other]), jnp.stack([other, mine])
                self.result = jnp.where(chip == 0, *ways)
                chain.token = self.result

        home_output, home_grad = Home(), Home()

        entry2, q1, k1, v1, lse1, mixed1, middle1, result1 = run(
            post_forward,
            dict(**post_qkv, **tables, w_out=post_out, attn_gain=post_attn_gain, **post_ffn)
            | dict(ffn_gain=post_ffn_gain, next_gain=pre_attn_gain),
            dict(own=own_one, sib=sib_one),
            dict(entry=rows_bf),
            saved | dict(middle=rows_f32, result=rows_f32),
            wide,
        )
        sib_two = sibling(entry2)
        mixed2, q2, k2, v2, lse2 = run(
            attention_forward,
            dict(**pre_qkv, **tables),
            dict(own=entry2, sib=sib_two),
            dict(mixed=saved.pop("mixed")),
            saved,
            {},
        )
        (cotangent,) = chain.after(cotangent)
        middle2, out_rows, dgate, dup, grads = run(
            pre_ffn_forward,
            dict(w_out=pre_out, result=result1, last_gain=post_ffn_gain, ffn_gain=pre_ffn_gain)
            | pre_ffn,
            dict(mixed=mixed2, cotangent=cotangent),
            dict(middle=rows_f32, output=rows_bf) | wide_back | ffn_grads,
            {},
            wide,
            1,
            ffn_pieces,
        )
        ffn2.put(grads)
        home_output.start(out_rows)

        held = {}

        def middle_back():
            held[0] = run(
                pre_middle_backward,
                dict(w_gate=pre_ffn["w_gate"], w_up=pre_ffn["w_up"])
                | dict(ffn_gain=pre_ffn_gain, w_out=pre_out, lse=lse2),
                dict(dgate=dgate, dup=dup, middle=middle2, cotangent=cotangent, mixed=mixed2),
                dict(grad_middle=rows_f32, grad_gain=gain_f32) | start_outs,
                {},
                {},
                token=1,
            )

        def heads(start, arrays, weights, first):
            fetched = dict(zip(("q", "k", "v"), arrays)) | tables | weights
            ins = dict(zip(("gmix", "delta_t", "lse_t"), start))
            if first is None:
                outs = heads_outs | dict(ge_sib=rows_f32)
                return run(first_heads_backward, fetched, ins, outs, {}, heads_tmp, token=2)
            ins |= dict(part_own=first[3], part_sib=first[4])
            outs = heads_outs | dict(ge_sib=rows_bf)
            return run(last_heads_backward, fetched, ins, outs, {}, heads_tmp, token=4)

        def pre_heads_a():
            held[1] = heads(held[0][2:], (q2, k2, v2), pre_qkv, None)

        def pre_heads_b():
            held[2] = heads(held[0][2:], (q2, k2, v2), pre_qkv, held[1])
            held[3] = sibling(held[2][4])

        def ffn_again():
            held[4] = run(
                post_ffn_again,
                dict(middle=middle1, attn_gain=post_attn_gain)
                | dict(w_gate=post_ffn["w_gate"], w_up=post_ffn["w_up"]),
                {},
                dict(ffn_in=rows_bf) | wide,
                {},
                {},
            )

        def ffn_back():
            ins = dict(zip(("ffn_in", "gate", "up", "hidden"), held[4]))
            *rest, grads = run(
                post_ffn_backward,
                dict(middle=middle1, result=result1, ffn_gain=post_ffn_gain)
                | dict(next_gain=pre_attn_gain, attn_gain=post_attn_gain)
                | dict(**post_ffn, w_out=post_out, mixed=mixed1, lse=lse1),
                ins
                | dict(grad_middle=held[0][0], grad_gain=held[0][1])
                | dict(ge_own=held[2][3], ge_recv=held[3]),
                dict(new_middle=rows_f32) | start_outs | ffn_grads,
                {},
                wide_back,
                2,
                ffn_pieces,
            )
            held[5] = rest
            ffn1.put(grads)

        def weight_grads(total, fetched, grad_middle, own, sib, first, last):
            (grads,) = run(
                attention_weight_grads,
                fetched,
                dict(grad_middle=grad_middle, own=own, sib=sib)
                | dict(zip(("dqa", "dka", "dva"), first))
                | dict(zip(("dqb", "dkb", "dvb"), last))
                | ({} if fetched else dict(mixed=mixed2)),
                attn_grads,
                {},
                {},
                0,
                attn_pieces,
            )
            total.put(grads)

        def pre_weights():
            weight_grads(attn2, {}, held[0][0], entry2, sib_two, held[1], held[2])

        def post_heads_a():
            held[6] = heads(held[5][1:], (q1, k1, v1), post_qkv, None)

        def post_heads_b():
            held[7] = heads(held[5][1:], (q1, k1, v1), post_qkv, held[6])
            held[8] = sibling(held[7][4])

        def post_weights():
            saved_mix = dict(mixed=mixed1)
            weight_grads(attn1, saved_mix, held[5][0], own_one, sib_one, held[6], held[7])

        def send_grad():
            total = held[5][0] + held[7][3] + held[8].astype(F32)
            home_grad.start(total.astype(BF))


        plan = (
            middle_back,
            ffn2,
            pre_heads_a,
            pre_heads_b,
            ffn2,
            home_output.finish,
            ffn_again,
            ffn_back,
            ffn2,
            ffn1,
            pre_weights,
            ffn2,
            attn2,
            post_heads_a,
            ffn2,
            ffn1,
            attn2,
            post_heads_b,
            ffn2,
            ffn1,
            attn2,
            post_weights,
            send_grad,
            ffn2,
            ffn1,
            attn2,
            attn1,
            home_grad.finish,
        )
        for action in plan:
            if isinstance(action, Sum):
                action.step()
            else:
                action()
        sums = (ffn2, ffn1, attn2, attn1)
        for again in range(2 * bits):
            for total in sums:
                total.step()
        for total in sums:
            total.unpack(scalars)
        down2, gate2, up2 = ffn2.result
        down1, gate1, up1, *gains = ffn1.result
        gain_pre_ffn, gain_pre_attn, gain_post_ffn, gain_post_attn = (g.reshape(D) for g in gains)
        out2, query2, key2, value2 = attn2.result
        out1, query1, key1, value1 = attn1.result
        post_grads = (query1, key1, value1, out1, gate1.T, up1.T, down1, gain_post_attn, gain_post_ffn)
        pre_grads = (query2, key2, value2, out2, gate2.T, up2.T, down2, gain_pre_attn, gain_pre_ffn)
        return (home_output.result, home_grad.result) + post_grads + pre_grads

    spread = P("dp", "sp", None)
    in_specs = (spread, P("dp")) + (P(),) * 18 + (spread,)
    out_specs = (spread, spread) + (P(),) * 18
    return jax.shard_map(body, mesh=mesh, in_specs=in_specs, out_specs=out_specs, check_vma=False)
```

```python
import jax
import jax.numpy as jnp
import numpy as np
from jax import lax
from jax.experimental import pallas as pl
from jax.experimental.pallas import tpu as pltpu
from jax.sharding import PartitionSpec as P

D = 512
HEADS = 8
HD = 64
FF = 1376
SEQ = 1024
EPS = 1e-06
NEG = -1000000000.0
AXES = ("dp", "sp")
BF = jnp.bfloat16
F32 = jnp.float32
LANES = 128
PANELS = D // LANES
BLK = SEQ // 4
ROWS = 2 * BLK
HALF = D // 2
SCALE = HD ** (-0.5)
FFN_ROWS = 3 * PANELS * FF
ATTN_ROWS = 4 * PANELS * D
GAIN_ROWS = 16
KEPT = "kept"
VMEM_LIMIT = 28 << 20


def dot(left, right):
    return lax.dot_general(left, right, (((1,), (0,)), ((), ())), preferred_element_type=F32)


def dot_nt(left, right):
    return lax.dot_general(left, right, (((1,), (1,)), ((), ())), preferred_element_type=F32)


def dot_tn(left, right):
    return lax.dot_general(left, right, (((0,), (0,)), ((), ())), preferred_element_type=F32)


def inv_rms(values):
    return lax.rsqrt(jnp.mean(values * values, axis=-1, keepdims=True) + EPS)


def rms_back(values, gain, upstream):
    scale = inv_rms(values)
    weighted = upstream * gain
    grad = scale * weighted - values * (
        scale * scale * scale * jnp.mean(weighted * values, axis=-1, keepdims=True)
    )
    grad_gain = jnp.sum(upstream * (values * scale), axis=0, keepdims=True)
    return grad, grad_gain


class Refs:
    def __init__(self, vmem, fetched, stored, sems):
        self.vmem, self.stored, self.sems = vmem, stored, sems
        self.waiting, self.sent = {}, []
        for name in fetched:
            copy = pltpu.make_async_copy(fetched[name], vmem[name], self.next_sem())
            copy.start()
            self.waiting[name] = copy

    used = 0

    def next_sem(self):
        self.used += 1
        return self.sems.at[self.used - 1]

    def __getattr__(self, name):
        if name in self.waiting:
            self.waiting.pop(name).wait()
        return self.vmem[name]

    def send(self, *refs):
        for ref in refs:
            for name in self.stored:
                if self.vmem[name] is ref:
                    self.send_as(name, ref)

    def send_as(self, name, ref):
        if name in self.stored:
            copy = pltpu.make_async_copy(ref, self.stored[name], self.next_sem())
            copy.start()
            self.sent.append(copy)

    def finish(self):
        for name in list(self.waiting):
            self.waiting.pop(name).wait()
        for copy in self.sent:
            copy.wait()


class Columns:
    def __init__(self, array, start):
        self.array, self.start = array, start


def in_hbm(array):
    if isinstance(array, Columns):
        array = array.array
    return pltpu.with_memory_space_constraint(array, pltpu.HBM)


def run_kernel(body, scalars, fetched, ins, outs, stored, scratch, mflops):
    names = list(ins) + list(outs) + list(fetched) + list(stored) + list(scratch)
    n_f, n_in, n_out, n_st = len(fetched), len(ins), len(outs), len(stored)
    shapes = []
    for array in fetched.values():
        if isinstance(array, Columns):
            shapes.append(pltpu.VMEM((array.array.shape[0], HALF), array.array.dtype))
        else:
            shapes.append(pltpu.VMEM(array.shape, array.dtype))
    shapes += [pltpu.VMEM((8, LANES) if n == KEPT else stored[n][0], stored[n][1]) for n in stored]
    shapes += [pltpu.VMEM(*scratch[n]) for n in scratch]

    def kernel(scalars_ref, *args):
        head = n_f + n_in + n_out
        hbm_in, on_chip, hbm_out = list(args[:n_f]), args[n_f:head], args[head : head + n_st]
        for k, array in enumerate(fetched.values()):
            if isinstance(array, Columns):
                hbm_in[k] = hbm_in[k].at[:, pl.ds(array.start, HALF)]
        vmem = dict(zip(names, on_chip + args[head + n_st : -1]))
        refs = Refs(vmem, dict(zip(fetched, hbm_in)), dict(zip(stored, hbm_out)), args[-1])
        body(refs, scalars_ref)
        refs.finish()

    on_chip, off_chip = (pl.BlockSpec(memory_space=m) for m in (pltpu.VMEM, pltpu.HBM))
    made = pl.pallas_call(
        kernel,
        name=body.__name__,
        out_shape=[jax.ShapeDtypeStruct(*outs[n]) for n in outs]
        + [pltpu.HBM(*stored[n]) for n in stored],
        grid_spec=pltpu.PrefetchScalarGridSpec(
            num_scalar_prefetch=1,
            grid=(),
            in_specs=[off_chip] * n_f + [on_chip] * n_in,
            out_specs=[on_chip] * n_out + [off_chip] * n_st,
            scratch_shapes=shapes + [pltpu.SemaphoreType.DMA((max(n_f + n_st, 1),))],
        ),
        compiler_params=pltpu.CompilerParams(vmem_limit_bytes=VMEM_LIMIT),
        cost_estimate=pl.CostEstimate(flops=mflops * 10**6, transcendentals=0, bytes_accessed=1),
    )(scalars, *[in_hbm(a) for a in fetched.values()], *ins.values())
    return made


def piece_position(j, me, order):
    where = 0
    for bit in order:
        where = where * 2 + (((me >> bit) & 1) ^ ((j >> bit) & 1))
    return where


def segments(pieces, start, end):
    rows = pieces[2]
    while start < end:
        stop = min(end, (start // rows + 1) * rows)
        yield start // rows, start % rows, start, stop - start
        start = stop


def put_rows(refs, pieces, start, block):
    orders, count, rows = pieces
    me = refs.me
    for j, inside, at, length in segments(pieces, start, start + block.shape[0]):
        spot = piece_position(j, me, orders[j & 1]) + ((me ^ j) & 1) * (count // 2)
        put = pl.ds(pl.multiple_of(spot * rows + inside, 16), length)
        refs.grads[put, :] = block[at - start : at - start + length, :]


def head_lanes(rows, which):
    lane = lax.broadcasted_iota(jnp.int32, (rows, LANES), 1)
    return (lane < HD) if which == 0 else (lane >= HD)


def only_head(panel, which):
    return jnp.where(head_lanes(panel.shape[0], which), panel, jnp.zeros_like(panel))


def turned(panel):
    lane = lax.broadcasted_iota(jnp.int32, panel.shape, 1)
    return jnp.where(
        lane % HD < HD // 2,
        pltpu.roll(panel, LANES - HD // 2, 1),
        pltpu.roll(panel, HD // 2, 1),
    )


def block_rows(index):
    return pl.ds(pl.multiple_of(index * BLK, BLK), BLK)


def rope_tables():
    lane = np.arange(LANES)
    inverse = np.float32(10000.0) ** (-np.arange(HD // 2, dtype=np.float32) * np.float32(2.0 / HD))
    places = np.concatenate([np.arange(BLK), np.arange(8) * BLK]).astype(np.float32)
    angles = (places[:, None] * inverse[None, :])[:, lane % (HD // 2)].astype(np.float64)
    sign = np.where(lane % HD < HD // 2, -1.0, 1.0)
    return np.cos(angles).astype(np.float32), (np.sin(angles) * sign).astype(np.float32)


def rope_of(refs, block):
    cosine, sine = refs.cosine[0:BLK, :], refs.sine[0:BLK, :]
    start = pl.ds(BLK + block, 1)
    start_cos, start_sin = refs.cosine[start, :], refs.sine[start, :]
    return cosine * start_cos - sine * start_sin, sine * start_cos + cosine * start_sin


def panel_cols(panel):
    return slice(panel * LANES, (panel + 1) * LANES)


def blocks_of(sp):
    return sp, 3 - sp


def project_heads(refs, sp, entry, own):
    for half, block in enumerate(blocks_of(sp)):
        here = slice(half * BLK, (half + 1) * BLK)
        there = block_rows(block)
        rows = entry[here, :]
        keys = dot(rows, refs.w_key[...])
        refs.v[there, :] = dot(rows, refs.w_value[...]).astype(BF)
        if own:
            queries = dot(rows, refs.w_query[...])
        cosine, sine = rope_of(refs, block)
        for panel in range(PANELS):
            cols = panel_cols(panel)
            part = keys[:, cols]
            refs.k[there, cols] = (part * cosine + turned(part) * sine).astype(BF)
            if own:
                part = queries[:, cols]
                refs.q[here, cols] = (part * cosine + turned(part) * sine).astype(BF) * SCALE


def query_blocks(sp, low):
    chip = sp >> 1
    return (block_rows(chip), low + 1), (block_rows(1 - chip), 4 - low)


def both_ways(sp, step):
    low = (sp & 1) ^ (sp >> 1)

    @pl.when(low == 0)
    def outer():
        step(0)

    @pl.when(low == 1)
    def inner():
        step(1)


def attend(refs, scalars, low):
    sp, length = scalars[1], scalars[2]
    lane = lax.broadcasted_iota(jnp.int32, (BLK, LANES), 1)

    def panel_step(panel, carry):
        cols = pl.ds(pl.multiple_of(panel * LANES, LANES), LANES)
        for rows, blocks in query_blocks(sp, low):
            seen = blocks * BLK
            queries = refs.q[rows, cols]
            outs, logs = [], []
            for which in range(2):
                scores = dot_nt(only_head(queries, which), refs.k[0:seen, cols])
                key_at = lax.broadcasted_iota(jnp.int32, (BLK, seen), 1)
                row_at = lax.broadcasted_iota(jnp.int32, (BLK, seen), 0) + (blocks - 1) * BLK
                scores = jnp.where((key_at <= row_at) & (key_at < length), scores, NEG)
                top = jnp.max(scores, axis=-1, keepdims=True)
                weights = jnp.exp(scores - top)
                total = jnp.sum(weights, axis=-1, keepdims=True)
                outs.append(dot(weights.astype(BF), refs.v[0:seen, cols]) / total)
                logs.append(top + jnp.log(total))
            refs.mixed[rows, cols] = jnp.where(head_lanes(BLK, 0), outs[0], outs[1]).astype(BF)
            kept = jnp.where(lane == 2 * panel, logs[0], refs.lse[rows, :])
            refs.lse[rows, :] = jnp.where(lane == 2 * panel + 1, logs[1], kept)
        return carry

    lax.fori_loop(0, PANELS, panel_step, 0)


def attention_forward(refs, scalars):
    sp = scalars[1]
    project_heads(refs, sp, refs.own, True)
    project_heads(refs, sp ^ 1, refs.sib, False)
    refs.send(refs.q, refs.k, refs.v)
    refs.lse[...] = jnp.zeros((ROWS, LANES), F32)
    both_ways(sp, lambda low: attend(refs, scalars, low))
    refs.send(refs.lse, refs.mixed)
    refs.send_as(KEPT, refs.mixed)


def ffn_forward(refs, ffn_in):
    for half in range(2):
        rows = slice(half * BLK, (half + 1) * BLK)
        gate = dot_nt(ffn_in[rows, :], refs.w_gate[...])
        up = dot_nt(ffn_in[rows, :], refs.w_up[...])
        refs.gate[rows, :] = gate
        refs.up[rows, :] = up
        refs.hidden[rows, :] = (gate * jax.nn.sigmoid(gate) * up).astype(BF)


def store_panels(refs, at, grad):
    height, width = grad.shape
    for panel in range(width // LANES):
        block = grad[:, panel_cols(panel)].astype(BF)
        put_rows(refs, refs.pieces, at + panel * height, block)


def ffn_weight_grads(refs, at, ffn_in, grad_result):
    grad_down = grad_result.astype(BF)
    store_panels(refs, at, dot_tn(refs.hidden[...], grad_down))
    for half in range(2):
        rows = slice(half * BLK, (half + 1) * BLK)
        grad_hidden = dot_nt(grad_down[rows, :], refs.w_down[...])
        gate = refs.gate[rows, :]
        sigma = jax.nn.sigmoid(gate)
        grad_gate = grad_hidden * refs.up[rows, :] * (sigma * (1.0 + gate * (1.0 - sigma)))
        refs.dgate[rows, :] = grad_gate.astype(BF)
        refs.dup[rows, :] = (grad_hidden * (gate * sigma)).astype(BF)
    store_panels(refs, at + PANELS * FF, dot_tn(refs.dgate[...], ffn_in))
    store_panels(refs, at + 2 * PANELS * FF, dot_tn(refs.dup[...], ffn_in))


def ffn_input_grad(refs):
    return dot(refs.dgate[...], refs.w_gate[...]) + dot(refs.dup[...], refs.w_up[...])


def store_tail(refs, gains):
    end = refs.grads.shape[0]
    row = lax.broadcasted_iota(jnp.int32, (end - FFN_ROWS, LANES), 0)
    block = jnp.zeros((end - FFN_ROWS, LANES), F32)
    for slot, gain in enumerate(gains):
        for panel in range(PANELS):
            block = jnp.where(row == PANELS * slot + panel, gain[:, panel_cols(panel)], block)
    put_rows(refs, refs.pieces, FFN_ROWS, block.astype(BF))


def post_forward(refs, scalars):
    attention_forward(refs, scalars)
    middle = refs.own[...].astype(F32) + dot(refs.mixed[...], refs.w_out[...])
    refs.middle[...] = middle
    refs.send(refs.middle)
    state = middle * inv_rms(middle) * refs.attn_gain[...]
    ffn_forward(refs, state.astype(BF))
    result = state + dot(refs.hidden[...], refs.w_down[...])
    refs.result[...] = result
    refs.send(refs.result)
    output = result * inv_rms(result) * refs.ffn_gain[...]
    entry = output * inv_rms(output) * refs.next_gain[...]
    refs.entry[...] = entry.astype(BF)


def masked_cotangent(refs, scalars):
    sp, length = scalars[1], scalars[2]
    row = lax.broadcasted_iota(jnp.int32, (BLK, D), 0)
    parts = []
    for block, ref in zip(blocks_of(sp), (refs.cot_mine, refs.cot_other)):
        parts.append(jnp.where(row + block * BLK < length, ref[...].astype(F32), 0.0))
    return jnp.concatenate(parts, axis=0)


def attend_back(refs, scalars, low, first_panel):
    sp, length = scalars[1], scalars[2]
    if low == 1:
        refs.dk[3 * BLK :, :] = jnp.zeros((BLK, HALF), F32)
        refs.dv[3 * BLK :, :] = jnp.zeros((BLK, HALF), F32)

    def panel_step(panel, carry):
        cols = pl.ds(pl.multiple_of((first_panel + panel) * LANES, LANES), LANES)
        put = pl.ds(pl.multiple_of(panel * LANES, LANES), LANES)
        for rows, blocks in reversed(query_blocks(sp, low)):
            seen = blocks * BLK
            queries = refs.q[rows, put]
            grads = refs.gmix[rows, cols]
            keys = refs.k[0:seen, put]
            values = refs.v[0:seen, put]
            key_at = lax.broadcasted_iota(jnp.int32, (seen, BLK), 0)
            row_at = lax.broadcasted_iota(jnp.int32, (seen, BLK), 1) + (blocks - 1) * BLK
            allowed = (key_at <= row_at) & (key_at < length)
            grad_q = jnp.zeros((BLK, LANES), F32)
            grad_k = jnp.zeros((seen, LANES), F32)
            grad_v = jnp.zeros((seen, LANES), F32)
            for which in range(2):
                q_head = only_head(queries, which)
                g_head = only_head(grads, which)
                at = pl.ds(2 * (first_panel + panel) + which, 1)
                scores = jnp.where(allowed, dot_nt(keys, q_head), NEG)
                probs = jnp.exp(scores - refs.lse_t[at, rows])
                grad_p = dot_nt(values, g_head)
                grad_s = (probs * (grad_p - refs.delta_t[at, rows])).astype(BF)
                grad_v = grad_v + dot(probs.astype(BF), g_head)
                grad_k = grad_k + dot(grad_s, q_head)
                grad_q = grad_q + dot_tn(grad_s, only_head(keys, which))
            refs.dq[rows, put] = grad_q * SCALE
            if blocks == 4 - low:
                refs.dk[0:seen, put] = grad_k
                refs.dv[0:seen, put] = grad_v
            else:
                refs.dk[0:seen, put] += grad_k
                refs.dv[0:seen, put] += grad_v
        return carry

    lax.fori_loop(0, PANELS // 2, panel_step, 0)


def start_attention_backward(refs, grad_middle):
    grad_mixed = dot_nt(grad_middle.astype(BF), refs.w_out[...]).astype(BF)
    refs.gmix[...] = grad_mixed
    product = grad_mixed.astype(F32) * refs.mixed[...].astype(F32)
    high = product.astype(BF)
    rest = (product - high.astype(F32)).astype(BF)
    head_of = lax.broadcasted_iota(jnp.int32, (HEADS, D), 1) // HD
    pick = (head_of == lax.broadcasted_iota(jnp.int32, (HEADS, D), 0)).astype(F32).astype(BF)
    refs.delta_t[...] = dot_nt(pick, high) + dot_nt(pick, rest)
    refs.lse_t[...] = jnp.transpose(refs.lse[...])[0:HEADS, :]


def attention_backward(refs, scalars, first_panel):
    sp = scalars[1]
    refs.q, refs.k, refs.v
    both_ways(sp, lambda low: attend_back(refs, scalars, low, first_panel))

    for spot, block in enumerate(blocks_of(sp) + blocks_of(sp ^ 1)):
        put, there = slice(spot * BLK, (spot + 1) * BLK), block_rows(block)
        refs.dvp[put, :] = refs.dv[there, :].astype(BF)
        cosine, sine = rope_of(refs, block)
        for panel in range(PANELS // 2):
            cols = panel_cols(panel)
            part = refs.dk[there, cols]
            refs.dkp[put, cols] = (part * cosine - turned(part) * sine).astype(BF)
            if spot < 2:
                part = refs.dq[put, cols]
                refs.dqp[put, cols] = (part * cosine - turned(part) * sine).astype(BF)
    w_query, w_key, w_value = refs.w_query[...], refs.w_key[...], refs.w_value[...]
    mine, theirs = slice(0, ROWS), slice(ROWS, 2 * ROWS)
    ge_sib = dot_nt(refs.dkp[theirs, :], w_key) + dot_nt(refs.dvp[theirs, :], w_value)
    ge_own = (
        dot_nt(refs.dqp[...], w_query)
        + dot_nt(refs.dkp[mine, :], w_key)
        + dot_nt(refs.dvp[mine, :], w_value)
    )
    return ge_own, ge_sib


def first_heads_backward(refs, scalars):
    refs.ge_own[...], refs.ge_sib[...] = attention_backward(refs, scalars, 0)


def last_heads_backward(refs, scalars):
    ge_own, ge_sib = attention_backward(refs, scalars, PANELS // 2)
    refs.ge_own[...] = refs.part_own[...] + ge_own
    refs.ge_sib[...] = (refs.part_sib[...] + ge_sib).astype(BF)


def pre_ffn(refs, scalars):
    store_tail(refs, ())
    result = refs.result[...]
    inputs = result * inv_rms(result) * refs.last_gain[...]
    middle = inputs + dot(refs.mixed[...], refs.w_out[...])
    gain = refs.ffn_gain[...]
    ffn_in = (middle * inv_rms(middle) * gain).astype(BF)
    ffn_forward(refs, ffn_in)
    output = middle + dot(refs.hidden[...], refs.w_down[...])
    refs.output[...] = output.astype(BF)
    cotangent = masked_cotangent(refs, scalars)
    ffn_weight_grads(refs, 0, ffn_in, cotangent)
    grad_normed, grad_gain = rms_back(middle, gain, ffn_input_grad(refs))
    grad_middle = cotangent + grad_normed
    refs.grad_middle[...] = grad_middle
    refs.grad_gain[...] = grad_gain
    start_attention_backward(refs, grad_middle)


def attention_weight_grads(refs, scalars):
    step = PANELS * D
    store_panels(refs, 0, dot_tn(refs.mixed[...], refs.grad_middle[...].astype(BF)))
    own, sib = refs.own[...], refs.sib[...]
    for half in range(2):
        put = half * step // 2
        dqp, dkp, dvp = ((refs.dqa, refs.dka, refs.dva), (refs.dqb, refs.dkb, refs.dvb))[half]
        store_panels(refs, step + put, dot_tn(own, dqp[...]))
        for k, ref in enumerate((dkp, dvp)):
            total = dot_tn(own, ref[0:ROWS, :]) + dot_tn(sib, ref[ROWS : 2 * ROWS, :])
            store_panels(refs, (k + 2) * step + put, total)


def post_ffn_again(refs, scalars):
    middle = refs.middle[...]
    ffn_in = (middle * inv_rms(middle) * refs.attn_gain[...]).astype(BF)
    refs.ffn_in[...] = ffn_in
    ffn_forward(refs, ffn_in)


def post_ffn_backward(refs, scalars):
    middle, result = refs.middle[...], refs.result[...]
    out_gain = refs.ffn_gain[...]
    inputs = result * inv_rms(result) * out_gain
    grad_entry = refs.ge_own[...] + refs.ge_recv[...].astype(F32)
    grad_normed, grad_next = rms_back(inputs, refs.next_gain[...], grad_entry)
    grad_result, grad_ffn_gain = rms_back(result, out_gain, refs.grad_middle[...] + grad_normed)
    ffn_weight_grads(refs, 0, refs.ffn_in[...], grad_result)
    upstream = grad_result + ffn_input_grad(refs)
    grad_middle, grad_attn_gain = rms_back(middle, refs.attn_gain[...], upstream)
    refs.new_middle[...] = grad_middle
    store_tail(refs, (refs.grad_gain[...], grad_next, grad_ffn_gain, grad_attn_gain))
    start_attention_backward(refs, grad_middle)


MFLOPS = {
    post_forward: 160000,
    attention_forward: 120000,
    pre_ffn: 140000,
    first_heads_backward: 90000,
    last_heads_backward: 90000,
    post_ffn_again: 50000,
    post_ffn_backward: 110000,
    attention_weight_grads: 30000,
}


def unpack(mine, other, scalars, pieces, heights, gains):
    orders, count, rows = pieces
    shapes = [(height, D) for height in heights] + [(PANELS, LANES)] * gains
    n_out = len(shapes)

    def unpack(scalars_ref, mine_ref, other_ref, *rest):
        outs, staged, sems = rest[:n_out], rest[n_out : 2 * n_out], rest[-1]
        me = scalars_ref[0]

        def lay_out(halves):
            sent, at = [], 0
            for k in range(n_out):
                height, width = shapes[k]
                if k < len(heights):
                    for panel in range(PANELS):
                        for j, inside, row, length in segments(pieces, at, at + height):
                            spot = piece_position(j, me, orders[j & 1]) * rows + inside
                            take = pl.ds(pl.multiple_of(spot, 16), length)
                            put = slice(row - at, row - at + length)
                            staged[k][put, panel_cols(panel)] = halves[j & 1][take, :].astype(F32)
                        at += height
                else:
                    if k == len(heights):
                        ((j, inside, row, length),) = segments(pieces, at, at + GAIN_ROWS)
                        spot = piece_position(j, me, orders[j & 1]) * rows + inside
                        take = pl.ds(pl.multiple_of(spot, 16), GAIN_ROWS)
                        block = halves[j & 1][take, :].astype(F32)
                    slot = (k - len(heights)) * PANELS
                    staged[k][...] = block[slot : slot + PANELS, :]
                sent.append(pltpu.make_async_copy(staged[k], outs[k], sems.at[k]))
                sent[-1].start()
            for copy in sent:
                copy.wait()

        @pl.when(me & 1 == 0)
        def even():
            lay_out((mine_ref, other_ref))

        @pl.when(me & 1 == 1)
        def odd():
            lay_out((other_ref, mine_ref))

    on_chip, off_chip = (pl.BlockSpec(memory_space=m) for m in (pltpu.VMEM, pltpu.HBM))
    return pl.pallas_call(
        unpack,
        name=unpack.__name__,
        out_shape=[jax.ShapeDtypeStruct(shape, F32) for shape in shapes],
        grid_spec=pltpu.PrefetchScalarGridSpec(
            num_scalar_prefetch=1,
            grid=(),
            in_specs=[on_chip] * 2,
            out_specs=[off_chip] * n_out,
            scratch_shapes=[pltpu.VMEM(shape, F32) for shape in shapes]
            + [pltpu.SemaphoreType.DMA((n_out,))],
        ),
        compiler_params=pltpu.CompilerParams(vmem_limit_bytes=VMEM_LIMIT),
        cost_estimate=pl.CostEstimate(
            flops=0, transcendentals=0, bytes_accessed=6 * mine.shape[0] * LANES * 2
        ),
    )(scalars, mine, other)


def solution(mesh):
    n_dp, n_sp = mesh.shape["dp"], mesh.shape["sp"]
    count = n_dp * n_sp
    if n_sp != 4 or n_dp & (n_dp - 1) or n_dp < 2:
        raise ValueError
    bits = count.bit_length() - 1

    def swap(array, move):
        return lax.ppermute(array, AXES, [(k, move(k)) for k in range(count)])

    def sibling(array):
        return swap(array, lambda k: k ^ 1)

    tail = list(range(3, bits))
    orders = ([1, 2] + tail, [2, 1] + tail)

    def pieces_for(used):
        return orders, count, pl.cdiv(pl.cdiv(used, count), 16) * 16

    class Chain:
        def __init__(self):
            self.token = None

        def after(self, *arrays):
            if self.token is None:
                return arrays
            return lax.optimization_barrier(arrays + (self.token,))[:-1]

    class Sum:
        def __init__(self, chain, scalars, pieces, heights, gains):
            self.chain, self.scalars, self.pieces = chain, scalars, pieces
            self.heights, self.gains = heights, gains
            self.stage, self.result = 0, None

        def move(self, stage):
            return lambda k: k ^ (1 << orders[k & 1][stage])

        def launch(self):
            (grads,) = self.chain.after(self.grads)
            half = grads.shape[0] // 2
            sent = grads[half:]
            self.keep, self.wire = grads[:half], sibling(sent)
            self.chain.token = sent

        def step(self):
            last = bits - 1
            if self.stage > 2 * last:
                return
            keep, wire = self.chain.after(self.keep, self.wire)
            if self.stage < last:
                half = keep.shape[0] // 2
                sent = (keep[half:].astype(F32) + wire[half:].astype(F32)).astype(BF)
                self.keep = (keep[:half].astype(F32) + wire[:half].astype(F32)).astype(BF)
                self.wire = swap(sent, self.move(self.stage))
            else:
                if self.stage == last:
                    sent = (keep.astype(F32) + wire.astype(F32)).astype(BF)
                else:
                    sent = jnp.concatenate([keep, wire], axis=0)
                back = 2 * last - 1 - self.stage
                self.keep = sent
                self.wire = sibling(sent) if back < 0 else swap(sent, self.move(back))
            self.chain.token = sent
            self.stage += 1

        def unpack(self):
            if self.result is None and self.stage == 2 * bits - 1:
                ready = self.chain.after(self.keep, self.wire)
                self.result = unpack(*ready, self.scalars, self.pieces, self.heights, self.gains)
                self.chain.token = self.result[-1]

    def body(tokens, lengths, *rest):
        out_grad = rest[-1]
        post_query, post_key, post_value, post_out, post_gate, post_up, post_down = rest[0:7]
        pre_query, pre_key, pre_value, pre_out, pre_gate, pre_up, pre_down = rest[9:16]
        gains = [rest[k].reshape(1, D) for k in (7, 8, 16, 17)]
        post_attn_gain, post_ffn_gain, pre_attn_gain, pre_ffn_gain = gains
        sp = lax.axis_index("sp")
        me = lax.axis_index("dp") * n_sp + sp
        chip = sp >> 1
        scalars = jnp.stack([me, sp, lengths[chip]]).astype(jnp.int32)

        def to_slot(array):
            mine = lax.dynamic_index_in_dim(array, chip, 0, keepdims=False)
            other = lax.dynamic_index_in_dim(array, 1 - chip, 0, keepdims=False)
            return mine, swap(other, lambda k: k ^ 3)

        cosine, sine = rope_tables()
        tables = dict(cosine=cosine, sine=sine)

        own_one = jnp.concatenate(to_slot(tokens), axis=0)
        sib_one = sibling(own_one)
        cotangent = dict(zip(("cot_mine", "cot_other"), to_slot(out_grad)))

        rows_bf, rows_f32, full_bf = ((ROWS, D), BF), ((ROWS, D), F32), ((SEQ, D), BF)
        wide_bf, wide_f32 = ((ROWS, FF), BF), ((ROWS, FF), F32)
        gain_f32, head_f32 = ((1, D), F32), ((HEADS, ROWS), F32)
        half_bf, half_f32 = ((SEQ, HALF), BF), ((SEQ, HALF), F32)
        half_rows_bf, half_rows_f32 = ((ROWS, HALF), BF), ((ROWS, HALF), F32)
        saved = dict(q=rows_bf, k=full_bf, v=full_bf, lse=((ROWS, LANES), F32), mixed=rows_bf)
        wide = dict(gate=wide_f32, up=wide_f32, hidden=wide_bf)
        wide_back = dict(dgate=wide_bf, dup=wide_bf)
        post_wide = dict(w_gate=post_gate.T, w_up=post_up.T, w_down=post_down)
        pre_wide = dict(w_gate=pre_gate.T, w_up=pre_up.T, w_down=pre_down)
        post_qkv = dict(w_key=post_key, w_value=post_value, w_query=post_query)
        pre_qkv = dict(w_key=pre_key, w_value=pre_value, w_query=pre_query)
        heads_outs = dict(dqp=half_rows_bf, dkp=half_bf, dvp=half_bf, ge_own=rows_f32)
        heads_tmp = dict(dq=half_rows_f32, dk=half_f32, dv=half_f32)
        start_outs = dict(gmix=rows_bf, delta_t=head_f32, lse_t=head_f32)

        chain = Chain()
        ffn_pieces, attn_pieces = pieces_for(FFN_ROWS + GAIN_ROWS), pieces_for(ATTN_ROWS)
        ffn_grads = dict(grads=((count * ffn_pieces[2], LANES), BF))
        attn_grads = dict(grads=((count * attn_pieces[2], LANES), BF))
        ffn2 = Sum(chain, scalars, ffn_pieces, [FF] * 3, 0)
        ffn1 = Sum(chain, scalars, ffn_pieces, [FF] * 3, 4)
        attn2 = Sum(chain, scalars, attn_pieces, [D] * 4, 0)
        attn1 = Sum(chain, scalars, attn_pieces, [D] * 4, 0)

        def run(body, fetched, ins, outs, stored, scratch, token=0, pieces=None):
            def bound(refs, scalars_ref):
                refs.pieces, refs.me = pieces, scalars_ref[0]
                body(refs, scalars_ref)

            bound.__name__ = body.__name__
            made = run_kernel(
                bound, *chain.after(scalars), fetched, ins, outs, stored, scratch, MFLOPS[body]
            )
            chain.token = made[token]
            return made

        class Home:
            def start(self, array):
                self.mine, (other,) = array[:BLK], chain.after(array[BLK:])
                self.wire = swap(other, lambda k: k ^ 3)
                chain.token = other

            def finish(self):
                mine, other = chain.after(self.mine, self.wire)
                ways = jnp.stack([mine, other]), jnp.stack([other, mine])
                self.result = jnp.where(chip == 0, *ways)
                chain.token = self.result

        home_output, home_grad = Home(), Home()

        entry2, q1, k1, v1, lse1, mixed1, middle1, result1 = run(
            post_forward,
            dict(**post_qkv, **tables, w_out=post_out, attn_gain=post_attn_gain, **post_wide)
            | dict(ffn_gain=post_ffn_gain, next_gain=pre_attn_gain),
            dict(own=own_one, sib=sib_one),
            dict(entry=rows_bf),
            saved | dict(middle=rows_f32, result=rows_f32),
            wide,
        )
        sib_two = sibling(entry2)
        mixed2, q2, k2, v2, lse2, kept2 = run(
            attention_forward,
            dict(**pre_qkv, **tables),
            dict(own=entry2, sib=sib_two),
            dict(mixed=saved.pop("mixed")),
            saved | {KEPT: rows_bf},
            {},
        )
        out_rows, grad_gain, grad_middle2, *start2, grads = run(
            pre_ffn,
            dict(w_out=pre_out, result=result1, last_gain=post_ffn_gain, ffn_gain=pre_ffn_gain)
            | dict(**pre_wide, lse=lse2),
            dict(mixed=mixed2, **cotangent),
            dict(output=rows_bf, grad_gain=gain_f32, grad_middle=rows_f32, **start_outs) | ffn_grads,
            {},
            wide | wide_back,
            1,
            ffn_pieces,
        )
        ffn2.grads = grads

        held = {}

        def heads(ready, arrays, weights, first):
            start = 0 if first is None else HALF
            fetched = dict(zip(("q", "k", "v"), arrays)) | weights
            fetched = {name: Columns(array, start) for name, array in fetched.items()} | tables
            ins = dict(zip(("gmix", "delta_t", "lse_t"), ready))
            if first is None:
                outs = heads_outs | dict(ge_sib=rows_f32)
                return run(first_heads_backward, fetched, ins, outs, {}, heads_tmp, token=2)
            ins |= dict(part_own=first[3], part_sib=first[4])
            outs = heads_outs | dict(ge_sib=rows_bf)
            return run(last_heads_backward, fetched, ins, outs, {}, heads_tmp, token=4)

        def pre_heads_a():
            held[1] = heads(start2, (q2, k2, v2), pre_qkv, None)

        def pre_heads_b():
            held[2] = heads(start2, (q2, k2, v2), pre_qkv, held[1])
            held[3] = sibling(held[2][4])

        def ffn_again():
            held[4] = run(
                post_ffn_again,
                dict(middle=middle1, attn_gain=post_attn_gain)
                | dict(w_gate=post_wide["w_gate"], w_up=post_wide["w_up"]),
                {},
                dict(ffn_in=rows_bf) | wide,
                {},
                {},
            )

        def ffn_back():
            ins = dict(zip(("ffn_in", "gate", "up", "hidden"), held[4]))
            *rest, grads = run(
                post_ffn_backward,
                dict(middle=middle1, result=result1, ffn_gain=post_ffn_gain)
                | dict(next_gain=pre_attn_gain, attn_gain=post_attn_gain)
                | dict(**post_wide, w_out=post_out, mixed=mixed1, lse=lse1),
                ins
                | dict(grad_middle=grad_middle2, grad_gain=grad_gain)
                | dict(ge_own=held[2][3], ge_recv=held[3]),
                dict(new_middle=rows_f32) | start_outs | ffn_grads,
                {},
                wide_back,
                2,
                ffn_pieces,
            )
            held[5] = rest
            ffn1.grads = grads

        def weight_grads(total, fetched, grad_middle, own, sib, first, last):
            (grads,) = run(
                attention_weight_grads,
                fetched,
                dict(grad_middle=grad_middle, own=own, sib=sib)
                | dict(zip(("dqa", "dka", "dva"), first))
                | dict(zip(("dqb", "dkb", "dvb"), last)),
                attn_grads,
                {},
                {},
                0,
                attn_pieces,
            )
            total.grads = grads

        def pre_weights():
            weight_grads(attn2, dict(mixed=kept2), grad_middle2, entry2, sib_two, held[1], held[2])

        def post_heads_a():
            held[6] = heads(held[5][1:], (q1, k1, v1), post_qkv, None)

        def post_heads_b():
            held[7] = heads(held[5][1:], (q1, k1, v1), post_qkv, held[6])

        def send_entry():
            (sent,) = chain.after(held[7][4])
            held[8] = sibling(sent)

        def post_weights():
            saved_mix = dict(mixed=mixed1)
            weight_grads(attn1, saved_mix, held[5][0], own_one, sib_one, held[6], held[7])

        def send_output():
            home_output.start(out_rows)

        def send_grad():
            (received,) = chain.after(held[8])
            total = held[5][0] + held[7][3] + received.astype(F32)
            home_grad.start(total.astype(BF))


        plan = (
            ffn2.launch,
            send_output,
            ffn_again,
            ffn2,
            pre_heads_a,
            home_output.finish,
            pre_heads_b,
            ffn2,
            ffn_back,
            ffn1.launch,
            ffn2,
            pre_weights,
            attn2.launch,
            ffn1,
            ffn2,
            post_heads_a,
            attn2,
            ffn2,
            ffn1,
            post_heads_b,
            ffn2,
            send_entry,
            ffn1,
            attn2,
            post_weights,
            ffn2,
            attn1.launch,
            attn2,
            attn1,
            ffn1,
            attn2,
            send_grad,
            ffn1,
            attn1,
            attn2,
            ffn2,
            ffn1,
            attn1,
            home_grad.finish,
            attn2,
            ffn1,
            ffn2,
            attn1,
            attn2,
            ffn1,
            attn1,
            attn1,
            attn1,
            ffn1,
            attn2,
            ffn2.unpack,
            attn1,
            attn2,
            ffn1.unpack,
            attn1,
            attn2.unpack,
            attn1.unpack,
        )
        for action in plan:
            if isinstance(action, Sum):
                action.step()
            else:
                action()
        sums = (ffn2, ffn1, attn2, attn1)
        for again in range(2 * bits):
            for total in sums:
                total.step()
        for total in sums:
            total.unpack()
        down2, gate2, up2 = ffn2.result
        down1, gate1, up1, *gains = ffn1.result
        gain_pre_ffn, gain_pre_attn, gain_post_ffn, gain_post_attn = (g.reshape(D) for g in gains)
        out2, query2, key2, value2 = attn2.result
        out1, query1, key1, value1 = attn1.result
        post_grads = (query1, key1, value1, out1, gate1.T, up1.T, down1, gain_post_attn, gain_post_ffn)
        pre_grads = (query2, key2, value2, out2, gate2.T, up2.T, down2, gain_pre_attn, gain_pre_ffn)
        return (home_output.result, home_grad.result) + post_grads + pre_grads

    spread = P("dp", "sp", None)
    in_specs = (spread, P("dp")) + (P(),) * 18 + (spread,)
    out_specs = (spread, spread) + (P(),) * 18
    return jax.shard_map(body, mesh=mesh, in_specs=in_specs, out_specs=out_specs, check_vma=False)
```

```python
import jax
import jax.numpy as jnp
import numpy as np
from jax import lax
from jax.experimental import pallas as pl
from jax.experimental.pallas import tpu as pltpu
from jax.sharding import PartitionSpec as P

D = 512
HEADS = 8
HD = 64
FF = 1376
SEQ = 1024
EPS = 1e-06
NEG = -1000000000.0
AXES = ("dp", "sp")
BF = jnp.bfloat16
F32 = jnp.float32
LANES = 128
PANELS = D // LANES
BLK = SEQ // 4
ROWS = 2 * BLK
HALF = D // 2
SCALE = HD ** (-0.5)
FFN_ROWS = 3 * PANELS * FF
ATTN_ROWS = 4 * PANELS * D
GAIN_ROWS = 16
KEPT = "kept"
VMEM_LIMIT = 28 << 20


def dot(left, right):
    return lax.dot_general(left, right, (((1,), (0,)), ((), ())), preferred_element_type=F32)


def dot_nt(left, right):
    return lax.dot_general(left, right, (((1,), (1,)), ((), ())), preferred_element_type=F32)


def dot_tn(left, right):
    return lax.dot_general(left, right, (((0,), (0,)), ((), ())), preferred_element_type=F32)


def inv_rms(values):
    return lax.rsqrt(jnp.mean(values * values, axis=-1, keepdims=True) + EPS)


def rms_back(values, gain, upstream):
    scale = inv_rms(values)
    weighted = upstream * gain
    grad = scale * weighted - values * (
        scale * scale * scale * jnp.mean(weighted * values, axis=-1, keepdims=True)
    )
    grad_gain = jnp.sum(upstream * (values * scale), axis=0, keepdims=True)
    return grad, grad_gain


class Refs:
    def __init__(self, vmem, fetched, stored, sems):
        self.vmem, self.stored, self.sems = vmem, stored, sems
        self.waiting, self.sent = {}, []
        for name in fetched:
            copy = pltpu.make_async_copy(fetched[name], vmem[name], self.next_sem())
            copy.start()
            self.waiting[name] = copy

    used = 0

    def next_sem(self):
        self.used += 1
        return self.sems.at[self.used - 1]

    def __getattr__(self, name):
        if name in self.waiting:
            self.waiting.pop(name).wait()
        return self.vmem[name]

    def send(self, *refs):
        for ref in refs:
            for name in self.stored:
                if self.vmem[name] is ref:
                    self.send_as(name, ref)

    def send_as(self, name, ref):
        if name in self.stored:
            copy = pltpu.make_async_copy(ref, self.stored[name], self.next_sem())
            copy.start()
            self.sent.append(copy)

    def finish(self):
        for name in list(self.waiting):
            self.waiting.pop(name).wait()
        for copy in self.sent:
            copy.wait()


class Columns:
    def __init__(self, array, start):
        self.array, self.start = array, start


def in_hbm(array):
    if isinstance(array, Columns):
        array = array.array
    return pltpu.with_memory_space_constraint(array, pltpu.HBM)


def run_kernel(body, scalars, fetched, ins, outs, stored, scratch, mflops):
    names = list(ins) + list(outs) + list(fetched) + list(stored) + list(scratch)
    n_f, n_in, n_out, n_st = len(fetched), len(ins), len(outs), len(stored)
    shapes = []
    for array in fetched.values():
        if isinstance(array, Columns):
            shapes.append(pltpu.VMEM((array.array.shape[0], HALF), array.array.dtype))
        else:
            shapes.append(pltpu.VMEM(array.shape, array.dtype))
    shapes += [pltpu.VMEM((8, LANES) if n == KEPT else stored[n][0], stored[n][1]) for n in stored]
    shapes += [pltpu.VMEM(*scratch[n]) for n in scratch]

    def kernel(scalars_ref, *args):
        head = n_f + n_in + n_out
        hbm_in, on_chip, hbm_out = list(args[:n_f]), args[n_f:head], args[head : head + n_st]
        for k, array in enumerate(fetched.values()):
            if isinstance(array, Columns):
                hbm_in[k] = hbm_in[k].at[:, pl.ds(array.start, HALF)]
        vmem = dict(zip(names, on_chip + args[head + n_st : -1]))
        refs = Refs(vmem, dict(zip(fetched, hbm_in)), dict(zip(stored, hbm_out)), args[-1])
        body(refs, scalars_ref)
        refs.finish()

    on_chip, off_chip = (pl.BlockSpec(memory_space=m) for m in (pltpu.VMEM, pltpu.HBM))
    made = pl.pallas_call(
        kernel,
        name=body.__name__,
        out_shape=[jax.ShapeDtypeStruct(*outs[n]) for n in outs]
        + [pltpu.HBM(*stored[n]) for n in stored],
        grid_spec=pltpu.PrefetchScalarGridSpec(
            num_scalar_prefetch=1,
            grid=(),
            in_specs=[off_chip] * n_f + [on_chip] * n_in,
            out_specs=[on_chip] * n_out + [off_chip] * n_st,
            scratch_shapes=shapes + [pltpu.SemaphoreType.DMA((max(n_f + n_st, 1),))],
        ),
        compiler_params=pltpu.CompilerParams(vmem_limit_bytes=VMEM_LIMIT),
        cost_estimate=pl.CostEstimate(flops=mflops * 10**6, transcendentals=0, bytes_accessed=1),
    )(scalars, *[in_hbm(a) for a in fetched.values()], *ins.values())
    return made


def piece_position(j, me, order):
    where = 0
    for bit in order:
        where = where * 2 + (((me >> bit) & 1) ^ ((j >> bit) & 1))
    return where


def segments(pieces, start, end):
    rows = pieces[2]
    while start < end:
        stop = min(end, (start // rows + 1) * rows)
        yield start // rows, start % rows, start, stop - start
        start = stop


def put_rows(refs, pieces, start, block):
    orders, count, rows = pieces
    me = refs.me
    for j, inside, at, length in segments(pieces, start, start + block.shape[0]):
        spot = piece_position(j, me, orders[j & 1]) + ((me ^ j) & 1) * (count // 2)
        put = pl.ds(pl.multiple_of(spot * rows + inside, 16), length)
        refs.grads[put, :] = block[at - start : at - start + length, :]


def head_lanes(rows, which):
    lane = lax.broadcasted_iota(jnp.int32, (rows, LANES), 1)
    return (lane < HD) if which == 0 else (lane >= HD)


def only_head(panel, which):
    return jnp.where(head_lanes(panel.shape[0], which), panel, jnp.zeros_like(panel))


def turned(panel):
    lane = lax.broadcasted_iota(jnp.int32, panel.shape, 1)
    return jnp.where(
        lane % HD < HD // 2,
        pltpu.roll(panel, LANES - HD // 2, 1),
        pltpu.roll(panel, HD // 2, 1),
    )


def block_rows(index):
    return pl.ds(pl.multiple_of(index * BLK, BLK), BLK)


def rope_tables():
    lane = np.arange(LANES)
    inverse = np.float32(10000.0) ** (-np.arange(HD // 2, dtype=np.float32) * np.float32(2.0 / HD))
    places = np.concatenate([np.arange(BLK), np.arange(8) * BLK]).astype(np.float32)
    angles = (places[:, None] * inverse[None, :])[:, lane % (HD // 2)].astype(np.float64)
    sign = np.where(lane % HD < HD // 2, -1.0, 1.0)
    return np.cos(angles).astype(np.float32), (np.sin(angles) * sign).astype(np.float32)


def rope_of(refs, block):
    cosine, sine = refs.cosine[0:BLK, :], refs.sine[0:BLK, :]
    start = pl.ds(BLK + block, 1)
    start_cos, start_sin = refs.cosine[start, :], refs.sine[start, :]
    return cosine * start_cos - sine * start_sin, sine * start_cos + cosine * start_sin


def panel_cols(panel):
    return slice(panel * LANES, (panel + 1) * LANES)


def blocks_of(sp):
    return sp, 3 - sp


def project_heads(refs, sp, entry, own):
    for half, block in enumerate(blocks_of(sp)):
        here = slice(half * BLK, (half + 1) * BLK)
        there = block_rows(block)
        rows = entry[here, :]
        keys = dot(rows, refs.w_key[...])
        refs.v[there, :] = dot(rows, refs.w_value[...]).astype(BF)
        if own:
            queries = dot(rows, refs.w_query[...])
        cosine, sine = rope_of(refs, block)
        for panel in range(PANELS):
            cols = panel_cols(panel)
            part = keys[:, cols]
            refs.k[there, cols] = (part * cosine + turned(part) * sine).astype(BF)
            if own:
                part = queries[:, cols]
                refs.q[here, cols] = (part * cosine + turned(part) * sine).astype(BF) * SCALE


def query_blocks(sp, low):
    chip = sp >> 1
    return (block_rows(chip), low + 1), (block_rows(1 - chip), 4 - low)


def both_ways(sp, step):
    low = (sp & 1) ^ (sp >> 1)

    @pl.when(low == 0)
    def outer():
        step(0)

    @pl.when(low == 1)
    def inner():
        step(1)


def attend(refs, scalars, low):
    sp, length = scalars[1], scalars[2]
    lane = lax.broadcasted_iota(jnp.int32, (BLK, LANES), 1)
    most = (4 - low) * BLK
    past = jnp.where(lax.broadcasted_iota(jnp.int32, (1, most), 1) < length, 0.0, NEG)
    causal = lax.broadcasted_iota(jnp.int32, (BLK, BLK), 1) <= lax.broadcasted_iota(
        jnp.int32, (BLK, BLK), 0
    )

    def panel_step(panel, carry):
        cols = pl.ds(pl.multiple_of(panel * LANES, LANES), LANES)
        jobs = []
        for rows, blocks in query_blocks(sp, low):
            queries = refs.q[rows, cols]
            for which in range(2):
                seen = blocks * BLK
                scores = dot_nt(only_head(queries, which), refs.k[0:seen, cols])
                jobs.append((rows, blocks, which, scores))
        done = {}
        for rows, blocks, which, scores in jobs:
            before = (blocks - 1) * BLK
            last = jnp.where(causal, scores[:, before:] + past[:, before : before + BLK], NEG)
            if before:
                scores = jnp.concatenate([scores[:, :before] + past[:, :before], last], axis=1)
            else:
                scores = last
            top = jnp.max(scores, axis=-1, keepdims=True)
            weights = jnp.exp(scores - top)
            total = jnp.sum(weights, axis=-1, keepdims=True)
            mixed = dot(weights.astype(BF), refs.v[0 : blocks * BLK, cols]) / total
            done[blocks, which] = mixed, top + jnp.log(total)
        for rows, blocks in query_blocks(sp, low):
            (one, log_one), (two, log_two) = done[blocks, 0], done[blocks, 1]
            refs.mixed[rows, cols] = jnp.where(head_lanes(BLK, 0), one, two).astype(BF)
            kept = jnp.where(lane == 2 * panel, log_one, refs.lse[rows, :])
            refs.lse[rows, :] = jnp.where(lane == 2 * panel + 1, log_two, kept)
        return carry

    lax.fori_loop(0, PANELS, panel_step, 0)


def attention_forward(refs, scalars):
    sp = scalars[1]
    project_heads(refs, sp, refs.own, True)
    project_heads(refs, sp ^ 1, refs.sib, False)
    refs.send(refs.q, refs.k, refs.v)
    refs.lse[...] = jnp.zeros((ROWS, LANES), F32)
    both_ways(sp, lambda low: attend(refs, scalars, low))
    refs.send(refs.lse, refs.mixed)
    refs.send_as(KEPT, refs.mixed)


def ffn_forward(refs, ffn_in):
    for half in range(2):
        rows = slice(half * BLK, (half + 1) * BLK)
        gate = dot_nt(ffn_in[rows, :], refs.w_gate[...])
        up = dot_nt(ffn_in[rows, :], refs.w_up[...])
        refs.gate[rows, :] = gate
        refs.up[rows, :] = up
        refs.hidden[rows, :] = (gate * jax.nn.sigmoid(gate) * up).astype(BF)


def store_panels(refs, at, grad):
    height, width = grad.shape
    for panel in range(width // LANES):
        block = grad[:, panel_cols(panel)].astype(BF)
        put_rows(refs, refs.pieces, at + panel * height, block)


def ffn_weight_grads(refs, at, ffn_in, grad_result):
    grad_down = grad_result.astype(BF)
    store_panels(refs, at, dot_tn(refs.hidden[...], grad_down))
    for half in range(2):
        rows = slice(half * BLK, (half + 1) * BLK)
        grad_hidden = dot_nt(grad_down[rows, :], refs.w_down[...])
        gate = refs.gate[rows, :]
        sigma = jax.nn.sigmoid(gate)
        grad_gate = grad_hidden * refs.up[rows, :] * (sigma * (1.0 + gate * (1.0 - sigma)))
        refs.dgate[rows, :] = grad_gate.astype(BF)
        refs.dup[rows, :] = (grad_hidden * (gate * sigma)).astype(BF)
    store_panels(refs, at + PANELS * FF, dot_tn(refs.dgate[...], ffn_in))
    store_panels(refs, at + 2 * PANELS * FF, dot_tn(refs.dup[...], ffn_in))


def ffn_input_grad(refs):
    return dot(refs.dgate[...], refs.w_gate[...]) + dot(refs.dup[...], refs.w_up[...])


def store_tail(refs, gains):
    end = refs.grads.shape[0]
    row = lax.broadcasted_iota(jnp.int32, (end - FFN_ROWS, LANES), 0)
    block = jnp.zeros((end - FFN_ROWS, LANES), F32)
    for slot, gain in enumerate(gains):
        for panel in range(PANELS):
            block = jnp.where(row == PANELS * slot + panel, gain[:, panel_cols(panel)], block)
    put_rows(refs, refs.pieces, FFN_ROWS, block.astype(BF))


def post_forward(refs, scalars):
    attention_forward(refs, scalars)
    middle = refs.own[...].astype(F32) + dot(refs.mixed[...], refs.w_out[...])
    refs.middle[...] = middle
    refs.send(refs.middle)
    state = middle * inv_rms(middle) * refs.attn_gain[...]
    ffn_forward(refs, state.astype(BF))
    result = state + dot(refs.hidden[...], refs.w_down[...])
    refs.result[...] = result
    refs.send(refs.result)
    output = result * inv_rms(result) * refs.ffn_gain[...]
    entry = output * inv_rms(output) * refs.next_gain[...]
    refs.entry[...] = entry.astype(BF)


def masked_cotangent(refs, scalars):
    sp, length = scalars[1], scalars[2]
    row = lax.broadcasted_iota(jnp.int32, (BLK, D), 0)
    parts = []
    for block, ref in zip(blocks_of(sp), (refs.cot_mine, refs.cot_other)):
        parts.append(jnp.where(row + block * BLK < length, ref[...].astype(F32), 0.0))
    return jnp.concatenate(parts, axis=0)


def attend_back(refs, scalars, low, first_panel):
    sp, length = scalars[1], scalars[2]
    if low == 1:
        refs.dk[3 * BLK :, :] = jnp.zeros((BLK, HALF), F32)
        refs.dv[3 * BLK :, :] = jnp.zeros((BLK, HALF), F32)

    def panel_step(panel, carry):
        cols = pl.ds(pl.multiple_of((first_panel + panel) * LANES, LANES), LANES)
        put = pl.ds(pl.multiple_of(panel * LANES, LANES), LANES)
        for rows, blocks in reversed(query_blocks(sp, low)):
            seen = blocks * BLK
            queries = refs.q[rows, put]
            grads = refs.gmix[rows, cols]
            keys = refs.k[0:seen, put]
            values = refs.v[0:seen, put]
            key_at = lax.broadcasted_iota(jnp.int32, (seen, BLK), 0)
            row_at = lax.broadcasted_iota(jnp.int32, (seen, BLK), 1) + (blocks - 1) * BLK
            allowed = (key_at <= row_at) & (key_at < length)
            grad_q = jnp.zeros((LANES, BLK), F32)
            grad_k = jnp.zeros((seen, LANES), F32)
            grad_v = jnp.zeros((seen, LANES), F32)
            jobs = []
            for which in range(2):
                q_head = only_head(queries, which)
                g_head = only_head(grads, which)
                jobs.append((q_head, g_head, dot_nt(keys, q_head), dot_nt(values, g_head)))
            for which, (q_head, g_head, scores, grad_p) in enumerate(jobs):
                at = pl.ds(2 * (first_panel + panel) + which, 1)
                probs = jnp.exp(jnp.where(allowed, scores, NEG) - refs.lse_t[at, rows])
                grad_s = (probs * (grad_p - refs.delta_t[at, rows])).astype(BF)
                grad_v = grad_v + dot(probs.astype(BF), g_head)
                grad_k = grad_k + dot(grad_s, q_head)
                grad_q = grad_q + dot_tn(only_head(keys, which), grad_s)
            refs.dq[rows, put] = jnp.transpose(grad_q) * SCALE
            if blocks == 4 - low:
                refs.dk[0:seen, put] = grad_k
                refs.dv[0:seen, put] = grad_v
            else:
                refs.dk[0:seen, put] += grad_k
                refs.dv[0:seen, put] += grad_v
        return carry

    lax.fori_loop(0, PANELS // 2, panel_step, 0)


def start_attention_backward(refs, grad_middle):
    grad_mixed = dot_nt(grad_middle.astype(BF), refs.w_out[...]).astype(BF)
    refs.gmix[...] = grad_mixed
    product = grad_mixed.astype(F32) * refs.mixed[...].astype(F32)
    high = product.astype(BF)
    rest = (product - high.astype(F32)).astype(BF)
    head_of = lax.broadcasted_iota(jnp.int32, (HEADS, D), 1) // HD
    pick = (head_of == lax.broadcasted_iota(jnp.int32, (HEADS, D), 0)).astype(F32).astype(BF)
    refs.delta_t[...] = dot_nt(pick, high) + dot_nt(pick, rest)
    refs.lse_t[...] = jnp.transpose(refs.lse[...])[0:HEADS, :]


def attention_backward(refs, scalars, first_panel):
    sp = scalars[1]
    refs.q, refs.k, refs.v
    both_ways(sp, lambda low: attend_back(refs, scalars, low, first_panel))

    for spot, block in enumerate(blocks_of(sp) + blocks_of(sp ^ 1)):
        put, there = slice(spot * BLK, (spot + 1) * BLK), block_rows(block)
        refs.dvp[put, :] = refs.dv[there, :].astype(BF)
        cosine, sine = rope_of(refs, block)
        for panel in range(PANELS // 2):
            cols = panel_cols(panel)
            part = refs.dk[there, cols]
            refs.dkp[put, cols] = (part * cosine - turned(part) * sine).astype(BF)
            if spot < 2:
                part = refs.dq[put, cols]
                refs.dqp[put, cols] = (part * cosine - turned(part) * sine).astype(BF)
    w_query, w_key, w_value = refs.w_query[...], refs.w_key[...], refs.w_value[...]
    mine, theirs = slice(0, ROWS), slice(ROWS, 2 * ROWS)
    ge_sib = dot_nt(refs.dkp[theirs, :], w_key) + dot_nt(refs.dvp[theirs, :], w_value)
    ge_own = (
        dot_nt(refs.dqp[...], w_query)
        + dot_nt(refs.dkp[mine, :], w_key)
        + dot_nt(refs.dvp[mine, :], w_value)
    )
    return ge_own, ge_sib


def first_heads_backward(refs, scalars):
    refs.ge_own[...], refs.ge_sib[...] = attention_backward(refs, scalars, 0)


def last_heads_backward(refs, scalars):
    ge_own, ge_sib = attention_backward(refs, scalars, PANELS // 2)
    refs.ge_own[...] = refs.part_own[...] + ge_own
    refs.ge_sib[...] = (refs.part_sib[...] + ge_sib).astype(BF)


def pre_ffn(refs, scalars):
    store_tail(refs, ())
    result = refs.result[...]
    inputs = result * inv_rms(result) * refs.last_gain[...]
    middle = inputs + dot(refs.mixed[...], refs.w_out[...])
    gain = refs.ffn_gain[...]
    ffn_in = (middle * inv_rms(middle) * gain).astype(BF)
    ffn_forward(refs, ffn_in)
    output = middle + dot(refs.hidden[...], refs.w_down[...])
    refs.output[...] = output.astype(BF)
    cotangent = masked_cotangent(refs, scalars)
    ffn_weight_grads(refs, 0, ffn_in, cotangent)
    grad_normed, grad_gain = rms_back(middle, gain, ffn_input_grad(refs))
    grad_middle = cotangent + grad_normed
    refs.grad_middle[...] = grad_middle
    refs.grad_gain[...] = grad_gain
    start_attention_backward(refs, grad_middle)


def attention_weight_grads(refs, scalars):
    step = PANELS * D
    store_panels(refs, 0, dot_tn(refs.mixed[...], refs.grad_middle[...].astype(BF)))
    own, sib = refs.own[...], refs.sib[...]
    for half in range(2):
        put = half * step // 2
        dqp, dkp, dvp = ((refs.dqa, refs.dka, refs.dva), (refs.dqb, refs.dkb, refs.dvb))[half]
        store_panels(refs, step + put, dot_tn(own, dqp[...]))
        for k, ref in enumerate((dkp, dvp)):
            total = dot_tn(own, ref[0:ROWS, :]) + dot_tn(sib, ref[ROWS : 2 * ROWS, :])
            store_panels(refs, (k + 2) * step + put, total)


def post_ffn_again(refs, scalars):
    middle = refs.middle[...]
    ffn_in = (middle * inv_rms(middle) * refs.attn_gain[...]).astype(BF)
    refs.ffn_in[...] = ffn_in
    ffn_forward(refs, ffn_in)


def post_ffn_backward(refs, scalars):
    middle, result = refs.middle[...], refs.result[...]
    out_gain = refs.ffn_gain[...]
    inputs = result * inv_rms(result) * out_gain
    grad_entry = refs.ge_own[...] + refs.ge_recv[...].astype(F32)
    grad_normed, grad_next = rms_back(inputs, refs.next_gain[...], grad_entry)
    grad_result, grad_ffn_gain = rms_back(result, out_gain, refs.grad_middle[...] + grad_normed)
    ffn_weight_grads(refs, 0, refs.ffn_in[...], grad_result)
    upstream = grad_result + ffn_input_grad(refs)
    grad_middle, grad_attn_gain = rms_back(middle, refs.attn_gain[...], upstream)
    refs.new_middle[...] = grad_middle
    store_tail(refs, (refs.grad_gain[...], grad_next, grad_ffn_gain, grad_attn_gain))
    start_attention_backward(refs, grad_middle)


MFLOPS = {
    post_forward: 120000,
    attention_forward: 90000,
    pre_ffn: 105000,
    first_heads_backward: 67500,
    last_heads_backward: 67500,
    post_ffn_again: 37500,
    post_ffn_backward: 82500,
    attention_weight_grads: 22500,
}


def unpack(mine, other, scalars, pieces, heights, gains):
    orders, count, rows = pieces
    shapes = [(height, D) for height in heights] + [(PANELS, LANES)] * gains
    n_out = len(shapes)

    def unpack(scalars_ref, mine_ref, other_ref, *rest):
        outs, staged, sems = rest[:n_out], rest[n_out : 2 * n_out], rest[-1]
        me = scalars_ref[0]

        def lay_out(halves):
            sent, at = [], 0
            for k in range(n_out):
                height, width = shapes[k]
                if k < len(heights):
                    for panel in range(PANELS):
                        for j, inside, row, length in segments(pieces, at, at + height):
                            spot = piece_position(j, me, orders[j & 1]) * rows + inside
                            take = pl.ds(pl.multiple_of(spot, 16), length)
                            put = slice(row - at, row - at + length)
                            staged[k][put, panel_cols(panel)] = halves[j & 1][take, :].astype(F32)
                        at += height
                else:
                    if k == len(heights):
                        ((j, inside, row, length),) = segments(pieces, at, at + GAIN_ROWS)
                        spot = piece_position(j, me, orders[j & 1]) * rows + inside
                        take = pl.ds(pl.multiple_of(spot, 16), GAIN_ROWS)
                        block = halves[j & 1][take, :].astype(F32)
                    slot = (k - len(heights)) * PANELS
                    staged[k][...] = block[slot : slot + PANELS, :]
                sent.append(pltpu.make_async_copy(staged[k], outs[k], sems.at[k]))
                sent[-1].start()
            for copy in sent:
                copy.wait()

        @pl.when(me & 1 == 0)
        def even():
            lay_out((mine_ref, other_ref))

        @pl.when(me & 1 == 1)
        def odd():
            lay_out((other_ref, mine_ref))

    on_chip, off_chip = (pl.BlockSpec(memory_space=m) for m in (pltpu.VMEM, pltpu.HBM))
    return pl.pallas_call(
        unpack,
        name=unpack.__name__,
        out_shape=[jax.ShapeDtypeStruct(shape, F32) for shape in shapes],
        grid_spec=pltpu.PrefetchScalarGridSpec(
            num_scalar_prefetch=1,
            grid=(),
            in_specs=[on_chip] * 2,
            out_specs=[off_chip] * n_out,
            scratch_shapes=[pltpu.VMEM(shape, F32) for shape in shapes]
            + [pltpu.SemaphoreType.DMA((n_out,))],
        ),
        compiler_params=pltpu.CompilerParams(vmem_limit_bytes=VMEM_LIMIT),
        cost_estimate=pl.CostEstimate(
            flops=0, transcendentals=0, bytes_accessed=6 * mine.shape[0] * LANES * 2
        ),
    )(scalars, mine, other)


def solution(mesh):
    n_dp, n_sp = mesh.shape["dp"], mesh.shape["sp"]
    count = n_dp * n_sp
    if n_sp != 4 or n_dp & (n_dp - 1) or n_dp < 2:
        raise ValueError
    bits = count.bit_length() - 1

    def swap(array, move):
        return lax.ppermute(array, AXES, [(k, move(k)) for k in range(count)])

    def sibling(array):
        return swap(array, lambda k: k ^ 1)

    tail = list(range(3, bits))
    orders = ([1, 2] + tail, [2, 1] + tail)

    def pieces_for(used):
        return orders, count, pl.cdiv(pl.cdiv(used, count), 16) * 16

    class Chain:
        def __init__(self):
            self.token = None

        def after(self, *arrays):
            if self.token is None:
                return arrays
            return lax.optimization_barrier(arrays + (self.token,))[:-1]

    class Sum:
        def __init__(self, chain, scalars, pieces, heights, gains):
            self.chain, self.scalars, self.pieces = chain, scalars, pieces
            self.heights, self.gains = heights, gains
            self.stage, self.result = 0, None

        def move(self, stage):
            return lambda k: k ^ (1 << orders[k & 1][stage])

        def launch(self):
            (grads,) = self.chain.after(self.grads)
            half = grads.shape[0] // 2
            sent = grads[half:]
            self.keep, self.wire = grads[:half], sibling(sent)
            self.chain.token = sent

        def step(self):
            last = bits - 1
            if self.stage > 2 * last:
                return
            keep, wire = self.chain.after(self.keep, self.wire)
            if self.stage < last:
                half = keep.shape[0] // 2
                sent = (keep[half:].astype(F32) + wire[half:].astype(F32)).astype(BF)
                self.keep = (keep[:half].astype(F32) + wire[:half].astype(F32)).astype(BF)
                self.wire = swap(sent, self.move(self.stage))
            else:
                if self.stage == last:
                    sent = (keep.astype(F32) + wire.astype(F32)).astype(BF)
                else:
                    sent = jnp.concatenate([keep, wire], axis=0)
                back = 2 * last - 1 - self.stage
                self.keep = sent
                self.wire = sibling(sent) if back < 0 else swap(sent, self.move(back))
            self.chain.token = sent
            self.stage += 1

        def unpack(self):
            if self.result is None and self.stage == 2 * bits - 1:
                ready = self.chain.after(self.keep, self.wire)
                self.result = unpack(*ready, self.scalars, self.pieces, self.heights, self.gains)
                self.chain.token = self.result[-1]

    def body(tokens, lengths, *rest):
        out_grad = rest[-1]
        post_query, post_key, post_value, post_out, post_gate, post_up, post_down = rest[0:7]
        pre_query, pre_key, pre_value, pre_out, pre_gate, pre_up, pre_down = rest[9:16]
        gains = [rest[k].reshape(1, D) for k in (7, 8, 16, 17)]
        post_attn_gain, post_ffn_gain, pre_attn_gain, pre_ffn_gain = gains
        sp = lax.axis_index("sp")
        me = lax.axis_index("dp") * n_sp + sp
        chip = sp >> 1
        scalars = jnp.stack([me, sp, lengths[chip]]).astype(jnp.int32)

        def to_slot(array):
            mine = lax.dynamic_index_in_dim(array, chip, 0, keepdims=False)
            other = lax.dynamic_index_in_dim(array, 1 - chip, 0, keepdims=False)
            return mine, swap(other, lambda k: k ^ 3)

        cosine, sine = rope_tables()
        tables = dict(cosine=cosine, sine=sine)

        own_one = jnp.concatenate(to_slot(tokens), axis=0)
        sib_one = sibling(own_one)
        cotangent = dict(zip(("cot_mine", "cot_other"), to_slot(out_grad)))

        rows_bf, rows_f32, full_bf = ((ROWS, D), BF), ((ROWS, D), F32), ((SEQ, D), BF)
        wide_bf, wide_f32 = ((ROWS, FF), BF), ((ROWS, FF), F32)
        gain_f32, head_f32 = ((1, D), F32), ((HEADS, ROWS), F32)
        half_bf, half_f32 = ((SEQ, HALF), BF), ((SEQ, HALF), F32)
        half_rows_bf, half_rows_f32 = ((ROWS, HALF), BF), ((ROWS, HALF), F32)
        saved = dict(q=rows_bf, k=full_bf, v=full_bf, lse=((ROWS, LANES), F32), mixed=rows_bf)
        wide = dict(gate=wide_f32, up=wide_f32, hidden=wide_bf)
        wide_back = dict(dgate=wide_bf, dup=wide_bf)
        post_wide = dict(w_gate=post_gate.T, w_up=post_up.T, w_down=post_down)
        pre_wide = dict(w_gate=pre_gate.T, w_up=pre_up.T, w_down=pre_down)
        post_qkv = dict(w_key=post_key, w_value=post_value, w_query=post_query)
        pre_qkv = dict(w_key=pre_key, w_value=pre_value, w_query=pre_query)
        heads_outs = dict(dqp=half_rows_bf, dkp=half_bf, dvp=half_bf, ge_own=rows_f32)
        heads_tmp = dict(dq=half_rows_f32, dk=half_f32, dv=half_f32)
        start_outs = dict(gmix=rows_bf, delta_t=head_f32, lse_t=head_f32)

        chain = Chain()
        ffn_pieces, attn_pieces = pieces_for(FFN_ROWS + GAIN_ROWS), pieces_for(ATTN_ROWS)
        ffn_grads = dict(grads=((count * ffn_pieces[2], LANES), BF))
        attn_grads = dict(grads=((count * attn_pieces[2], LANES), BF))
        ffn2 = Sum(chain, scalars, ffn_pieces, [FF] * 3, 0)
        ffn1 = Sum(chain, scalars, ffn_pieces, [FF] * 3, 4)
        attn2 = Sum(chain, scalars, attn_pieces, [D] * 4, 0)
        attn1 = Sum(chain, scalars, attn_pieces, [D] * 4, 0)

        def run(body, fetched, ins, outs, stored, scratch, token=0, pieces=None):
            def bound(refs, scalars_ref):
                refs.pieces, refs.me = pieces, scalars_ref[0]
                body(refs, scalars_ref)

            bound.__name__ = body.__name__
            made = run_kernel(
                bound, *chain.after(scalars), fetched, ins, outs, stored, scratch, MFLOPS[body]
            )
            chain.token = made[token]
            return made

        class Home:
            def start(self, array):
                self.mine, (other,) = array[:BLK], chain.after(array[BLK:])
                self.wire = swap(other, lambda k: k ^ 3)
                chain.token = other

            def finish(self):
                mine, other = chain.after(self.mine, self.wire)
                ways = jnp.stack([mine, other]), jnp.stack([other, mine])
                self.result = jnp.where(chip == 0, *ways)
                chain.token = self.result

        home_output, home_grad = Home(), Home()

        entry2, q1, k1, v1, lse1, mixed1, middle1, result1 = run(
            post_forward,
            dict(**post_qkv, **tables, w_out=post_out, attn_gain=post_attn_gain, **post_wide)
            | dict(ffn_gain=post_ffn_gain, next_gain=pre_attn_gain),
            dict(own=own_one, sib=sib_one),
            dict(entry=rows_bf),
            saved | dict(middle=rows_f32, result=rows_f32),
            wide,
        )
        sib_two = sibling(entry2)
        mixed2, q2, k2, v2, lse2, kept2 = run(
            attention_forward,
            dict(**pre_qkv, **tables),
            dict(own=entry2, sib=sib_two),
            dict(mixed=saved.pop("mixed")),
            saved | {KEPT: rows_bf},
            {},
        )
        out_rows, grad_gain, grad_middle2, *start2, grads = run(
            pre_ffn,
            dict(w_out=pre_out, result=result1, last_gain=post_ffn_gain, ffn_gain=pre_ffn_gain)
            | dict(**pre_wide, lse=lse2),
            dict(mixed=mixed2, **cotangent),
            dict(output=rows_bf, grad_gain=gain_f32, grad_middle=rows_f32, **start_outs) | ffn_grads,
            {},
            wide | wide_back,
            1,
            ffn_pieces,
        )
        ffn2.grads = grads

        held = {}

        def heads(ready, arrays, weights, first):
            start = 0 if first is None else HALF
            fetched = dict(zip(("q", "k", "v"), arrays)) | weights
            fetched = {name: Columns(array, start) for name, array in fetched.items()} | tables
            ins = dict(zip(("gmix", "delta_t", "lse_t"), ready))
            if first is None:
                outs = heads_outs | dict(ge_sib=rows_f32)
                return run(first_heads_backward, fetched, ins, outs, {}, heads_tmp, token=2)
            ins |= dict(part_own=first[3], part_sib=first[4])
            outs = heads_outs | dict(ge_sib=rows_bf)
            return run(last_heads_backward, fetched, ins, outs, {}, heads_tmp, token=4)

        def pre_heads_a():
            held[1] = heads(start2, (q2, k2, v2), pre_qkv, None)

        def pre_heads_b():
            held[2] = heads(start2, (q2, k2, v2), pre_qkv, held[1])
            held[3] = sibling(held[2][4])

        def ffn_again():
            held[4] = run(
                post_ffn_again,
                dict(middle=middle1, attn_gain=post_attn_gain)
                | dict(w_gate=post_wide["w_gate"], w_up=post_wide["w_up"]),
                {},
                dict(ffn_in=rows_bf) | wide,
                {},
                {},
            )

        def ffn_back():
            ins = dict(zip(("ffn_in", "gate", "up", "hidden"), held[4]))
            *rest, grads = run(
                post_ffn_backward,
                dict(middle=middle1, result=result1, ffn_gain=post_ffn_gain)
                | dict(next_gain=pre_attn_gain, attn_gain=post_attn_gain)
                | dict(**post_wide, w_out=post_out, mixed=mixed1, lse=lse1),
                ins
                | dict(grad_middle=grad_middle2, grad_gain=grad_gain)
                | dict(ge_own=held[2][3], ge_recv=held[3]),
                dict(new_middle=rows_f32) | start_outs | ffn_grads,
                {},
                wide_back,
                2,
                ffn_pieces,
            )
            held[5] = rest
            ffn1.grads = grads

        def weight_grads(total, fetched, grad_middle, own, sib, first, last):
            (grads,) = run(
                attention_weight_grads,
                fetched,
                dict(grad_middle=grad_middle, own=own, sib=sib)
                | dict(zip(("dqa", "dka", "dva"), first))
                | dict(zip(("dqb", "dkb", "dvb"), last)),
                attn_grads,
                {},
                {},
                0,
                attn_pieces,
            )
            total.grads = grads

        def pre_weights():
            weight_grads(attn2, dict(mixed=kept2), grad_middle2, entry2, sib_two, held[1], held[2])

        def post_heads_a():
            held[6] = heads(held[5][1:], (q1, k1, v1), post_qkv, None)

        def post_heads_b():
            held[7] = heads(held[5][1:], (q1, k1, v1), post_qkv, held[6])

        def send_entry():
            (sent,) = chain.after(held[7][4])
            held[8] = sibling(sent)

        def post_weights():
            saved_mix = dict(mixed=mixed1)
            weight_grads(attn1, saved_mix, held[5][0], own_one, sib_one, held[6], held[7])

        def send_output():
            home_output.start(out_rows)

        def send_grad():
            (received,) = chain.after(held[8])
            total = held[5][0] + held[7][3] + received.astype(F32)
            home_grad.start(total.astype(BF))


        plan = (
            ffn2.launch,
            send_output,
            ffn_again,
            ffn2,
            pre_heads_a,
            home_output.finish,
            pre_heads_b,
            ffn2,
            ffn_back,
            ffn1.launch,
            ffn2,
            pre_weights,
            attn2.launch,
            ffn1,
            ffn2,
            post_heads_a,
            attn2,
            ffn2,
            ffn1,
            post_heads_b,
            ffn2,
            send_entry,
            ffn1,
            attn2,
            post_weights,
            ffn2,
            attn1.launch,
            attn2,
            attn1,
            ffn1,
            attn2,
            send_grad,
            ffn1,
            attn1,
            attn2,
            ffn2,
            ffn1,
            attn1,
            home_grad.finish,
            attn2,
            ffn1,
            ffn2,
            attn1,
            attn2,
            ffn1,
            attn1,
            attn1,
            attn1,
            ffn1,
            attn2,
            ffn2.unpack,
            attn1,
            attn2,
            ffn1.unpack,
            attn1,
            attn2.unpack,
            attn1.unpack,
        )
        for action in plan:
            if isinstance(action, Sum):
                action.step()
            else:
                action()
        sums = (ffn2, ffn1, attn2, attn1)
        for again in range(2 * bits):
            for total in sums:
                total.step()
        for total in sums:
            total.unpack()
        down2, gate2, up2 = ffn2.result
        down1, gate1, up1, *gains = ffn1.result
        gain_pre_ffn, gain_pre_attn, gain_post_ffn, gain_post_attn = (g.reshape(D) for g in gains)
        out2, query2, key2, value2 = attn2.result
        out1, query1, key1, value1 = attn1.result
        post_grads = (query1, key1, value1, out1, gate1.T, up1.T, down1, gain_post_attn, gain_post_ffn)
        pre_grads = (query2, key2, value2, out2, gate2.T, up2.T, down2, gain_pre_attn, gain_pre_ffn)
        return (home_output.result, home_grad.result) + post_grads + pre_grads

    spread = P("dp", "sp", None)
    in_specs = (spread, P("dp")) + (P(),) * 18 + (spread,)
    out_specs = (spread, spread) + (P(),) * 18
    return jax.shard_map(body, mesh=mesh, in_specs=in_specs, out_specs=out_specs, check_vma=False)
```

```python
import jax
import jax.numpy as jnp
import numpy as np
from jax import lax
from jax.experimental import pallas as pl
from jax.experimental.pallas import tpu as pltpu
from jax.sharding import PartitionSpec as P

D = 512
HEADS = 8
HD = 64
FF = 1376
SEQ = 1024
EPS = 1e-06
NEG = -1000000000.0
AXES = ("dp", "sp")
BF = jnp.bfloat16
F32 = jnp.float32
LANES = 128
PANELS = D // LANES
BLK = SEQ // 4
ROWS = 2 * BLK
HALF = D // 2
SCALE = HD ** (-0.5)
FFN_ROWS = 3 * PANELS * FF
ATTN_ROWS = 4 * PANELS * D
GAIN_ROWS = 16
KEPT = "kept"
VMEM_LIMIT = 28 << 20


def dot(left, right):
    return lax.dot_general(left, right, (((1,), (0,)), ((), ())), preferred_element_type=F32)


def dot_nt(left, right):
    return lax.dot_general(left, right, (((1,), (1,)), ((), ())), preferred_element_type=F32)


def dot_tn(left, right):
    return lax.dot_general(left, right, (((0,), (0,)), ((), ())), preferred_element_type=F32)


def inv_rms(values):
    return lax.rsqrt(jnp.mean(values * values, axis=-1, keepdims=True) + EPS)


def rms_back(values, gain, upstream):
    scale = inv_rms(values)
    weighted = upstream * gain
    grad = scale * weighted - values * (
        scale * scale * scale * jnp.mean(weighted * values, axis=-1, keepdims=True)
    )
    grad_gain = jnp.sum(upstream * (values * scale), axis=0, keepdims=True)
    return grad, grad_gain


class Refs:
    def __init__(self, vmem, fetched, stored, sems):
        self.vmem, self.stored, self.sems = vmem, stored, sems
        self.waiting, self.sent = {}, []
        for name in fetched:
            copy = pltpu.make_async_copy(fetched[name], vmem[name], self.next_sem())
            copy.start()
            self.waiting[name] = copy

    used = 0

    def next_sem(self):
        self.used += 1
        return self.sems.at[self.used - 1]

    def __getattr__(self, name):
        if name in self.waiting:
            self.waiting.pop(name).wait()
        return self.vmem[name]

    def send(self, *refs):
        for ref in refs:
            for name in self.stored:
                if self.vmem[name] is ref:
                    self.send_as(name, ref)

    def send_as(self, name, ref):
        if name in self.stored:
            copy = pltpu.make_async_copy(ref, self.stored[name], self.next_sem())
            copy.start()
            self.sent.append(copy)

    def finish(self):
        for name in list(self.waiting):
            self.waiting.pop(name).wait()
        for copy in self.sent:
            copy.wait()


class Columns:
    def __init__(self, array, start):
        self.array, self.start = array, start


def in_hbm(array):
    if isinstance(array, Columns):
        array = array.array
    return pltpu.with_memory_space_constraint(array, pltpu.HBM)


def run_kernel(body, scalars, fetched, ins, outs, stored, scratch, mflops):
    names = list(ins) + list(outs) + list(fetched) + list(stored) + list(scratch)
    n_f, n_in, n_out, n_st = len(fetched), len(ins), len(outs), len(stored)
    shapes = []
    for array in fetched.values():
        if isinstance(array, Columns):
            shapes.append(pltpu.VMEM((array.array.shape[0], HALF), array.array.dtype))
        else:
            shapes.append(pltpu.VMEM(array.shape, array.dtype))
    shapes += [pltpu.VMEM((8, LANES) if n == KEPT else stored[n][0], stored[n][1]) for n in stored]
    shapes += [pltpu.VMEM(*scratch[n]) for n in scratch]

    def kernel(scalars_ref, *args):
        head = n_f + n_in + n_out
        hbm_in, on_chip, hbm_out = list(args[:n_f]), args[n_f:head], args[head : head + n_st]
        for k, array in enumerate(fetched.values()):
            if isinstance(array, Columns):
                hbm_in[k] = hbm_in[k].at[:, pl.ds(array.start, HALF)]
        vmem = dict(zip(names, on_chip + args[head + n_st : -1]))
        refs = Refs(vmem, dict(zip(fetched, hbm_in)), dict(zip(stored, hbm_out)), args[-1])
        body(refs, scalars_ref)
        refs.finish()

    on_chip, off_chip = (pl.BlockSpec(memory_space=m) for m in (pltpu.VMEM, pltpu.HBM))
    made = pl.pallas_call(
        kernel,
        name=body.__name__,
        out_shape=[jax.ShapeDtypeStruct(*outs[n]) for n in outs]
        + [pltpu.HBM(*stored[n]) for n in stored],
        grid_spec=pltpu.PrefetchScalarGridSpec(
            num_scalar_prefetch=1,
            grid=(),
            in_specs=[off_chip] * n_f + [on_chip] * n_in,
            out_specs=[on_chip] * n_out + [off_chip] * n_st,
            scratch_shapes=shapes + [pltpu.SemaphoreType.DMA((max(n_f + n_st, 1),))],
        ),
        compiler_params=pltpu.CompilerParams(vmem_limit_bytes=VMEM_LIMIT),
        cost_estimate=pl.CostEstimate(flops=mflops * 10**6, transcendentals=0, bytes_accessed=1),
    )(scalars, *[in_hbm(a) for a in fetched.values()], *ins.values())
    return made


def piece_position(j, me, order):
    where = 0
    for bit in order:
        where = where * 2 + (((me >> bit) & 1) ^ ((j >> bit) & 1))
    return where


def segments(pieces, start, end):
    rows = pieces[2]
    while start < end:
        stop = min(end, (start // rows + 1) * rows)
        yield start // rows, start % rows, start, stop - start
        start = stop


def put_rows(refs, pieces, start, block):
    orders, count, rows = pieces
    me = refs.me
    for j, inside, at, length in segments(pieces, start, start + block.shape[0]):
        spot = piece_position(j, me, orders[j & 1]) + ((me ^ j) & 1) * (count // 2)
        put = pl.ds(pl.multiple_of(spot * rows + inside, 16), length)
        refs.grads[put, :] = block[at - start : at - start + length, :]


def head_lanes(rows, which):
    lane = lax.broadcasted_iota(jnp.int32, (rows, LANES), 1)
    return (lane < HD) if which == 0 else (lane >= HD)


def only_head(panel, which):
    return jnp.where(head_lanes(panel.shape[0], which), panel, jnp.zeros_like(panel))


def turned(panel):
    lane = lax.broadcasted_iota(jnp.int32, panel.shape, 1)
    return jnp.where(
        lane % HD < HD // 2,
        pltpu.roll(panel, LANES - HD // 2, 1),
        pltpu.roll(panel, HD // 2, 1),
    )


def block_rows(index):
    return pl.ds(pl.multiple_of(index * BLK, BLK), BLK)


def rope_tables():
    lane = np.arange(LANES)
    inverse = np.float32(10000.0) ** (-np.arange(HD // 2, dtype=np.float32) * np.float32(2.0 / HD))
    places = np.concatenate([np.arange(BLK), np.arange(8) * BLK]).astype(np.float32)
    angles = (places[:, None] * inverse[None, :])[:, lane % (HD // 2)].astype(np.float64)
    sign = np.where(lane % HD < HD // 2, -1.0, 1.0)
    return np.cos(angles).astype(np.float32), (np.sin(angles) * sign).astype(np.float32)


def rope_of(refs, block):
    cosine, sine = refs.cosine[0:BLK, :], refs.sine[0:BLK, :]
    start = pl.ds(BLK + block, 1)
    start_cos, start_sin = refs.cosine[start, :], refs.sine[start, :]
    return cosine * start_cos - sine * start_sin, sine * start_cos + cosine * start_sin


def panel_cols(panel):
    return slice(panel * LANES, (panel + 1) * LANES)


def blocks_of(sp):
    return sp, 3 - sp


def project_heads(refs, sp, entry, own):
    for half, block in enumerate(blocks_of(sp)):
        here = slice(half * BLK, (half + 1) * BLK)
        there = block_rows(block)
        rows = entry[here, :]
        keys = dot(rows, refs.w_key[...])
        refs.v[there, :] = dot(rows, refs.w_value[...]).astype(BF)
        if own:
            queries = dot(rows, refs.w_query[...])
        cosine, sine = rope_of(refs, block)
        for panel in range(PANELS):
            cols = panel_cols(panel)
            part = keys[:, cols]
            refs.k[there, cols] = (part * cosine + turned(part) * sine).astype(BF)
            if own:
                part = queries[:, cols]
                refs.q[here, cols] = (part * cosine + turned(part) * sine).astype(BF) * SCALE


def query_blocks(sp, low):
    chip = sp >> 1
    return (block_rows(chip), low + 1), (block_rows(1 - chip), 4 - low)


def both_ways(sp, step):
    low = (sp & 1) ^ (sp >> 1)

    @pl.when(low == 0)
    def outer():
        step(0)

    @pl.when(low == 1)
    def inner():
        step(1)


def attend(refs, scalars, low):
    sp, length = scalars[1], scalars[2]
    lane = lax.broadcasted_iota(jnp.int32, (BLK, LANES), 1)
    most = (4 - low) * BLK
    past = jnp.where(lax.broadcasted_iota(jnp.int32, (1, most), 1) < length, 0.0, NEG)
    causal = lax.broadcasted_iota(jnp.int32, (BLK, BLK), 1) <= lax.broadcasted_iota(
        jnp.int32, (BLK, BLK), 0
    )

    def panel_step(panel, carry):
        cols = pl.ds(pl.multiple_of(panel * LANES, LANES), LANES)
        jobs = []
        for rows, blocks in query_blocks(sp, low):
            queries = refs.q[rows, cols]
            for which in range(2):
                seen = blocks * BLK
                scores = dot_nt(only_head(queries, which), refs.k[0:seen, cols])
                jobs.append((rows, blocks, which, scores))
        done = {}
        for rows, blocks, which, scores in jobs:
            before = (blocks - 1) * BLK
            last = jnp.where(causal, scores[:, before:] + past[:, before : before + BLK], NEG)
            if before:
                scores = jnp.concatenate([scores[:, :before] + past[:, :before], last], axis=1)
            else:
                scores = last
            top = jnp.max(scores, axis=-1, keepdims=True)
            weights = jnp.exp(scores - top)
            total = jnp.sum(weights, axis=-1, keepdims=True)
            mixed = dot(weights.astype(BF), refs.v[0 : blocks * BLK, cols]) / total
            done[blocks, which] = mixed, top + jnp.log(total)
        for rows, blocks in query_blocks(sp, low):
            (one, log_one), (two, log_two) = done[blocks, 0], done[blocks, 1]
            refs.mixed[rows, cols] = jnp.where(head_lanes(BLK, 0), one, two).astype(BF)
            kept = jnp.where(lane == 2 * panel, log_one, refs.lse[rows, :])
            refs.lse[rows, :] = jnp.where(lane == 2 * panel + 1, log_two, kept)
        return carry

    lax.fori_loop(0, PANELS, panel_step, 0)


def attention_forward(refs, scalars):
    sp = scalars[1]
    project_heads(refs, sp, refs.own, True)
    project_heads(refs, sp ^ 1, refs.sib, False)
    refs.send(refs.q, refs.k, refs.v)
    refs.lse[...] = jnp.zeros((ROWS, LANES), F32)
    both_ways(sp, lambda low: attend(refs, scalars, low))
    refs.send(refs.lse, refs.mixed)
    refs.send_as(KEPT, refs.mixed)


def ffn_forward(refs, ffn_in):
    for half in range(2):
        rows = slice(half * BLK, (half + 1) * BLK)
        gate = dot_nt(ffn_in[rows, :], refs.w_gate[...])
        up = dot_nt(ffn_in[rows, :], refs.w_up[...])
        refs.gate[rows, :] = gate
        refs.up[rows, :] = up
        refs.hidden[rows, :] = (gate * jax.nn.sigmoid(gate) * up).astype(BF)


def store_panels(refs, at, grad):
    height, width = grad.shape
    for panel in range(width // LANES):
        block = grad[:, panel_cols(panel)].astype(BF)
        put_rows(refs, refs.pieces, at + panel * height, block)


def ffn_weight_grads(refs, at, ffn_in, grad_result):
    grad_down = grad_result.astype(BF)
    store_panels(refs, at, dot_tn(refs.hidden[...], grad_down))
    for half in range(2):
        rows = slice(half * BLK, (half + 1) * BLK)
        grad_hidden = dot_nt(grad_down[rows, :], refs.w_down[...])
        gate = refs.gate[rows, :]
        sigma = jax.nn.sigmoid(gate)
        grad_gate = grad_hidden * refs.up[rows, :] * (sigma * (1.0 + gate * (1.0 - sigma)))
        refs.dgate[rows, :] = grad_gate.astype(BF)
        refs.dup[rows, :] = (grad_hidden * (gate * sigma)).astype(BF)
    store_panels(refs, at + PANELS * FF, dot_tn(refs.dgate[...], ffn_in))
    store_panels(refs, at + 2 * PANELS * FF, dot_tn(refs.dup[...], ffn_in))


def ffn_input_grad(refs):
    return dot(refs.dgate[...], refs.w_gate[...]) + dot(refs.dup[...], refs.w_up[...])


def store_tail(refs, gains):
    end = refs.grads.shape[0]
    row = lax.broadcasted_iota(jnp.int32, (end - FFN_ROWS, LANES), 0)
    block = jnp.zeros((end - FFN_ROWS, LANES), F32)
    for slot, gain in enumerate(gains):
        for panel in range(PANELS):
            block = jnp.where(row == PANELS * slot + panel, gain[:, panel_cols(panel)], block)
    put_rows(refs, refs.pieces, FFN_ROWS, block.astype(BF))


def post_forward(refs, scalars):
    attention_forward(refs, scalars)
    middle = refs.own[...].astype(F32) + dot(refs.mixed[...], refs.w_out[...])
    refs.middle[...] = middle
    refs.send(refs.middle)
    state = middle * inv_rms(middle) * refs.attn_gain[...]
    ffn_forward(refs, state.astype(BF))
    result = state + dot(refs.hidden[...], refs.w_down[...])
    refs.result[...] = result
    refs.send(refs.result)
    output = result * inv_rms(result) * refs.ffn_gain[...]
    entry = output * inv_rms(output) * refs.next_gain[...]
    refs.entry[...] = entry.astype(BF)


def masked_cotangent(refs, scalars):
    sp, length = scalars[1], scalars[2]
    row = lax.broadcasted_iota(jnp.int32, (BLK, D), 0)
    parts = []
    for block, ref in zip(blocks_of(sp), (refs.cot_mine, refs.cot_other)):
        parts.append(jnp.where(row + block * BLK < length, ref[...].astype(F32), 0.0))
    return jnp.concatenate(parts, axis=0)


def attend_back(refs, scalars, low, first_panel):
    sp, length = scalars[1], scalars[2]
    if low == 1:
        refs.dk[3 * BLK :, :] = jnp.zeros((BLK, HALF), F32)
        refs.dv[3 * BLK :, :] = jnp.zeros((BLK, HALF), F32)

    def panel_step(panel, carry):
        cols = pl.ds(pl.multiple_of((first_panel + panel) * LANES, LANES), LANES)
        put = pl.ds(pl.multiple_of(panel * LANES, LANES), LANES)
        for rows, blocks in reversed(query_blocks(sp, low)):
            seen = blocks * BLK
            queries = refs.q[rows, put]
            grads = refs.gmix[rows, cols]
            keys = refs.k[0:seen, put]
            values = refs.v[0:seen, put]
            key_at = lax.broadcasted_iota(jnp.int32, (seen, BLK), 0)
            row_at = lax.broadcasted_iota(jnp.int32, (seen, BLK), 1) + (blocks - 1) * BLK
            allowed = (key_at <= row_at) & (key_at < length)
            grad_q = jnp.zeros((LANES, BLK), F32)
            grad_k = jnp.zeros((seen, LANES), F32)
            grad_v = jnp.zeros((seen, LANES), F32)
            jobs = []
            for which in range(2):
                q_head = only_head(queries, which)
                g_head = only_head(grads, which)
                jobs.append((q_head, g_head, dot_nt(keys, q_head), dot_nt(values, g_head)))
            for which, (q_head, g_head, scores, grad_p) in enumerate(jobs):
                at = pl.ds(2 * (first_panel + panel) + which, 1)
                probs = jnp.exp(jnp.where(allowed, scores, NEG) - refs.lse_t[at, rows])
                grad_s = (probs * (grad_p - refs.delta_t[at, rows])).astype(BF)
                grad_v = grad_v + dot(probs.astype(BF), g_head)
                grad_k = grad_k + dot(grad_s, q_head)
                grad_q = grad_q + dot_tn(only_head(keys, which), grad_s)
            refs.dq[rows, put] = jnp.transpose(grad_q) * SCALE
            if blocks == 4 - low:
                refs.dk[0:seen, put] = grad_k
                refs.dv[0:seen, put] = grad_v
            else:
                refs.dk[0:seen, put] += grad_k
                refs.dv[0:seen, put] += grad_v
        return carry

    lax.fori_loop(0, PANELS // 2, panel_step, 0)


def start_attention_backward(refs, grad_middle):
    grad_mixed = dot_nt(grad_middle.astype(BF), refs.w_out[...]).astype(BF)
    refs.gmix[...] = grad_mixed
    product = grad_mixed.astype(F32) * refs.mixed[...].astype(F32)
    high = product.astype(BF)
    rest = (product - high.astype(F32)).astype(BF)
    head_of = lax.broadcasted_iota(jnp.int32, (HEADS, D), 1) // HD
    pick = (head_of == lax.broadcasted_iota(jnp.int32, (HEADS, D), 0)).astype(F32).astype(BF)
    refs.delta_t[...] = dot_nt(pick, high) + dot_nt(pick, rest)
    refs.lse_t[...] = jnp.transpose(refs.lse[...])[0:HEADS, :]


def attention_backward(refs, scalars, first_panel):
    sp = scalars[1]
    refs.q, refs.k, refs.v
    both_ways(sp, lambda low: attend_back(refs, scalars, low, first_panel))

    for spot, block in enumerate(blocks_of(sp) + blocks_of(sp ^ 1)):
        put, there = slice(spot * BLK, (spot + 1) * BLK), block_rows(block)
        refs.dvp[put, :] = refs.dv[there, :].astype(BF)
        cosine, sine = rope_of(refs, block)
        for panel in range(PANELS // 2):
            cols = panel_cols(panel)
            part = refs.dk[there, cols]
            refs.dkp[put, cols] = (part * cosine - turned(part) * sine).astype(BF)
            if spot < 2:
                part = refs.dq[put, cols]
                refs.dqp[put, cols] = (part * cosine - turned(part) * sine).astype(BF)
    w_query, w_key, w_value = refs.w_query[...], refs.w_key[...], refs.w_value[...]
    mine, theirs = slice(0, ROWS), slice(ROWS, 2 * ROWS)
    ge_sib = dot_nt(refs.dkp[theirs, :], w_key) + dot_nt(refs.dvp[theirs, :], w_value)
    ge_own = (
        dot_nt(refs.dqp[...], w_query)
        + dot_nt(refs.dkp[mine, :], w_key)
        + dot_nt(refs.dvp[mine, :], w_value)
    )
    return ge_own, ge_sib


def first_heads_backward(refs, scalars):
    refs.ge_own[...], refs.ge_sib[...] = attention_backward(refs, scalars, 0)


def last_heads_backward(refs, scalars):
    ge_own, ge_sib = attention_backward(refs, scalars, PANELS // 2)
    refs.ge_own[...] = refs.part_own[...] + ge_own
    refs.ge_sib[...] = (refs.part_sib[...] + ge_sib).astype(BF)


def pre_ffn(refs, scalars):
    store_tail(refs, ())
    result = refs.result[...]
    inputs = result * inv_rms(result) * refs.last_gain[...]
    middle = inputs + dot(refs.mixed[...], refs.w_out[...])
    gain = refs.ffn_gain[...]
    ffn_in = (middle * inv_rms(middle) * gain).astype(BF)
    ffn_forward(refs, ffn_in)
    output = middle + dot(refs.hidden[...], refs.w_down[...])
    refs.output[...] = output.astype(BF)
    cotangent = masked_cotangent(refs, scalars)
    ffn_weight_grads(refs, 0, ffn_in, cotangent)
    grad_normed, grad_gain = rms_back(middle, gain, ffn_input_grad(refs))
    grad_middle = cotangent + grad_normed
    refs.grad_middle[...] = grad_middle
    refs.grad_gain[...] = grad_gain
    start_attention_backward(refs, grad_middle)


def attention_weight_grads(refs, scalars):
    step = PANELS * D
    store_panels(refs, 0, dot_tn(refs.mixed[...], refs.grad_middle[...].astype(BF)))
    own, sib = refs.own[...], refs.sib[...]
    for half in range(2):
        put = half * step // 2
        dqp, dkp, dvp = ((refs.dqa, refs.dka, refs.dva), (refs.dqb, refs.dkb, refs.dvb))[half]
        store_panels(refs, step + put, dot_tn(own, dqp[...]))
        for k, ref in enumerate((dkp, dvp)):
            total = dot_tn(own, ref[0:ROWS, :]) + dot_tn(sib, ref[ROWS : 2 * ROWS, :])
            store_panels(refs, (k + 2) * step + put, total)


def post_ffn_again(refs, scalars):
    middle = refs.middle[...]
    ffn_in = (middle * inv_rms(middle) * refs.attn_gain[...]).astype(BF)
    refs.ffn_in[...] = ffn_in
    ffn_forward(refs, ffn_in)


def post_ffn_backward(refs, scalars):
    middle, result = refs.middle[...], refs.result[...]
    out_gain = refs.ffn_gain[...]
    inputs = result * inv_rms(result) * out_gain
    grad_entry = refs.ge_own[...] + refs.ge_recv[...].astype(F32)
    grad_normed, grad_next = rms_back(inputs, refs.next_gain[...], grad_entry)
    grad_result, grad_ffn_gain = rms_back(result, out_gain, refs.grad_middle[...] + grad_normed)
    ffn_weight_grads(refs, 0, refs.ffn_in[...], grad_result)
    upstream = grad_result + ffn_input_grad(refs)
    grad_middle, grad_attn_gain = rms_back(middle, refs.attn_gain[...], upstream)
    refs.new_middle[...] = grad_middle
    store_tail(refs, (refs.grad_gain[...], grad_next, grad_ffn_gain, grad_attn_gain))
    start_attention_backward(refs, grad_middle)


MFLOPS = {
    post_forward: 120000,
    attention_forward: 90000,
    pre_ffn: 105000,
    first_heads_backward: 67500,
    last_heads_backward: 67500,
    post_ffn_again: 37500,
    post_ffn_backward: 82500,
    attention_weight_grads: 22500,
}


def unpack(mine, other, scalars, pieces, heights, gains):
    orders, count, rows = pieces
    shapes = [(height, D) for height in heights] + [(PANELS, LANES)] * gains
    n_out = len(shapes)

    def unpack(scalars_ref, mine_ref, other_ref, *rest):
        outs, staged, sems = rest[:n_out], rest[n_out : 2 * n_out], rest[-1]
        me = scalars_ref[0]

        def lay_out(halves):
            sent, at = [], 0
            for k in range(n_out):
                height, width = shapes[k]
                if k < len(heights):
                    for panel in range(PANELS):
                        for j, inside, row, length in segments(pieces, at, at + height):
                            spot = piece_position(j, me, orders[j & 1]) * rows + inside
                            take = pl.ds(pl.multiple_of(spot, 16), length)
                            put = slice(row - at, row - at + length)
                            staged[k][put, panel_cols(panel)] = halves[j & 1][take, :].astype(F32)
                        at += height
                else:
                    if k == len(heights):
                        ((j, inside, row, length),) = segments(pieces, at, at + GAIN_ROWS)
                        spot = piece_position(j, me, orders[j & 1]) * rows + inside
                        take = pl.ds(pl.multiple_of(spot, 16), GAIN_ROWS)
                        block = halves[j & 1][take, :].astype(F32)
                    slot = (k - len(heights)) * PANELS
                    staged[k][...] = block[slot : slot + PANELS, :]
                sent.append(pltpu.make_async_copy(staged[k], outs[k], sems.at[k]))
                sent[-1].start()
            for copy in sent:
                copy.wait()

        @pl.when(me & 1 == 0)
        def even():
            lay_out((mine_ref, other_ref))

        @pl.when(me & 1 == 1)
        def odd():
            lay_out((other_ref, mine_ref))

    on_chip, off_chip = (pl.BlockSpec(memory_space=m) for m in (pltpu.VMEM, pltpu.HBM))
    return pl.pallas_call(
        unpack,
        name=unpack.__name__,
        out_shape=[jax.ShapeDtypeStruct(shape, F32) for shape in shapes],
        grid_spec=pltpu.PrefetchScalarGridSpec(
            num_scalar_prefetch=1,
            grid=(),
            in_specs=[on_chip] * 2,
            out_specs=[off_chip] * n_out,
            scratch_shapes=[pltpu.VMEM(shape, F32) for shape in shapes]
            + [pltpu.SemaphoreType.DMA((n_out,))],
        ),
        compiler_params=pltpu.CompilerParams(vmem_limit_bytes=VMEM_LIMIT),
        cost_estimate=pl.CostEstimate(
            flops=0, transcendentals=0, bytes_accessed=6 * mine.shape[0] * LANES * 2
        ),
    )(scalars, mine, other)


def solution(mesh):
    n_dp, n_sp = mesh.shape["dp"], mesh.shape["sp"]
    count = n_dp * n_sp
    if n_sp != 4 or n_dp & (n_dp - 1) or n_dp < 2:
        raise ValueError
    bits = count.bit_length() - 1

    def swap(array, move):
        return lax.ppermute(array, AXES, [(k, move(k)) for k in range(count)])

    def sibling(array):
        return swap(array, lambda k: k ^ 1)

    tail = list(range(3, bits))
    orders = ([1, 2] + tail, [2, 1] + tail)

    def pieces_for(used):
        return orders, count, pl.cdiv(pl.cdiv(used, count), 16) * 16

    class Chain:
        def __init__(self):
            self.token = None

        def after(self, *arrays):
            if self.token is None:
                return arrays
            return lax.optimization_barrier(arrays + (self.token,))[:-1]

    class Sum:
        def __init__(self, chain, scalars, pieces, heights, gains):
            self.chain, self.scalars, self.pieces = chain, scalars, pieces
            self.heights, self.gains = heights, gains
            self.stage, self.result = 0, None

        def move(self, stage):
            return lambda k: k ^ (1 << orders[k & 1][stage])

        def launch(self):
            (grads,) = self.chain.after(self.grads)
            half = grads.shape[0] // 2
            sent = grads[half:]
            self.keep, self.wire = grads[:half], sibling(sent)
            self.chain.token = sent

        def step(self):
            last = bits - 1
            if self.stage > 2 * last:
                return
            keep, wire = self.chain.after(self.keep, self.wire)
            if self.stage < last:
                half = keep.shape[0] // 2
                sent = (keep[half:].astype(F32) + wire[half:].astype(F32)).astype(BF)
                self.keep = (keep[:half].astype(F32) + wire[:half].astype(F32)).astype(BF)
                self.wire = swap(sent, self.move(self.stage))
            else:
                if self.stage == last:
                    sent = (keep.astype(F32) + wire.astype(F32)).astype(BF)
                else:
                    sent = jnp.concatenate([keep, wire], axis=0)
                back = 2 * last - 1 - self.stage
                self.keep = sent
                self.wire = sibling(sent) if back < 0 else swap(sent, self.move(back))
            self.chain.token = sent
            self.stage += 1

        def unpack(self):
            if self.result is None and self.stage == 2 * bits - 1:
                ready = self.chain.after(self.keep, self.wire)
                self.result = unpack(*ready, self.scalars, self.pieces, self.heights, self.gains)
                self.chain.token = self.result[-1]

    def body(tokens, lengths, *rest):
        out_grad = rest[-1]
        post_query, post_key, post_value, post_out, post_gate, post_up, post_down = rest[0:7]
        pre_query, pre_key, pre_value, pre_out, pre_gate, pre_up, pre_down = rest[9:16]
        gains = [rest[k].reshape(1, D) for k in (7, 8, 16, 17)]
        post_attn_gain, post_ffn_gain, pre_attn_gain, pre_ffn_gain = gains
        sp = lax.axis_index("sp")
        me = lax.axis_index("dp") * n_sp + sp
        chip = sp >> 1
        scalars = jnp.stack([me, sp, lengths[chip]]).astype(jnp.int32)

        def to_slot(array):
            mine = lax.dynamic_index_in_dim(array, chip, 0, keepdims=False)
            other = lax.dynamic_index_in_dim(array, 1 - chip, 0, keepdims=False)
            return mine, swap(other, lambda k: k ^ 3)

        cosine, sine = rope_tables()
        tables = dict(cosine=cosine, sine=sine)

        own_one = jnp.concatenate(to_slot(tokens), axis=0)
        sib_one = sibling(own_one)
        cotangent = dict(zip(("cot_mine", "cot_other"), to_slot(out_grad)))

        rows_bf, rows_f32, full_bf = ((ROWS, D), BF), ((ROWS, D), F32), ((SEQ, D), BF)
        wide_bf, wide_f32 = ((ROWS, FF), BF), ((ROWS, FF), F32)
        gain_f32, head_f32 = ((1, D), F32), ((HEADS, ROWS), F32)
        half_bf, half_f32 = ((SEQ, HALF), BF), ((SEQ, HALF), F32)
        half_rows_bf, half_rows_f32 = ((ROWS, HALF), BF), ((ROWS, HALF), F32)
        saved = dict(q=rows_bf, k=full_bf, v=full_bf, lse=((ROWS, LANES), F32), mixed=rows_bf)
        wide = dict(gate=wide_f32, up=wide_f32, hidden=wide_bf)
        wide_back = dict(dgate=wide_bf, dup=wide_bf)
        post_wide = dict(w_gate=post_gate.T, w_up=post_up.T, w_down=post_down)
        pre_wide = dict(w_gate=pre_gate.T, w_up=pre_up.T, w_down=pre_down)
        post_qkv = dict(w_key=post_key, w_value=post_value, w_query=post_query)
        pre_qkv = dict(w_key=pre_key, w_value=pre_value, w_query=pre_query)
        heads_outs = dict(dqp=half_rows_bf, dkp=half_bf, dvp=half_bf, ge_own=rows_f32)
        heads_tmp = dict(dq=half_rows_f32, dk=half_f32, dv=half_f32)
        start_outs = dict(gmix=rows_bf, delta_t=head_f32, lse_t=head_f32)

        chain = Chain()
        ffn_pieces, attn_pieces = pieces_for(FFN_ROWS + GAIN_ROWS), pieces_for(ATTN_ROWS)
        ffn_grads = dict(grads=((count * ffn_pieces[2], LANES), BF))
        attn_grads = dict(grads=((count * attn_pieces[2], LANES), BF))
        ffn2 = Sum(chain, scalars, ffn_pieces, [FF] * 3, 0)
        ffn1 = Sum(chain, scalars, ffn_pieces, [FF] * 3, 4)
        attn2 = Sum(chain, scalars, attn_pieces, [D] * 4, 0)
        attn1 = Sum(chain, scalars, attn_pieces, [D] * 4, 0)

        def run(body, fetched, ins, outs, stored, scratch, token=0, pieces=None):
            def bound(refs, scalars_ref):
                refs.pieces, refs.me = pieces, scalars_ref[0]
                body(refs, scalars_ref)

            bound.__name__ = body.__name__
            made = run_kernel(
                bound, *chain.after(scalars), fetched, ins, outs, stored, scratch, MFLOPS[body]
            )
            chain.token = made[token]
            return made

        class Home:
            def start(self, array):
                self.mine, (other,) = array[:BLK], chain.after(array[BLK:])
                self.wire = swap(other, lambda k: k ^ 3)
                chain.token = other

            def finish(self):
                mine, other = chain.after(self.mine, self.wire)
                ways = jnp.stack([mine, other]), jnp.stack([other, mine])
                self.result = jnp.where(chip == 0, *ways)
                chain.token = self.result

        home_output, home_grad = Home(), Home()

        entry2, q1, k1, v1, lse1, mixed1, middle1, result1 = run(
            post_forward,
            dict(**post_qkv, **tables, w_out=post_out, attn_gain=post_attn_gain, **post_wide)
            | dict(ffn_gain=post_ffn_gain, next_gain=pre_attn_gain),
            dict(own=own_one, sib=sib_one),
            dict(entry=rows_bf),
            saved | dict(middle=rows_f32, result=rows_f32),
            wide,
        )
        sib_two = sibling(entry2)
        mixed2, q2, k2, v2, lse2, kept2 = run(
            attention_forward,
            dict(**pre_qkv, **tables),
            dict(own=entry2, sib=sib_two),
            dict(mixed=saved.pop("mixed")),
            saved | {KEPT: rows_bf},
            {},
        )
        out_rows, grad_gain, grad_middle2, *start2, grads = run(
            pre_ffn,
            dict(w_out=pre_out, result=result1, last_gain=post_ffn_gain, ffn_gain=pre_ffn_gain)
            | dict(**pre_wide, lse=lse2),
            dict(mixed=mixed2, **cotangent),
            dict(output=rows_bf, grad_gain=gain_f32, grad_middle=rows_f32, **start_outs) | ffn_grads,
            {},
            wide | wide_back,
            1,
            ffn_pieces,
        )
        ffn2.grads = grads

        held = {}

        def heads(ready, arrays, weights, first):
            start = 0 if first is None else HALF
            fetched = dict(zip(("q", "k", "v"), arrays)) | weights
            fetched = {name: Columns(array, start) for name, array in fetched.items()} | tables
            ins = dict(zip(("gmix", "delta_t", "lse_t"), ready))
            if first is None:
                outs = heads_outs | dict(ge_sib=rows_f32)
                return run(first_heads_backward, fetched, ins, outs, {}, heads_tmp, token=2)
            ins |= dict(part_own=first[3], part_sib=first[4])
            outs = heads_outs | dict(ge_sib=rows_bf)
            return run(last_heads_backward, fetched, ins, outs, {}, heads_tmp, token=4)

        def pre_heads_a():
            held[1] = heads(start2, (q2, k2, v2), pre_qkv, None)

        def pre_heads_b():
            held[2] = heads(start2, (q2, k2, v2), pre_qkv, held[1])
            held[3] = sibling(held[2][4])

        def ffn_again():
            held[4] = run(
                post_ffn_again,
                dict(middle=middle1, attn_gain=post_attn_gain)
                | dict(w_gate=post_wide["w_gate"], w_up=post_wide["w_up"]),
                {},
                dict(ffn_in=rows_bf) | wide,
                {},
                {},
            )

        def ffn_back():
            ins = dict(zip(("ffn_in", "gate", "up", "hidden"), held[4]))
            *rest, grads = run(
                post_ffn_backward,
                dict(middle=middle1, result=result1, ffn_gain=post_ffn_gain)
                | dict(next_gain=pre_attn_gain, attn_gain=post_attn_gain)
                | dict(**post_wide, w_out=post_out, mixed=mixed1, lse=lse1),
                ins
                | dict(grad_middle=grad_middle2, grad_gain=grad_gain)
                | dict(ge_own=held[2][3], ge_recv=held[3]),
                dict(new_middle=rows_f32) | start_outs | ffn_grads,
                {},
                wide_back,
                2,
                ffn_pieces,
            )
            held[5] = rest
            ffn1.grads = grads

        def weight_grads(total, fetched, grad_middle, own, sib, first, last):
            (grads,) = run(
                attention_weight_grads,
                fetched,
                dict(grad_middle=grad_middle, own=own, sib=sib)
                | dict(zip(("dqa", "dka", "dva"), first))
                | dict(zip(("dqb", "dkb", "dvb"), last)),
                attn_grads,
                {},
                {},
                0,
                attn_pieces,
            )
            total.grads = grads

        def pre_weights():
            weight_grads(attn2, dict(mixed=kept2), grad_middle2, entry2, sib_two, held[1], held[2])

        def post_heads_a():
            held[6] = heads(held[5][1:], (q1, k1, v1), post_qkv, None)

        def post_heads_b():
            held[7] = heads(held[5][1:], (q1, k1, v1), post_qkv, held[6])

        def send_entry():
            (sent,) = chain.after(held[7][4])
            held[8] = sibling(sent)

        def post_weights():
            saved_mix = dict(mixed=mixed1)
            weight_grads(attn1, saved_mix, held[5][0], own_one, sib_one, held[6], held[7])

        def send_output():
            home_output.start(out_rows)

        def send_grad():
            (received,) = chain.after(held[8])
            total = held[5][0] + held[7][3] + received.astype(F32)
            home_grad.start(total.astype(BF))


        plan = (
            ffn2.launch,
            send_output,
            ffn_again,
            ffn2,
            pre_heads_a,
            home_output.finish,
            pre_heads_b,
            ffn2,
            ffn_back,
            ffn1.launch,
            ffn2,
            pre_weights,
            attn2.launch,
            ffn1,
            ffn2,
            post_heads_a,
            attn2,
            ffn2,
            ffn1,
            post_heads_b,
            post_weights,
            ffn2,
            attn1.launch,
            send_entry,
            ffn1,
            attn2,
            ffn2,
            attn2,
            attn1,
            ffn1,
            attn2,
            send_grad,
            ffn1,
            attn1,
            attn2,
            ffn2,
            ffn1,
            attn1,
            home_grad.finish,
            attn2,
            ffn1,
            ffn2,
            attn1,
            attn2,
            ffn1,
            attn1,
            attn1,
            attn1,
            ffn1,
            attn2,
            ffn2.unpack,
            attn1,
            attn2,
            ffn1.unpack,
            attn1,
            attn2.unpack,
            attn1.unpack,
        )
        for action in plan:
            if isinstance(action, Sum):
                action.step()
            else:
                action()
        sums = (ffn2, ffn1, attn2, attn1)
        for again in range(2 * bits):
            for total in sums:
                total.step()
        for total in sums:
            total.unpack()
        down2, gate2, up2 = ffn2.result
        down1, gate1, up1, *gains = ffn1.result
        gain_pre_ffn, gain_pre_attn, gain_post_ffn, gain_post_attn = (g.reshape(D) for g in gains)
        out2, query2, key2, value2 = attn2.result
        out1, query1, key1, value1 = attn1.result
        post_grads = (query1, key1, value1, out1, gate1.T, up1.T, down1, gain_post_attn, gain_post_ffn)
        pre_grads = (query2, key2, value2, out2, gate2.T, up2.T, down2, gain_pre_attn, gain_pre_ffn)
        return (home_output.result, home_grad.result) + post_grads + pre_grads

    spread = P("dp", "sp", None)
    in_specs = (spread, P("dp")) + (P(),) * 18 + (spread,)
    out_specs = (spread, spread) + (P(),) * 18
    return jax.shard_map(body, mesh=mesh, in_specs=in_specs, out_specs=out_specs, check_vma=False)
```
